32 devices in a mesh: dp: 8 (over z, x), expert: 4 (over y, core).
Axes of the slice: x: 2, y: 2, z: 4, core: 2. Of those that a mesh axis runs over, the one named last changes fastest.
Arguments:
- tokens: bfloat16 [37632, 384], P(('dp', 'expert')), may hold values from -6 to 6
- cotangent: float32 [37632, 384], P(('dp', 'expert')), may hold values from -6 to 6
- routes: int32 [37632, 1], P(('dp', 'expert')), may hold values from 0 to 3; in each aligned block of 1176 rows (0 to 1175, 1176 to 2351, ...) at most 588 rows name the same one
- valid_mask: int32 [37632], P(('dp', 'expert')), may hold values from 0 to 1, as said below
- shift_region: int32 [37632], P(('dp', 'expert')), may hold values from 0 to 8, as said below
- qkv_weight: float32 [384, 1152], P('dp'), may hold values from -0.4375 to 0.4375
- proj_weight: float32 [384, 384], P('dp'), may hold values from -1.25 to 1.25
- router_weight: float32 [384, 4], P('dp'), may hold values from -0.21875 to 0.21875
- norm_params: float32 [384, 4], P('dp'), may hold values from -0.9 to 1.4, as said below
- expert_in: float32 [4, 384, 1536], P('expert', 'dp'), may hold values from -0.3125 to 0.3125
- expert_out: float32 [4, 384, 1536], P('expert', 'dp'), may hold values from -1.75 to 1.75
- qkv_first: float32 [384, 1152], P('dp'), may hold values from -121.46295 to 121.46295
- qkv_second: float32 [384, 1152], P('dp'), may hold values from 3.7632 to 15.0528
- proj_first: float32 [384, 384], P('dp'), may hold values from -85.887279 to 85.887279
- proj_second: float32 [384, 384], P('dp'), may hold values from 1.8816 to 7.5264
- router_first: float32 [384, 4], P('dp'), may hold values from -5008.046 to 5008.046
- router_second: float32 [384, 4], P('dp'), may hold values from 6397.44 to 25589.76
- norm_first: float32 [384, 4], P('dp'), may hold values from -384.09959 to 384.09959
- norm_second: float32 [384, 4], P('dp'), may hold values from 37.632 to 150.528
- in_first: float32 [4, 384, 1536], P('expert', 'dp'), may hold values from -66.528 to 66.528
- in_second: float32 [4, 384, 1536], P('expert', 'dp'), may hold values from 1.12896 to 4.51584
- out_first: float32 [4, 384, 1536], P('expert', 'dp'), may hold values from -12.1462954 to 12.1462954
- out_second: float32 [4, 384, 1536], P('expert', 'dp'), may hold values from 0.037632 to 0.150528
Outputs:
- block_output: bfloat16 [37632, 384], P(('dp', 'expert'))
- input_grad: float32 [37632, 384], P(('dp', 'expert'))
- qkv_weight_new: float32 [384, 1152], P('dp')
- proj_weight_new: float32 [384, 384], P('dp')
- router_weight_new: float32 [384, 4], P('dp')
- norm_params_new: float32 [384, 4], P('dp')
- expert_in_new: float32 [4, 384, 1536], P('expert', 'dp')
- expert_out_new: float32 [4, 384, 1536], P('expert', 'dp')
- qkv_first_new: float32 [384, 1152], P('dp')
- proj_first_new: float32 [384, 384], P('dp')
- router_first_new: float32 [384, 4], P('dp')
- norm_first_new: float32 [384, 4], P('dp')
- in_first_new: float32 [4, 384, 1536], P('expert', 'dp')
- out_first_new: float32 [4, 384, 1536], P('expert', 'dp')
- qkv_second_new: float32 [384, 1152], P('dp')
- proj_second_new: float32 [384, 384], P('dp')
- router_second_new: float32 [384, 4], P('dp')
- norm_second_new: float32 [384, 4], P('dp')
- in_second_new: float32 [4, 384, 1536], P('expert', 'dp')
- out_second_new: float32 [4, 384, 1536], P('expert', 'dp')
- trust_norms: float32 [4, 6, 2], P('expert')
The draws below stay inside these ranges and needn't reach their ends.
Inputs may be any that keep to these rules, and one draw needn't show every extreme that they name: `routes`: in each aligned block of 1176 rows (the rows of one device) at most 588 rows name one expert, a bound that some block reaches. `valid_mask`: windows come from images of 12 x 12, 14 x 14 or 16 x 16 patches, padded to whole windows; padding is 0. `shift_region`: region of the grid after a cyclic shift by 3 patches; 0 in windows away from the grid's last row and column of windows. `norm_params`: columns 0 and 2 are gains, columns 1 and 3 shifts.
All inputs are finite; a program needn't handle non-finite values.
Results may differ from the reference program's by a relative error of at most 0.014.
The reference program's roundings to bfloat16 on the way count: a program that leaves them out, or rounds other values in their place, can miss the bound.
Values may be sent and summed in bfloat16 or wider, within the bound.
A program may use at most 128 MiB of HBM per device.

```python
import math
import jax
import jax.numpy as jnp
import numpy as np
from jax import lax

D = 384
HEADS = 12
HEAD_DIM = 32
FF = 1536
WINDOW = 49
STEP = 5
EXPERTS = 4
TOK_DEV = 1176
TOKENS = 37632
CAP = 588


def window_layout(key):
    groups = TOKENS // WINDOW
    base = jax.random.fold_in(key, 11)
    kind_key, row_key, col_key = jax.random.split(base, 3)
    grid = 12 + 2 * jax.random.randint(kind_key, (groups,), 0, 3)
    across = (grid + 6) // 7
    win_row = jax.random.randint(row_key, (groups,), 0, across)
    win_col = jax.random.randint(col_key, (groups,), 0, across)
    inner = jnp.arange(WINDOW, dtype=jnp.int32)
    inner_row = inner // 7
    inner_col = inner % 7
    padded = (7 * across)[:, None]
    cell_row = win_row[:, None] * 7 + inner_row[None, :]
    cell_col = win_col[:, None] * 7 + inner_col[None, :]
    orig_row = (cell_row + 3) % padded
    orig_col = (cell_col + 3) % padded
    valid = ((orig_row < grid[:, None]) & (orig_col < grid[:, None])).astype(jnp.int32)
    band_row = (cell_row >= padded - 7).astype(jnp.int32) + (cell_row >= padded - 3).astype(jnp.int32)
    band_col = (cell_col >= padded - 7).astype(jnp.int32) + (cell_col >= padded - 3).astype(jnp.int32)
    region = 3 * band_row + band_col
    return (valid.reshape(-1).astype(jnp.int32), region.reshape(-1).astype(jnp.int32))


def draw_valid_mask(key, part):
    return window_layout(key)[0]


def draw_shift_region(key, part):
    return window_layout(key)[1]


def draw_norm_params(key, part):
    gain_key, shift_key = jax.random.split(jax.random.fold_in(key, 23))
    gains = jax.random.uniform(gain_key, (D, 4), jnp.float32, 0.6, 1.4)
    shifts = jnp.clip(0.3 * jax.random.normal(shift_key, (D, 4), jnp.float32), -0.9, 0.9)
    column = jnp.arange(4) % 2
    return jnp.where(column[None, :] == 0, gains, shifts).astype(jnp.float32)


def rising_moment(key, salt, shape, row_axis, scale):
    noise = jnp.clip(jax.random.normal(jax.random.fold_in(key, salt), shape, jnp.float32), -6.0, 6.0)
    position = jnp.arange(D, dtype=jnp.float32) / max(D - 1, 1)
    factor = jnp.exp(math.log(0.3) + math.log(10.0) * position)
    view = [1] * len(shape)
    view[row_axis] = D
    return (scale * noise * factor.reshape(view)).astype(jnp.float32)


def draw_qkv_first(key, part):
    return rising_moment(key, 31, (D, 3 * D), 0, 0.11 * (0.1 * TOKENS) ** 0.5)


def draw_proj_first(key, part):
    return rising_moment(key, 32, (D, D), 0, 0.11 * (0.05 * TOKENS) ** 0.5)


def draw_router_first(key, part):
    return rising_moment(key, 33, (D, EXPERTS), 0, 0.11 * (170 * TOKENS) ** 0.5)


def draw_norm_first(key, part):
    return rising_moment(key, 34, (D, 4), 0, 0.11 * TOKENS ** 0.5)


def draw_in_first(key, part):
    return rising_moment(key, 35, (EXPERTS, D, FF), 1, 0.11 * (0.12 * (TOKENS // EXPERTS)) ** 0.5)


def draw_out_first(key, part):
    return rising_moment(key, 36, (EXPERTS, D, FF), 1, 0.11 * (0.004 * (TOKENS // EXPERTS)) ** 0.5)


def level_of(rng, shape, cuts, smallest, top_value):
    loudness, own = 1.0, jax.random.fold_in(rng, 6)
    for dim, shards_of in cuts:
        draws = jnp.exp(jax.random.uniform(jax.random.fold_in(own, dim), (shards_of,), jnp.float32, smallest / len(cuts), top_value / len(cuts)))
        loudness = loudness * jnp.repeat(draws, shape[dim] // shards_of).reshape([-1 if axis == dim else 1 for axis in range(len(shape))])
    return loudness


def routed_block(own_key, own, number, rows, count, top, limit, slope):
    ranking = jax.random.permutation(own_key, count)
    packed, common = portions_of(count, rows * top, limit, slope, True), portions_of(count, rows * top, limit, slope, False)
    places = jnp.arange(count)

    def named(sizes, rotation):
        used = int((sizes > 0).sum())
        fixed = max(1, used // 4)
        moved = fixed + (places - fixed + rotation * (used - fixed)) % max(1, count - fixed)
        return jnp.zeros((count,), jnp.int32).at[ranking[jnp.where(places < fixed, places, moved)]].set(jnp.asarray(sizes, jnp.int32))

    sizes = jnp.where(number % 4 == 0, named(packed, number // 4), named(common, number - number // 4 - 1))
    mixed = jax.random.permutation(jax.random.fold_in(own, 3), count)
    giver, taker = mixed[0:count // 2 * 2:2], mixed[1:count // 2 * 2:2]
    margin = jnp.minimum(sizes[giver] - 1, limit - sizes[taker]) // 2
    margin = jnp.where((giver == ranking[0]) | (taker == ranking[0]) | (sizes[taker] == 0), 0, jnp.maximum(margin, 0))
    moved = jax.random.randint(jax.random.fold_in(own, 4), (count // 2,), 0, 1 << 20) % (margin + 1)
    sizes = sizes.at[giver].add(-moved).at[taker].add(moved)
    labels = jnp.searchsorted(jnp.cumsum(sizes), jnp.arange(rows * top), side="right").astype(jnp.int32)
    listing = labels.reshape(top, rows).T
    listing = listing[jax.random.permutation(jax.random.fold_in(own, 1), rows)]
    rotation = jax.random.randint(jax.random.fold_in(own, 2), (rows, 1), 0, top)
    return jnp.take_along_axis(listing, (jnp.arange(top)[None, :] + rotation) % top, axis=1)


def portions_of(amount, total, bound, skew, full):
    loads = [(1 << 20) // math.isqrt(standing ** skew) + 1 for standing in range(1, amount + 1)]
    largest = bound if full else min(bound, max(-(-total // amount), total * loads[0] // sum(loads)))
    least = 1 if total - largest >= amount - 1 else 0
    given, spare = [largest] + [least] * (amount - 1), total - largest - least * (amount - 1)
    while spare > 0:
        movable = [i for i in range(1, amount) if given[i] < largest] or [i for i in range(1, amount) if given[i] < bound]
        mass, remaining = sum([loads[i] for i in movable]), spare
        for i in movable:
            more = min(bound - given[i], max(1, remaining * loads[i] // mass), spare)
            given[i] = given[i] + more
            spare = spare - more
    return np.array(given)


def bell_draw(key, dims, scale, bound, cuts=(), kind=jnp.bfloat16):
    values = scale * jax.random.normal(key, dims, jnp.float32)
    if cuts:
        values = values * level_of(key, dims, cuts, -0.22, 0.18)
    return jnp.clip(values, -bound, bound).astype(kind)


def setup_inputs(seed: int = 0) -> dict:
    key_list = jax.random.split(jax.random.key(seed), 24)
    tokens = bell_draw(key_list[0], (TOKENS, D), 1.0, 6.0, ((0, 32),))
    cotangent = bell_draw(key_list[1], (TOKENS, D), 1.0, 6.0, ((0, 32),), jnp.float32)
    routes_keys = jax.random.split(jax.random.fold_in(key_list[2], 1), TOKENS // TOK_DEV)
    routes_turns = jax.random.permutation(jax.random.fold_in(key_list[2], 3), TOKENS // TOK_DEV)
    routes = jax.vmap(lambda own, number: routed_block(jax.random.fold_in(key_list[2], 2), own, number, TOK_DEV, EXPERTS, 1, CAP, 1))(routes_keys, routes_turns).reshape((TOKENS, 1))
    valid_mask = draw_valid_mask(jax.random.fold_in(key_list[23], 71), 0)
    shift_region = draw_shift_region(jax.random.fold_in(key_list[23], 71), 0)
    qkv_weight = bell_draw(key_list[5], (D, 3 * D), (D // 2) ** -0.5, 0.4375, ((0, 8),), jnp.float32)
    proj_weight = bell_draw(key_list[6], (D, D), (D // 16) ** -0.5, 1.25, ((0, 8),), jnp.float32)
    router_weight = bell_draw(key_list[7], (D, EXPERTS), (2 * D) ** -0.5, 0.21875, ((0, 8),), jnp.float32)
    norm_params = draw_norm_params(jax.random.fold_in(key_list[23], 71), 0)
    expert_in = bell_draw(key_list[9], (EXPERTS, D, FF), D ** -0.5, 0.3125, ((0, 4), (1, 8)), jnp.float32)
    expert_out = bell_draw(key_list[10], (EXPERTS, D, FF), (FF // 128) ** -0.5, 1.75, ((0, 4), (1, 8)), jnp.float32)
    qkv_first = draw_qkv_first(jax.random.fold_in(key_list[23], 71), 0)
    qkv_second = jnp.clip(jnp.exp(math.log(15.0528) - 1.3862944 * jax.random.uniform(key_list[12], (D, 3 * D), jnp.float32) ** level_of(key_list[12], (D, 3 * D), ((0, 8),), -0.2, 0.2)), 3.7632, 15.0528)
    proj_first = draw_proj_first(jax.random.fold_in(key_list[23], 71), 0)
    proj_second = jnp.clip(jnp.exp(math.log(7.5264) - 1.3862944 * jax.random.uniform(key_list[14], (D, D), jnp.float32) ** level_of(key_list[14], (D, D), ((0, 8),), -0.2, 0.2)), 1.8816, 7.5264)
    router_first = draw_router_first(jax.random.fold_in(key_list[23], 71), 0)
    router_second = jnp.clip(jnp.exp(math.log(25589.76) - 1.3862944 * jax.random.uniform(key_list[16], (D, EXPERTS), jnp.float32) ** level_of(key_list[16], (D, EXPERTS), ((0, 8),), -0.2, 0.2)), 6397.44, 25589.76)
    norm_first = draw_norm_first(jax.random.fold_in(key_list[23], 71), 0)
    norm_second = jnp.clip(jnp.exp(math.log(150.528) - 1.3862944 * jax.random.uniform(key_list[18], (D, 4), jnp.float32) ** level_of(key_list[18], (D, 4), ((0, 8),), -0.2, 0.2)), 37.632, 150.528)
    in_first = draw_in_first(jax.random.fold_in(key_list[23], 71), 0)
    in_second = jnp.clip(jnp.exp(math.log(4.51584) - 1.3862944 * jax.random.uniform(key_list[20], (EXPERTS, D, FF), jnp.float32) ** level_of(key_list[20], (EXPERTS, D, FF), ((0, 4), (1, 8)), -0.2, 0.2)), 1.12896, 4.51584)
    out_first = draw_out_first(jax.random.fold_in(key_list[23], 71), 0)
    out_second = jnp.clip(jnp.exp(math.log(0.150528) - 1.3862944 * jax.random.uniform(key_list[22], (EXPERTS, D, FF), jnp.float32) ** level_of(key_list[22], (EXPERTS, D, FF), ((0, 4), (1, 8)), -0.2, 0.2)), 0.037632, 0.150528)
    return {"tokens": tokens, "cotangent": cotangent, "routes": routes, "valid_mask": valid_mask, "shift_region": shift_region, "qkv_weight": qkv_weight, "proj_weight": proj_weight, "router_weight": router_weight, "norm_params": norm_params, "expert_in": expert_in, "expert_out": expert_out, "qkv_first": qkv_first, "qkv_second": qkv_second, "proj_first": proj_first, "proj_second": proj_second, "router_first": router_first, "router_second": router_second, "norm_first": norm_first, "norm_second": norm_second, "in_first": in_first, "in_second": in_second, "out_first": out_first, "out_second": out_second}


@jax.custom_vjp
def low(v):
    return lax.optimization_barrier(v.astype(jnp.bfloat16)).astype(jnp.float32)

@jax.custom_vjp
def low_back(v):
    return v

def low_keep(v):
    return (low(v), None)

def low_pass(kept, grad):
    return (grad,)

def back_keep(v):
    return (v, None)

def back_low(kept, grad):
    return (low(grad),)
low.defvjp(low_keep, low_pass)
low_back.defvjp(back_keep, back_low)
HIGH = lax.Precision.HIGHEST
NORM_EPS = 1e-05
MASKED = -1e+30
BETA_ONE = 0.9
BETA_TWO = 0.999
ADAM_EPS = 1e-06
DECAY = 0.01
RATE = 0.3

def layer_norm(values, gain, shift):
    average = lax.optimization_barrier(jnp.mean(values, axis=-1, keepdims=True))
    centred = values - average
    variance = lax.optimization_barrier(jnp.mean(centred * centred, axis=-1, keepdims=True))
    return centred * lax.rsqrt(variance + NORM_EPS) * gain + shift

def allowed_pairs(valid_mask, shift_region, groups):
    valid_w = valid_mask.reshape(groups, WINDOW)
    region_w = shift_region.reshape(groups, WINDOW)
    same_region = region_w[:, :, None] == region_w[:, None, :]
    keeps = same_region & (valid_w[:, None, :] == 1)
    diagonal = jnp.eye(WINDOW, dtype=jnp.bool_)
    return keeps | diagonal[None]

def lamb_full(weight, grad, first, second):
    first_new = BETA_ONE * first + (1.0 - BETA_ONE) * grad
    second_new = BETA_TWO * second + (1.0 - BETA_TWO) * grad * grad
    first_hat = first_new / (1.0 - BETA_ONE ** STEP)
    second_hat = second_new / (1.0 - BETA_TWO ** STEP)
    direction = first_hat / (jnp.sqrt(second_hat) + ADAM_EPS) + DECAY * weight
    weight_norm = jnp.sqrt(jnp.sum(weight * weight))
    update_norm = jnp.sqrt(jnp.sum(direction * direction))
    weight_new = weight - RATE * (weight_norm / (update_norm + 1e-06)) * direction
    return (weight_new, first_new, second_new, weight_norm, update_norm)

def reference(tokens, cotangent, routes, valid_mask, shift_region, qkv_weight, proj_weight, router_weight, norm_params, expert_in, expert_out, qkv_first, qkv_second, proj_first, proj_second, router_first, router_second, norm_first, norm_second, in_first, in_second, out_first, out_second):
    blocks = TOKENS // TOK_DEV
    groups = TOKENS // WINDOW
    route_ids = routes[:, 0].astype(jnp.int32)
    onehot = route_ids[:, None] == jnp.arange(EXPERTS, dtype=jnp.int32)[None, :]
    counts_int = onehot.astype(jnp.int32).reshape(blocks, TOK_DEV, EXPERTS)
    slot_index = lax.optimization_barrier(jnp.sum((jnp.cumsum(counts_int, axis=1) - 1) * counts_int, axis=2)).astype(jnp.int32)
    route_block = route_ids.reshape(blocks, TOK_DEV)
    block_index = jnp.broadcast_to(jnp.arange(blocks, dtype=jnp.int32)[:, None], (blocks, TOK_DEV))
    allowed = allowed_pairs(valid_mask, shift_region, groups)
    col_scale = jnp.concatenate([jnp.full((D,), HEAD_DIM ** (-0.5), jnp.float32), jnp.ones((2 * D,), jnp.float32)])
    onehot_f = onehot.astype(jnp.float32)

    def forward(x_f, w_qkv, w_proj, w_router, w_norm, w_up, w_down):
        qkv_low = low(w_qkv)
        proj_low = low(w_proj)
        router_low = low(w_router)
        norm_low = low(w_norm)
        up_low = low(w_up)
        down_low = low(w_down)
        h_one = low(layer_norm(x_f, norm_low[:, 0], norm_low[:, 1]))
        raw = low_back(jnp.dot(h_one, qkv_low, precision=HIGH))
        qkv = low(raw * col_scale)
        query_heads = qkv[:, :D].reshape(groups, WINDOW, HEADS, HEAD_DIM)
        key_heads = qkv[:, D:2 * D].reshape(groups, WINDOW, HEADS, HEAD_DIM)
        value_heads = qkv[:, 2 * D:].reshape(groups, WINDOW, HEADS, HEAD_DIM)
        scores = low_back(jnp.einsum('wqhd,wkhd->whqk', query_heads, key_heads, precision=HIGH))
        scores = jnp.where(allowed[:, None], scores, MASKED)
        attn_probs = low(jax.nn.softmax(scores, axis=-1))
        mixed = jnp.einsum('whqk,wkhd->wqhd', attn_probs, value_heads, precision=HIGH).reshape(TOKENS, D)
        mixed = low(low_back(mixed))
        y_one = x_f + low_back(jnp.dot(mixed, proj_low, precision=HIGH))
        h_two = low(layer_norm(y_one, norm_low[:, 2], norm_low[:, 3]))
        logits = low_back(jnp.dot(h_two, router_low, precision=HIGH))
        gate_prob = lax.optimization_barrier(jnp.sum(jax.nn.softmax(logits, axis=-1) * onehot_f, axis=-1))
        sent = low_back(h_two).reshape(blocks, TOK_DEV, D)
        buffers = jnp.zeros((blocks, EXPERTS, CAP, D), jnp.float32).at[block_index, route_block, slot_index].set(sent)
        rows_all = jnp.transpose(buffers, (1, 0, 2, 3)).reshape(EXPERTS, blocks * CAP, D)
        up_proj = low_back(jnp.einsum('erd,edf->erf', rows_all, up_low, precision=HIGH))
        hidden = low(jax.nn.gelu(up_proj, approximate=False))
        returned = low(low_back(jnp.einsum('erf,edf->erd', hidden, down_low, precision=HIGH)))
        returned = jnp.transpose(returned.reshape(EXPERTS, blocks, CAP, D), (1, 0, 2, 3))
        expert_tok = returned[block_index, route_block, slot_index].reshape(TOKENS, D)
        return y_one + gate_prob[:, None] * expert_tok
    x_f = tokens.astype(jnp.float32)
    output_f, pull = jax.vjp(forward, x_f, qkv_weight, proj_weight, router_weight, norm_params, expert_in, expert_out)
    grad_out = cotangent * valid_mask.astype(jnp.float32)[:, None]
    input_grad, grad_qkv, grad_proj, grad_router, grad_norm, grad_in, grad_down = pull(grad_out)
    qkv_new, qkv_m, qkv_s, qkv_wn, qkv_un = lamb_full(qkv_weight, grad_qkv, qkv_first, qkv_second)
    proj_new, proj_m, proj_s, proj_wn, proj_un = lamb_full(proj_weight, grad_proj, proj_first, proj_second)
    router_new, router_m, router_s, router_wn, router_un = lamb_full(router_weight, grad_router, router_first, router_second)
    norm_new, norm_m, norm_s, norm_wn, norm_un = lamb_full(norm_params, grad_norm, norm_first, norm_second)
    in_new, in_m, in_s, in_wn, in_un = jax.vmap(lamb_full)(expert_in, grad_in, in_first, in_second)
    out_new, out_m, out_s, out_wn, out_un = jax.vmap(lamb_full)(expert_out, grad_down, out_first, out_second)
    shared_rows = jnp.stack([jnp.stack([qkv_wn, qkv_un]), jnp.stack([proj_wn, proj_un]), jnp.stack([router_wn, router_un]), jnp.stack([norm_wn, norm_un])])
    shared_rows = jnp.broadcast_to(shared_rows[None], (EXPERTS, 4, 2))
    expert_rows = jnp.stack([jnp.stack([in_wn, in_un], axis=1), jnp.stack([out_wn, out_un], axis=1)], axis=1)
    trust_norms = jnp.concatenate([shared_rows, expert_rows], axis=1)
    return (output_f.astype(jnp.bfloat16), input_grad, qkv_new, proj_new, router_new, norm_new, in_new, out_new, qkv_m, proj_m, router_m, norm_m, in_m, out_m, qkv_s, proj_s, router_s, norm_s, in_s, out_s, trust_norms)
```

```python
import functools

import jax
import jax.numpy as jnp
from jax import lax
from jax.experimental import pallas as pl
from jax.experimental.pallas import tpu as pltpu
from jax.sharding import PartitionSpec as P

HEADS = 12
HEAD_DIM = 32
WINDOW = 49
PAD = 64
STEP = 5
TILE = 128
NORM_EPS = 1e-05
MASKED = -1e30
BETA_ONE = 0.9
BETA_TWO = 0.999
ADAM_EPS = 1e-06
DECAY = 0.01
RATE = 0.3
VMEM_BYTES = 60 * 1024 * 1024

f32 = jnp.float32
bf16 = jnp.bfloat16


def dot_nn(a, b):
    return lax.dot_general(a, b, (((1,), (0,)), ((), ())), preferred_element_type=f32)


def dot_nt(a, b):
    return lax.dot_general(a, b, (((1,), (1,)), ((), ())), preferred_element_type=f32)


def dot_tn(a, b):
    return lax.dot_general(a, b, (((0,), (0,)), ((), ())), preferred_element_type=f32)


def norm_stats(v):
    width = v.shape[-1]
    mean = jnp.sum(v, axis=-1, keepdims=True) * (1.0 / width)
    centred = v - mean
    var = jnp.sum(centred * centred, axis=-1, keepdims=True) * (1.0 / width)
    rstd = lax.rsqrt(var + NORM_EPS)
    return centred * rstd, rstd


def norm_back(d, normed, rstd, gain):
    width = d.shape[-1]
    dn = d * gain
    m1 = jnp.sum(dn, axis=-1, keepdims=True) * (1.0 / width)
    m2 = jnp.sum(dn * normed, axis=-1, keepdims=True) * (1.0 / width)
    return rstd * (dn - m1 - normed * m2)


def head_masks():
    lane = lax.broadcasted_iota(jnp.int32, (PAD, 128), 1)
    return [lane // HEAD_DIM == h for h in range(4)]


def spread_heads(v, masks):
    zero = jnp.zeros_like(v)
    return jnp.concatenate([jnp.where(m, v, zero) for m in masks], axis=0)


def gather_heads(v, masks):
    out = jnp.where(masks[0], v[0:PAD], 0.0)
    for h in range(1, 4):
        out = jnp.where(masks[h], v[h * PAD : (h + 1) * PAD], out)
    return out


def weight_part(w_ref, part):
    width = w_ref.shape[1]
    at = (part % 2) * width
    return w_ref[part // 2, :, at : at + width]


def load_windows(src_ref, dst_ref, per_group):
    width = dst_ref.shape[-1]
    for k in range(per_group):
        dst_ref[k * PAD : k * PAD + WINDOW, :] = src_ref[0, k * WINDOW : (k + 1) * WINDOW, :]
        dst_ref[k * PAD + WINDOW : (k + 1) * PAD, :] = jnp.zeros((PAD - WINDOW, width), f32)


def forward_kernel(
    experts,
    slots,
    per_group,
    x_ref,
    g_ref,
    meta_ref,
    row_ref,
    w_ref,
    hz_ref,
    y1_ref,
    pr_ref,
    attn_ref,
    qkv_ref,
    p_ref,
    key_ref,
    count_ref,
    xp,
    gp,
    carry,
):
    step = pl.program_id(0)
    rows = per_group * PAD
    width = x_ref.shape[-1]
    groups = width // 128
    load_windows(x_ref, xp, per_group)
    load_windows(g_ref, gp, per_group)

    @pl.when(step == 0)
    def _():
        carry[...] = jnp.zeros_like(carry)

    small = w_ref[0, :, 2 * width :]
    small_t = jnp.transpose(small.astype(f32))
    a1, b1, a2, b2 = (small_t[experts + i : experts + i + 1, :] for i in range(4))
    normed, _ = norm_stats(xp[...])
    h1 = (normed * a1 + b1).astype(bf16)
    for part in range(3):
        raw = dot_nn(h1, weight_part(w_ref, part))
        if part == 0:
            raw = raw * (HEAD_DIM**-0.5)
        qkv_ref[:, :, part * width : (part + 1) * width] = raw.astype(bf16).reshape(per_group, PAD, width)

    meta = meta_ref[...]
    valid = meta[:, 2:3].astype(f32)
    masks = head_masks()
    key_i = lax.broadcasted_iota(jnp.int32, (PAD, 4 * PAD), 0)
    lane_i = lax.broadcasted_iota(jnp.int32, (PAD, 4 * PAD), 1)
    diagonal = key_i == lax.rem(lane_i, PAD)

    def window(w, _):
        code = meta_ref[pl.ds(pl.multiple_of(w * PAD, PAD), PAD), 0:1]
        allowed = (code == row_ref[w]) | diagonal
        for lg in range(groups):
            q = qkv_ref[w, :, lg * 128 : (lg + 1) * 128]
            k = qkv_ref[w, :, width + lg * 128 : width + (lg + 1) * 128]
            v = qkv_ref[w, :, 2 * width + lg * 128 : 2 * width + (lg + 1) * 128]
            s = dot_nt(k, spread_heads(q, masks))
            s = jnp.where(allowed, s, MASKED)
            e = jnp.exp(s - jnp.max(s, axis=0, keepdims=True))
            p = e * (1.0 / jnp.sum(e, axis=0, keepdims=True))
            p_ref[w, lg] = p
            o = dot_tn(p.astype(bf16), v)
            attn_ref[pl.ds(pl.multiple_of(w * PAD, PAD), PAD), lg * 128 : (lg + 1) * 128] = gather_heads(
                o, masks
            ).astype(bf16)
        return 0

    lax.fori_loop(0, per_group, window, 0)

    y1 = xp[...] + dot_nn(attn_ref[...], weight_part(w_ref, 3))
    y1_ref[...] = y1
    normed2, _ = norm_stats(y1)
    h2 = (normed2 * a2 + b2).astype(bf16)
    lane = lax.broadcasted_iota(jnp.int32, (rows, 128), 1)
    logits = jnp.where(lane < experts, dot_nn(h2, small), MASKED)
    e = jnp.exp(logits - jnp.max(logits, axis=-1, keepdims=True))
    pr = e * (1.0 / jnp.sum(e, axis=-1, keepdims=True))
    pr_ref[...] = pr
    chosen = lane == meta[:, 1:2]
    gate = jnp.sum(jnp.where(chosen, pr, 0.0), axis=-1, keepdims=True)
    gv = gp[...] * valid
    hz_ref[:, 0:width] = h2
    hz_ref[:, width : 2 * width] = (gate * gv).astype(bf16)

    onehot = jnp.where(chosen, 1.0, 0.0)
    before = lax.broadcasted_iota(jnp.int32, (rows, rows), 1) < lax.broadcasted_iota(jnp.int32, (rows, rows), 0)
    ranks = dot_nn(jnp.where(before, 1.0, 0.0).astype(bf16), onehot.astype(bf16)) + carry[0:1, :]
    slot = jnp.sum(ranks * onehot, axis=-1, keepdims=True)
    seen = jnp.sum(onehot, axis=-1, keepdims=True)
    key = (meta[:, 1:2].astype(f32) * slots + slot) * seen + (seen - 1.0)
    key_ref[...] = jnp.broadcast_to(key, (rows, 128)).astype(jnp.int32)
    carry[...] = carry[...] + jnp.sum(onehot, axis=0, keepdims=True)
    count_ref[...] = carry[...].astype(jnp.int32)


def expert_kernel(slots, counts_ref, hz_ref, keyrow_ref, keycol_ref, we_ref, grad_ref, tok_ref, acc):
    e = pl.program_id(0)
    width = hz_ref.shape[-1] // 2
    total = hz_ref.shape[0]

    @pl.when(e == 0)
    def _():
        tok_ref[...] = jnp.zeros_like(tok_ref)

    acc[...] = jnp.zeros_like(acc)
    used = counts_ref[e]

    def tile(t, _):
        base = e * slots + t * TILE
        pick = keyrow_ref[...] == base + lax.broadcasted_iota(jnp.int32, (TILE, total), 0)
        both = dot_nn(jnp.where(pick, 1.0, 0.0).astype(bf16), hz_ref[...]).astype(bf16)
        rows, dz = both[:, 0:width], both[:, width : 2 * width]
        up = dot_nn(rows, we_ref[0, 0])
        cdf = 0.5 * (1.0 + lax.erf(up * 2.0**-0.5))
        hidden = (up * cdf).astype(bf16)
        slope = cdf + up * (jnp.exp(-0.5 * up * up) * (2.0 * jnp.pi) ** -0.5)
        ret = dot_nt(hidden, we_ref[0, 1]).astype(bf16)
        dup = (dot_nn(dz, we_ref[0, 1]) * slope).astype(bf16)
        back = dot_nt(dup, we_ref[0, 0]).astype(bf16)
        acc[1] += dot_tn(dz, hidden)
        acc[0] += dot_tn(rows, dup)
        put = keycol_ref[...] == base + lax.broadcasted_iota(jnp.int32, (total, TILE), 1)
        tok_ref[...] += dot_nn(jnp.where(put, 1.0, 0.0).astype(bf16), jnp.concatenate([ret, back], axis=1))
        return 0

    lax.fori_loop(0, (used + TILE - 1) // TILE, tile, 0)
    grad_ref[0] = acc[...].astype(bf16)


def backward_kernel(
    experts,
    per_group,
    x_ref,
    g_ref,
    meta_ref,
    w_ref,
    tok_ref,
    hz_ref,
    y1_ref,
    pr_ref,
    attn_ref,
    qkv_ref,
    p_ref,
    out_ref,
    dx_ref,
    shared_ref,
    small_ref,
    xp,
    gp,
    outp,
    dattn,
    dqkv,
    acc,
    acc_s,
):
    step = pl.program_id(0)
    rows = per_group * PAD
    width = x_ref.shape[-1]
    groups = width // 128
    scale = HEAD_DIM**-0.5

    @pl.when(step == 0)
    def _():
        acc[...] = jnp.zeros_like(acc)
        acc_s[...] = jnp.zeros_like(acc_s)

    load_windows(x_ref, xp, per_group)
    load_windows(g_ref, gp, per_group)
    meta = meta_ref[...]
    valid = meta[:, 2:3].astype(f32)
    small = w_ref[0, :, 2 * width :]
    small_t = jnp.transpose(small.astype(f32))
    a1, b1, a2, b2 = (small_t[experts + i : experts + i + 1, :] for i in range(4))
    y1 = y1_ref[...]
    gv = gp[...] * valid
    z = tok_ref[:, 0:width]
    lane = lax.broadcasted_iota(jnp.int32, (rows, 128), 1)
    chosen = lane == meta[:, 1:2]
    pr = pr_ref[...]
    gate = jnp.sum(jnp.where(chosen, pr, 0.0), axis=-1, keepdims=True)
    outp[...] = y1 + gate * z
    for k in range(per_group):
        out_ref[0, k * WINDOW : (k + 1) * WINDOW, :] = outp[k * PAD : k * PAD + WINDOW, :]
    dgate = jnp.sum(gv * z, axis=-1, keepdims=True)
    kept = jnp.where(lane < experts, jnp.where(chosen, 1.0, 0.0) - pr, 0.0)
    dlogits = (dgate * gate * kept).astype(bf16)
    h2 = hz_ref[:, 0:width]
    acc_s[0:128] += dot_tn(dlogits, h2)
    dh2 = dot_nt(dlogits, small) + tok_ref[:, width : 2 * width]
    n2, r2 = norm_stats(y1)
    acc_s[130:131] += jnp.sum(dh2 * n2, axis=0, keepdims=True)
    acc_s[131:132] += jnp.sum(dh2, axis=0, keepdims=True)
    dy1 = gv + norm_back(dh2, n2, r2, a2)
    gp[...] = dy1
    da = dy1.astype(bf16)
    acc[3] += dot_tn(attn_ref[...], da)
    dattn[...] = dot_nt(da, weight_part(w_ref, 3)).astype(bf16)

    masks = head_masks()

    def window(w, _):
        at = pl.ds(pl.multiple_of(w * PAD, PAD), PAD)
        for lg in range(groups):
            cols = slice(lg * 128, (lg + 1) * 128)
            q = qkv_ref[w, :, lg * 128 : (lg + 1) * 128]
            k = qkv_ref[w, :, width + lg * 128 : width + (lg + 1) * 128]
            v = qkv_ref[w, :, 2 * width + lg * 128 : 2 * width + (lg + 1) * 128]
            d_all = spread_heads(dattn[at, cols], masks)
            q_all = spread_heads(q, masks)
            p = p_ref[w, lg]
            dp = dot_nt(v, d_all)
            ds = (p * (dp - jnp.sum(dp * p, axis=0, keepdims=True))).astype(bf16)
            dv = dot_nn(p.astype(bf16), d_all)
            dk = dot_nn(ds, q_all)
            dq = gather_heads(dot_tn(ds, k), masks) * scale
            dqkv[0, at, cols] = dq.astype(bf16)
            dqkv[1, at, cols] = dk.astype(bf16)
            dqkv[2, at, cols] = dv.astype(bf16)
        return 0

    lax.fori_loop(0, per_group, window, 0)

    n1, r1 = norm_stats(xp[...])
    h1 = (n1 * a1 + b1).astype(bf16)
    dh1 = jnp.zeros((rows, width), f32)
    for part in range(3):
        dpart = dqkv[part]
        acc[part] += dot_tn(h1, dpart)
        dh1 = dh1 + dot_nt(dpart, weight_part(w_ref, part))
    acc_s[128:129] += jnp.sum(dh1 * n1, axis=0, keepdims=True)
    acc_s[129:130] += jnp.sum(dh1, axis=0, keepdims=True)
    outp[...] = gp[...] + norm_back(dh1, n1, r1, a1)
    for k in range(per_group):
        dx_ref[0, k * WINDOW : (k + 1) * WINDOW, :] = outp[k * PAD : k * PAD + WINDOW, :]

    @pl.when(step == pl.num_programs(0) - 1)
    def _():
        for part in range(4):
            shared_ref[part] = acc[part].astype(bf16)
        small_ref[0:8] = acc_s[0:8]
        small_ref[8:16] = acc_s[128:136]


def place():
    dp, ex = lax.axis_index("dp"), lax.axis_index("expert")
    return lax.div(dp, 2), lax.rem(dp, 2), lax.div(ex, 2), lax.rem(ex, 2)


def at(z, x, y, c):
    return (z * 2 + x, y * 2 + c)


def push(src, dst, send_sem, recv_sem, device):
    copy = pltpu.make_async_remote_copy(
        src_ref=src,
        dst_ref=dst,
        send_sem=send_sem,
        recv_sem=recv_sem,
        device_id=device,
        device_id_type=pl.DeviceIdType.MESH,
    )
    return copy


def meet(z, x, y, c, depth):
    barrier = pltpu.get_barrier_semaphore()

    def greet(device):
        pl.semaphore_signal(barrier, inc=1, device_id=device, device_id_type=pl.DeviceIdType.MESH)

    greet(at(z, x, y, 1 - c))
    greet(at(z, 1 - x, y, c))
    greet(at(z, x, 1 - y, c))
    for other in range(depth):
        @pl.when(z != other)
        def _():
            greet(at(other, x, y, c))

    pl.semaphore_wait(barrier, 3 + depth - 1)


class Gather:
    def __init__(self, depth, ex_ref, we_ref, sems):
        self.depth = depth
        self.ex, self.we = ex_ref, we_ref
        (self.loc, self.zs, self.zr, self.xs, self.xr, self.ys, self.yr, self.cs, self.cr) = sems
        self.z, self.x, self.y, self.c = place()

    @staticmethod
    def semaphores(depth):
        dma = pltpu.SemaphoreType.DMA
        return [
            dma((1,)),
            dma((2, depth)),
            dma((depth,)),
            dma((3, depth)),
            dma((3, depth)),
            dma((3, depth)),
            dma((3, depth)),
            dma((7, depth)),
            dma((7, depth)),
        ]

    def e(self, y, c):
        return y * 2 + c

    def block(self, y, c, s, z, x):
        return self.we.at[y * 2 + c, s, z * 2 + x]

    def pair(self, y, c, z, x):
        return self.we.at[y * 2 + c, :, z * 2 + x]

    def z_copy(self, up, zo, first=False):
        mine = self.ex if first else self.pair(self.y, self.c, zo, self.x)
        target = self.z + 1 if up else self.z - 1
        return push(
            mine,
            self.pair(self.y, self.c, zo, self.x),
            self.zs.at[0 if up else 1, zo],
            self.zr.at[zo],
            at(target, self.x, self.y, self.c),
        )

    def x_copy(self, kind, zo, y, first=False):
        s = 0 if kind == 0 else 1
        dst = self.block(y, self.c, s, zo, self.x)
        src = self.ex.at[s] if first else dst
        return push(src, dst, self.xs.at[kind, zo], self.xr.at[kind, zo], at(self.z, 1 - self.x, self.y, self.c))

    def y_copy(self, kind, zo, x, first=False):
        s = 1 if kind == 0 else 0
        dst = self.block(self.y, self.c, s, zo, x)
        src = self.ex.at[s] if first else dst
        return push(src, dst, self.ys.at[kind, zo], self.yr.at[kind, zo], at(self.z, self.x, 1 - self.y, self.c))

    def c_copy(self, kind, zo, c, first=False):
        x, y = self.x, self.y
        if kind == 0:
            dst = self.pair(y, c, zo, x)
        elif kind == 1:
            dst = self.block(y, c, 0, zo, 1 - x)
        elif kind == 2:
            dst = self.block(1 - y, c, 1, zo, x)
        elif kind in (3, 4):
            dst = self.block(1 - y, c, 0, zo, x if kind == 3 else 1 - x)
        else:
            dst = self.block(y if kind == 5 else 1 - y, c, 1, zo, 1 - x)
        src = self.ex if first else dst
        return push(src, dst, self.cs.at[kind, zo], self.cr.at[kind, zo], at(self.z, x, y, 1 - self.c))

    def spread(self, zo, first=False):
        self.x_copy(0, zo, self.y, first).start()
        self.y_copy(0, zo, self.x, first).start()
        self.y_copy(1, zo, self.x, first).start()
        self.x_copy(1, zo, self.y, first).start()
        self.c_copy(0, zo, self.c, first).start()

    def begin(self):
        z = self.z
        self.local = pltpu.make_async_copy(self.ex, self.pair(self.y, self.c, z, self.x), self.loc.at[0])
        self.local.start()

        @pl.when(z < self.depth - 1)
        def _():
            self.z_copy(True, z, True).start()

        @pl.when(z > 0)
        def _():
            self.z_copy(False, z, True).start()

        self.spread(z, True)

    def line(self, s):
        z = self.z

        @pl.when(z - s >= 0)
        def _():
            self.z_copy(True, z - s).wait_recv()

            @pl.when(z < self.depth - 1)
            def _():
                self.z_copy(True, z - s).start()

            self.spread(z - s)

        @pl.when(z + s < self.depth)
        def _():
            self.z_copy(True, z + s).wait_recv()

            @pl.when(z > 0)
            def _():
                self.z_copy(False, z + s).start()

            self.spread(z + s)

    def turn(self, zo):
        self.x_copy(0, zo, self.y).wait_recv()
        self.y_copy(2, zo, 1 - self.x).start()
        self.c_copy(1, zo, self.c).start()
        self.y_copy(0, zo, self.x).wait_recv()
        self.x_copy(2, zo, 1 - self.y).start()
        self.c_copy(2, zo, self.c).start()

    def turns(self, s):
        z = self.z
        if s == 0:
            self.turn(z)
            return

        @pl.when(z - s >= 0)
        def _():
            self.turn(z - s)

        @pl.when(z + s < self.depth)
        def _():
            self.turn(z + s)

    def last(self):
        for zo in range(self.depth):
            for kind, ck in ((1, 3), (2, 4)):
                self.y_copy(kind, zo, self.x).wait_recv()
                self.c_copy(ck, zo, self.c).start()
            for kind, ck in ((1, 5), (2, 6)):
                self.x_copy(kind, zo, self.y).wait_recv()
                self.c_copy(ck, zo, self.c).start()

    def finish(self):
        z = self.z
        for zo in range(self.depth):
            for kind in range(7):
                self.c_copy(kind, zo, 1 - self.c).wait_recv()
        self.local.wait()
        for zo in range(self.depth):
            @pl.when((z < self.depth - 1) & (zo <= z))
            def _():
                self.z_copy(True, zo).wait_send()

            @pl.when((z > 0) & (zo >= z))
            def _():
                self.z_copy(False, zo).wait_send()

            for kind in range(3):
                self.x_copy(kind, zo, self.y).wait_send()
                self.y_copy(kind, zo, self.x).wait_send()
            for kind in range(7):
                self.c_copy(kind, zo, self.c).wait_send()


def shared_gather_kernel(depth, sh_ref, ws_ref, loc, zs, zr, xs, xr, cs, cr):
    z, x, y, c = place()

    def slot(h, zo, xo):
        return ws_ref.at[h, zo * 2 + xo]

    def z_copy(up, zo, first=False):
        dst = slot(c, zo, x)
        src = sh_ref.at[c] if first else dst
        return push(src, dst, zs.at[0 if up else 1, zo], zr.at[zo], at(z + 1 if up else z - 1, x, y, c))

    def x_copy(zo, first=False):
        dst = slot(c, zo, x)
        return push(sh_ref.at[c] if first else dst, dst, xs.at[zo], xr.at[zo], at(z, 1 - x, y, c))

    def c_copy(zo, xo, first=False):
        dst = slot(c, zo, xo)
        return push(
            sh_ref.at[c] if first else dst, dst, cs.at[xo, zo], cr.at[xo, zo], at(z, x, y, 1 - c)
        )

    meet(z, x, y, c, depth)
    local = pltpu.make_async_copy(sh_ref.at[c], slot(c, z, x), loc.at[0])
    local.start()

    @pl.when(z < depth - 1)
    def _():
        z_copy(True, z, True).start()

    @pl.when(z > 0)
    def _():
        z_copy(False, z, True).start()

    x_copy(z, True).start()
    c_copy(z, x, True).start()
    for s in range(1, depth):

        def step(zo, up, more):
            z_copy(True, zo).wait_recv()

            @pl.when(more)
            def _():
                z_copy(up, zo).start()

            x_copy(zo).start()
            c_copy(zo, x).start()

        @pl.when(z - s >= 0)
        def _():
            step(z - s, True, z < depth - 1)

        @pl.when(z + s < depth)
        def _():
            step(z + s, False, z > 0)

    for j in range(depth):
        zo = lax.rem(z + j, depth)
        x_copy(zo).wait_recv()
        c_copy(zo, 1 - x).start()
    for zo in range(depth):
        for xo in range(2):
            c_copy(zo, xo).wait_recv()
    local.wait()
    for zo in range(depth):
        @pl.when((z < depth - 1) & (zo <= z))
        def _():
            z_copy(True, zo).wait_send()

        @pl.when((z > 0) & (zo >= z))
        def _():
            z_copy(False, zo).wait_send()

        x_copy(zo).wait_send()
        for xo in range(2):
            c_copy(zo, xo).wait_send()


def expert_gather_kernel(depth, ex_ref, we_ref, *sems):
    gather = Gather(depth, ex_ref, we_ref, sems)
    meet(gather.z, gather.x, gather.y, gather.c, depth)
    gather.begin()
    gather.turns(0)
    for s in range(1, depth):
        gather.line(s)
        if s > 1:
            gather.turns(s - 1)
    gather.turns(depth - 1)
    gather.last()
    gather.finish()


class Scatter:
    def __init__(self, depth, ge_ref, bufs, sems):
        self.depth = depth
        self.ge = ge_ref
        self.t, self.rc, self.r1, self.r2, self.r3 = bufs
        (self.ls, self.cs, self.cr, self.s1, self.q1, self.s2, self.q2, self.s3, self.q3) = sems
        self.z, self.x, self.y, self.c = place()

    @staticmethod
    def scratch(depth, cols, shard):
        dma = pltpu.SemaphoreType.DMA
        bufs = [
            pltpu.VMEM((2, 2, depth, 2, shard, cols), bf16),
            pltpu.VMEM((2, 2, depth, 2, shard, cols), bf16),
            pltpu.VMEM((2, depth, 2, shard, cols), bf16),
            pltpu.VMEM((2, depth, shard, cols), bf16),
            pltpu.VMEM((2, depth, shard, cols), bf16),
        ]
        sems = [
            dma((2, 2)),
            dma((2, 2)),
            dma((2, 2)),
            dma((2, depth, 2)),
            dma((2, depth, 2)),
            dma((2, depth)),
            dma((2, depth)),
            dma((2, depth)),
            dma((2, depth)),
        ]
        return bufs + sems

    def local(self, i, s):
        y = self.y if i == 0 else 1 - self.y
        return pltpu.make_async_copy(self.ge.at[y * 2 + self.c, s], self.t.at[i, s], self.ls.at[i, s])

    def core(self, i, s):
        y = self.y if i == 0 else 1 - self.y
        return push(
            self.ge.at[y * 2 + 1 - self.c, s],
            self.rc.at[i, s],
            self.cs.at[i, s],
            self.cr.at[i, s],
            at(self.z, self.x, self.y, 1 - self.c),
        )

    def one(self, s, zo, k):
        if s == 0:
            src, device = self.t.at[1, 0, zo, k], at(self.z, self.x, 1 - self.y, self.c)
        else:
            src, device = self.t.at[k, 1, zo, 1 - self.x], at(self.z, 1 - self.x, self.y, self.c)
        return push(src, self.r1.at[s, zo, k], self.s1.at[s, zo, k], self.q1.at[s, zo, k], device)

    def two(self, s, zo):
        if s == 0:
            src, device = self.t.at[0, 0, zo, 1 - self.x], at(self.z, 1 - self.x, self.y, self.c)
        else:
            src, device = self.t.at[1, 1, zo, self.x], at(self.z, self.x, 1 - self.y, self.c)
        return push(src, self.r2.at[s, zo], self.s2.at[s, zo], self.q2.at[s, zo], device)

    def three(self, s, zo):
        return push(
            self.t.at[0, s, zo, self.x],
            self.r3.at[s, self.z],
            self.s3.at[s, zo],
            self.q3.at[s, self.z],
            at(zo, self.x, self.y, self.c),
        )

    def arrived(self, s, zo):
        return push(
            self.r3.at[s, zo], self.r3.at[s, zo], self.s3.at[s, zo], self.q3.at[s, zo], at(zo, self.x, self.y, self.c)
        )

    def begin(self):
        for i, s in ((1, 0), (0, 1), (1, 1), (0, 0)):
            self.core(i, s).start()
            self.local(i, s).start()

    def order(self, j):
        return lax.rem(self.z + j + 1, self.depth)

    def fold(self, ref, other):
        ref[...] = (ref[...].astype(f32) + other[...].astype(f32)).astype(bf16)

    def merge(self, i, s):
        self.core(i, s).wait_recv()
        self.local(i, s).wait()

        def body(j, _):
            zo = self.order(j)
            for xo in range(2):
                self.fold(self.t.at[i, s, zo, xo], self.rc.at[i, s, zo, xo])
            if (i, s) == (1, 0):
                self.one(0, zo, 0).start()
                self.one(0, zo, 1).start()
            if s == 1:
                self.one(1, zo, i).start()
            return 0

        lax.fori_loop(0, self.depth, body, 0)

    def second(self):
        def body(j, _):
            zo = self.order(j)
            for k in range(2):
                self.one(0, zo, k).wait_recv()
                self.fold(self.t.at[0, 0, zo, k], self.r1.at[0, zo, k])
            self.two(0, zo).start()
            for k in range(2):
                self.one(1, zo, k).wait_recv()
                self.fold(self.t.at[k, 1, zo, self.x], self.r1.at[1, zo, k])
            self.two(1, zo).start()
            return 0

        lax.fori_loop(0, self.depth, body, 0)

    def third(self):
        def body(j, _):
            zo = self.order(j)
            for s in range(2):
                self.two(s, zo).wait_recv()
                self.fold(self.t.at[0, s, zo, self.x], self.r2.at[s, zo])

                @pl.when(zo != self.z)
                def _():
                    self.three(s, zo).start()

            return 0

        lax.fori_loop(0, self.depth, body, 0)

    def result(self, s):
        total = self.t[0, s, self.z, self.x].astype(f32)
        for j in range(1, self.depth):
            zo = lax.rem(self.z + j, self.depth)
            self.arrived(s, zo).wait_recv()
            total = total + self.r3[s, zo].astype(f32)
        return total

    def finish(self):
        for i in range(2):
            for s in range(2):
                self.core(i, s).wait_send()

        def body(j, _):
            zo = self.order(j)
            for s in range(2):
                for k in range(2):
                    self.one(s, zo, k).wait_send()
                self.two(s, zo).wait_send()

                @pl.when(zo != self.z)
                def _():
                    self.three(s, zo).wait_send()

            return 0

        lax.fori_loop(0, self.depth, body, 0)


def expert_scatter_kernel(depth, ge_ref, out_ref, *scratch):
    scatter = Scatter(depth, ge_ref, scratch[:5], scratch[5:])
    meet(scatter.z, scatter.x, scatter.y, scatter.c, depth)
    scatter.begin()
    scatter.merge(1, 0)
    scatter.merge(0, 1)
    scatter.merge(1, 1)
    scatter.merge(0, 0)
    scatter.second()
    scatter.third()
    for s in range(2):
        out_ref[s] = scatter.result(s)
    scatter.finish()


def lamb_parts(weight, grad, first, second):
    first_new = BETA_ONE * first + (1.0 - BETA_ONE) * grad
    second_new = BETA_TWO * second + (1.0 - BETA_TWO) * grad * grad
    first_hat = first_new / (1.0 - BETA_ONE**STEP)
    second_hat = second_new / (1.0 - BETA_TWO**STEP)
    direction = first_hat / (jnp.sqrt(second_hat) + ADAM_EPS) + DECAY * weight
    return first_new, second_new, direction


def row_norms(values, lane0):
    lane = lax.broadcasted_iota(jnp.int32, (1, 128), 1)
    out = jnp.zeros((1, 128), f32)
    for i, v in enumerate(values):
        out = out + jnp.where(lane == lane0 + i, jnp.sum(v * v), 0.0)
    return out


def shared_scatter_kernel(depth, experts, *refs):
    (gs_ref, sm_ref, ge_ref), weights, firsts, seconds = refs[:3], refs[3:9], refs[9:15], refs[15:21]
    fs_ref, gsm_ref, norm_ref = refs[21:24]
    (t, rc, r1, r2, r3, src_c, src_y, src_x, sz, cur, wide, nb) = refs[24:36]
    (ccs, ccr, s1, q1, s2, q2, s3, q3, s4, q4, ms, mr, zs, zr, ns, nr) = refs[36:]
    z, x, y, c = place()
    dp, ex = z * 2 + x, y * 2 + c
    shard = fs_ref.shape[1]
    width = fs_ref.shape[2]

    barrier = pltpu.get_barrier_semaphore()

    def greet(device):
        pl.semaphore_signal(barrier, inc=1, device_id=device, device_id_type=pl.DeviceIdType.MESH)

    def peers(n, me):
        return [lax.rem(me + j, n) for j in range(1, n)]

    n_dp, n_ex = 2 * depth, 4
    for other in peers(n_dp, dp):
        greet((other, ex))
    for other in peers(n_ex, ex):
        greet((dp, other))
    pl.semaphore_wait(barrier, n_dp + n_ex - 2)

    near = [at(z, x, y, 1 - c), at(z, x, 1 - y, c), at(z, 1 - x, y, c)]
    y_of = [y, 1 - y]

    def core(i):
        return push(gs_ref.at[y_of[i], 1 - c], rc.at[i], ccs.at[i], ccr.at[i], near[0])

    def one(zo, k):
        if zo % 2 == 0:
            return push(t.at[1, zo, k], r1.at[zo, k], s1.at[zo, k], q1.at[zo, k], near[1])
        return push(t.at[k, zo, 1 - x], r1.at[zo, k], s1.at[zo, k], q1.at[zo, k], near[2])

    def two(zo):
        if zo % 2 == 0:
            return push(t.at[0, zo, 1 - x], r2.at[zo], s2.at[zo], q2.at[zo], near[2])
        return push(t.at[1, zo, x], r2.at[zo], s2.at[zo], q2.at[zo], near[1])

    def three(zo):
        return push(t.at[0, zo, x], r3.at[z], s3.at[zo], q3.at[z], at(zo, x, y, c))

    def arrived(zo):
        return push(r3.at[zo], r3.at[zo], s3.at[zo], q3.at[zo], at(zo, x, y, c))

    def small_hop(k):
        src = sm_ref if k == 0 else cur.at[k - 1]
        return push(src, (src_c, src_y, src_x)[k], ms.at[k], mr.at[k], near[k])

    def small_z(zo):
        return push(cur.at[2], sz.at[z], zs.at[zo], zr.at[z], at(zo, x, y, c))

    def small_from(zo):
        return push(sz.at[zo], sz.at[zo], zs.at[zo], zr.at[zo], at(zo, x, y, c))

    def fold(ref, a, b):
        ref[...] = (a[...].astype(f32) + b[...].astype(f32)).astype(bf16)

    small_hop(0).start()
    core(1).start()
    core(0).start()
    totals = row_norms([w[...] for w in weights], 0)
    for i in range(2):
        direction = lamb_parts(weights[4 + i][...], ge_ref[i], firsts[4 + i][...], seconds[4 + i][...])[2]
        totals = totals + row_norms([direction], 10 + i)
    small_hop(0).wait_recv()
    cur[0] = sm_ref[...] + src_c[...]
    small_hop(1).start()
    for i in (1, 0):
        core(i).wait_recv()
        for zo in range(depth):
            for k in range(2):
                fold(t.at[i, zo, k], gs_ref.at[y_of[i], c, zo, k], rc.at[i, zo, k])
            if zo % 2 == 0:
                if i == 1:
                    one(zo, 0).start()
                    one(zo, 1).start()
            else:
                one(zo, i).start()
    small_hop(1).wait_recv()
    cur[1] = cur[0] + src_y[...]
    small_hop(2).start()
    for zo in range(depth):
        for k in range(2):
            one(zo, k).wait_recv()
            target = t.at[0, zo, k] if zo % 2 == 0 else t.at[k, zo, x]
            fold(target, target, r1.at[zo, k])
        two(zo).start()
    small_hop(2).wait_recv()
    cur[2] = cur[1] + src_x[...]
    sz[z] = cur[2]
    for zo in range(depth):
        @pl.when(zo != z)
        def _():
            small_z(zo).start()

    for zo in range(depth):
        two(zo).wait_recv()
        target = t.at[0, zo, x]
        fold(target, target, r2.at[zo])

        @pl.when(zo != z)
        def _():
            three(zo).start()

    total = t[0, z, x].astype(f32)
    for zo in peers(depth, z):
        arrived(zo).wait_recv()
        total = total + r3[zo].astype(f32)
    fs_ref[ex] = total

    def four(e):
        return push(fs_ref.at[ex], fs_ref.at[ex], s4.at[e], q4.at[ex], (dp, e))

    def four_from(e):
        return push(fs_ref.at[e], fs_ref.at[e], s4.at[e], q4.at[e], (dp, e))

    for e in peers(n_ex, ex):
        four(e).start()
    for zo in peers(depth, z):
        small_from(zo).wait_recv()
    small = sz[0]
    for zo in range(1, depth):
        small = small + sz[zo]
    wide[...] = jnp.transpose(jnp.concatenate([small, jnp.zeros((128 - 16, small.shape[1]), f32)], axis=0))
    mine = jnp.transpose(wide[pl.ds(pl.multiple_of(dp * shard, 16), shard), :])[0:16]
    gsm_ref[...] = mine
    for i, g in ((2, mine[0:experts]), (3, mine[8:12])):
        direction = lamb_parts(weights[i][...], g, firsts[i][...], seconds[i][...])[2]
        totals = totals + row_norms([direction], 6 + i)
    for e in peers(n_ex, ex):
        four_from(e).wait_recv()
    for part in range(4):
        i = 1 if part == 3 else 0
        cols = slice(0, width) if part == 3 else slice(part * width, (part + 1) * width)
        direction = lamb_parts(weights[i][:, cols], fs_ref[part], firsts[i][:, cols], seconds[i][:, cols])[2]
        totals = totals + row_norms([direction], 6 + i)
    nb[dp] = jnp.broadcast_to(totals, (8, 128))

    def norm_push(r):
        return push(nb.at[dp], nb.at[dp], ns.at[r], nr.at[dp], (r, ex))

    def norm_from(r):
        return push(nb.at[r], nb.at[r], ns.at[r], nr.at[r], (r, ex))

    for r in peers(n_dp, dp):
        norm_push(r).start()
    for r in peers(n_dp, dp):
        norm_from(r).wait_recv()
    summed = nb[0]
    for r in range(1, n_dp):
        summed = summed + nb[r]
    norm_ref[...] = summed

    for r in peers(n_dp, dp):
        norm_push(r).wait_send()
    for e in peers(n_ex, ex):
        four(e).wait_send()
    for i in range(2):
        core(i).wait_send()
    for k in range(3):
        small_hop(k).wait_send()
    for zo in range(depth):
        for k in range(2):
            one(zo, k).wait_send()
        two(zo).wait_send()

        @pl.when(zo != z)
        def _():
            three(zo).wait_send()
            small_z(zo).wait_send()


def shared_scatter_scratch(depth, shard, width):
    dma = pltpu.SemaphoreType.DMA
    return [
        pltpu.VMEM((2, depth, 2, shard, width), bf16),
        pltpu.VMEM((2, depth, 2, shard, width), bf16),
        pltpu.VMEM((depth, 2, shard, width), bf16),
        pltpu.VMEM((depth, shard, width), bf16),
        pltpu.VMEM((depth, shard, width), bf16),
        pltpu.VMEM((16, width), f32),
        pltpu.VMEM((16, width), f32),
        pltpu.VMEM((16, width), f32),
        pltpu.VMEM((depth, 16, width), f32),
        pltpu.VMEM((3, 16, width), f32),
        pltpu.VMEM((width, 128), f32),
        pltpu.VMEM((2 * depth, 8, 128), f32),
        dma((2,)),
        dma((2,)),
        dma((depth, 2)),
        dma((depth, 2)),
        dma((depth,)),
        dma((depth,)),
        dma((depth,)),
        dma((depth,)),
        dma((4,)),
        dma((4,)),
        dma((3,)),
        dma((3,)),
        dma((depth,)),
        dma((depth,)),
        dma((2 * depth,)),
        dma((2 * depth,)),
    ]


def update_kernel(experts, *refs):
    (gsh_ref, gsm_ref, ge_ref, norm_ref), weights, firsts, seconds = refs[:4], refs[4:10], refs[10:16], refs[16:22]
    w_out, m_out, s_out = refs[22:28], refs[28:34], refs[34:40]
    trust_ref = refs[40]
    width = gsh_ref.shape[2]
    totals = norm_ref[0:1, :]
    lane = lax.broadcasted_iota(jnp.int32, (1, 128), 1)

    def pick(i):
        return jnp.sqrt(jnp.sum(jnp.where(lane == i, totals, 0.0), axis=-1, keepdims=True))

    row = lax.broadcasted_iota(jnp.int32, (6, 2), 0)
    col = lax.broadcasted_iota(jnp.int32, (6, 2), 1)
    trust = jnp.zeros((6, 2), f32)
    whole = slice(None)
    jobs = [(0, slice(p * width, (p + 1) * width), lambda p=p: gsh_ref[p]) for p in range(3)]
    jobs += [(1, whole, lambda: gsh_ref[3]), (2, whole, lambda: gsm_ref[0:experts]), (3, whole, lambda: gsm_ref[8:12])]
    jobs += [(4, whole, lambda: ge_ref[0]), (5, whole, lambda: ge_ref[1])]
    ratios = []
    for i in range(6):
        wn, un = pick(i), pick(6 + i)
        ratios.append(wn / (un + 1e-06))
        trust = jnp.where((row == i) & (col == 0), wn, jnp.where((row == i) & (col == 1), un, trust))
    trust_ref[...] = trust
    for i, cols, grad in jobs:
        weight = weights[i][:, cols]
        first, second, direction = lamb_parts(weight, grad(), firsts[i][:, cols], seconds[i][:, cols])
        w_out[i][:, cols] = weight - RATE * ratios[i] * direction
        m_out[i][:, cols] = first
        s_out[i][:, cols] = second


def per_device(
    dims,
    tokens,
    cotangent,
    routes,
    valid_mask,
    shift_region,
    qkv_weight,
    proj_weight,
    router_weight,
    norm_params,
    expert_in,
    expert_out,
    qkv_first,
    qkv_second,
    proj_first,
    proj_second,
    router_first,
    router_second,
    norm_first,
    norm_second,
    in_first,
    in_second,
    out_first,
    out_second,
):
    rows_here, width = tokens.shape
    experts = router_weight.shape[1]
    hidden = expert_in.shape[2]
    shard = qkv_weight.shape[0]
    capacity = 2 * rows_here // experts
    slots = -(-capacity // TILE) * TILE
    windows = rows_here // WINDOW
    per_group = 8
    steps = windows // per_group
    group_rows = per_group * WINDOW
    padded = windows * PAD

    fast = dims == (8, 4)
    depth = dims[0] // 2
    vmem = pl.BlockSpec(memory_space=pltpu.VMEM)
    anywhere = pl.BlockSpec(memory_space=pl.ANY)

    def remote(collective_id):
        return pltpu.CompilerParams(
            vmem_limit_bytes=VMEM_BYTES, collective_id=collective_id, has_side_effects=True
        )

    pack = jnp.concatenate([router_weight, norm_params], axis=1)
    pack = jnp.pad(pack, ((0, 0), (0, 128 - pack.shape[1])))
    shared_shard = jnp.concatenate([qkv_weight[:, : 2 * width], pack, qkv_weight[:, 2 * width :], proj_weight, pack], axis=1)
    shared_shard = jnp.stack(jnp.split(shared_shard.astype(bf16), 2, axis=1))
    expert_shard = jnp.stack([expert_in[0], expert_out[0]]).astype(bf16)
    if fast:
        dma = pltpu.SemaphoreType.DMA
        w_all = pl.pallas_call(
            functools.partial(shared_gather_kernel, depth),
            in_specs=[vmem],
            out_specs=anywhere,
            out_shape=jax.ShapeDtypeStruct((2, 2 * depth, shard, 2 * width + 128), bf16),
            scratch_shapes=[dma((1,)), dma((2, depth)), dma((depth,)), dma((depth,)), dma((depth,)), dma((2, depth)), dma((2, depth))],
            compiler_params=remote(0),
            name="shared_gather",
        )(shared_shard)
        w_exp = pl.pallas_call(
            functools.partial(expert_gather_kernel, depth),
            in_specs=[vmem],
            out_specs=anywhere,
            out_shape=jax.ShapeDtypeStruct((experts, 2, 2 * depth, shard, hidden), bf16),
            scratch_shapes=Gather.semaphores(depth),
            compiler_params=remote(1),
            name="expert_gather",
        )(expert_shard)
    else:
        w_all = lax.all_gather(shared_shard, "dp", axis=1, tiled=True)
        w_exp = lax.all_gather(lax.all_gather(expert_shard, "dp", axis=1, tiled=True), "expert", axis=0, tiled=False)
    w_all = w_all.reshape(2, width, 2 * width + 128)
    w_exp = w_exp.reshape(experts, 2, width, hidden)

    x3 = tokens.astype(f32).reshape(steps, group_rows, width)
    g3 = cotangent.reshape(steps, group_rows, width)
    fill = ((0, 0), (0, PAD - WINDOW))
    valid_w = valid_mask.reshape(windows, WINDOW)
    region_w = shift_region.reshape(windows, WINDOW)
    code = jnp.pad(jnp.where(valid_w == 1, region_w, -1), fill, constant_values=-2)
    route_p = jnp.pad(routes.reshape(windows, WINDOW), fill, constant_values=-1)
    meta = jnp.stack([code.reshape(-1), route_p.reshape(-1), jnp.pad(valid_w, fill).reshape(-1)], axis=1)
    region_row = jnp.tile(jnp.pad(region_w, fill, constant_values=-3), (1, 4)).reshape(windows, 1, 4 * PAD)

    rows = per_group * PAD
    params = pltpu.CompilerParams(vmem_limit_bytes=VMEM_BYTES, dimension_semantics=("arbitrary",))

    def by_step(*shape):
        zeros = (0,) * (len(shape) - 1)
        return pl.BlockSpec(shape, lambda i: (i,) + zeros)

    def whole(*shape):
        zeros = (0,) * len(shape)
        return pl.BlockSpec(shape, lambda i, *_: zeros)

    lanes = width // 128
    hz, y1, pr, attn, qkv, probs, key, counts = pl.pallas_call(
        functools.partial(forward_kernel, experts, slots, per_group),
        grid=(steps,),
        in_specs=[
            by_step(1, group_rows, width),
            by_step(1, group_rows, width),
            by_step(rows, 3),
            by_step(per_group, 1, 4 * PAD),
            whole(2, width, 2 * width + 128),
        ],
        out_specs=[
            by_step(rows, 2 * width),
            by_step(rows, width),
            by_step(rows, 128),
            by_step(rows, width),
            by_step(per_group, PAD, 3 * width),
            by_step(per_group, lanes, PAD, 4 * PAD),
            by_step(rows, 128),
            whole(1, 128),
        ],
        out_shape=[
            jax.ShapeDtypeStruct((padded, 2 * width), bf16),
            jax.ShapeDtypeStruct((padded, width), f32),
            jax.ShapeDtypeStruct((padded, 128), f32),
            jax.ShapeDtypeStruct((padded, width), bf16),
            jax.ShapeDtypeStruct((windows, PAD, 3 * width), bf16),
            jax.ShapeDtypeStruct((windows, lanes, PAD, 4 * PAD), f32),
            jax.ShapeDtypeStruct((padded, 128), jnp.int32),
            jax.ShapeDtypeStruct((1, 128), jnp.int32),
        ],
        scratch_shapes=[pltpu.VMEM((rows, width), f32), pltpu.VMEM((rows, width), f32), pltpu.VMEM((1, 128), f32)],
        compiler_params=params,
        name="attention_forward",
    )(x3, g3, meta, region_row, w_all)

    key_row = key[:, 0].reshape(1, padded)
    grads, tok = pl.pallas_call(
        functools.partial(expert_kernel, slots),
        grid_spec=pltpu.PrefetchScalarGridSpec(
            num_scalar_prefetch=1,
            grid=(experts,),
            in_specs=[
                whole(padded, 2 * width),
                whole(1, padded),
                whole(padded, 128),
                pl.BlockSpec((1, 2, width, hidden), lambda e, *_: (e, 0, 0, 0)),
            ],
            out_specs=[
                pl.BlockSpec((1, 2, width, hidden), lambda e, *_: (e, 0, 0, 0)),
                whole(padded, 2 * width),
            ],
            scratch_shapes=[pltpu.VMEM((2, width, hidden), f32)],
        ),
        out_shape=[
            jax.ShapeDtypeStruct((experts, 2, width, hidden), bf16),
            jax.ShapeDtypeStruct((padded, 2 * width), f32),
        ],
        compiler_params=params,
        name="experts",
    )(counts[0], hz, key_row, key, w_exp)

    out3, dx3, shared_grad, small_grad = pl.pallas_call(
        functools.partial(backward_kernel, experts, per_group),
        grid=(steps,),
        in_specs=[
            by_step(1, group_rows, width),
            by_step(1, group_rows, width),
            by_step(rows, 3),
            whole(2, width, 2 * width + 128),
            by_step(rows, 2 * width),
            by_step(rows, 2 * width),
            by_step(rows, width),
            by_step(rows, 128),
            by_step(rows, width),
            by_step(per_group, PAD, 3 * width),
            by_step(per_group, lanes, PAD, 4 * PAD),
        ],
        out_specs=[
            by_step(1, group_rows, width),
            by_step(1, group_rows, width),
            whole(4, width, width),
            whole(16, width),
        ],
        out_shape=[
            jax.ShapeDtypeStruct((steps, group_rows, width), f32),
            jax.ShapeDtypeStruct((steps, group_rows, width), f32),
            jax.ShapeDtypeStruct((4, width, width), bf16),
            jax.ShapeDtypeStruct((16, width), f32),
        ],
        scratch_shapes=[
            pltpu.VMEM((rows, width), f32),
            pltpu.VMEM((rows, width), f32),
            pltpu.VMEM((rows, width), f32),
            pltpu.VMEM((rows, width), bf16),
            pltpu.VMEM((3, rows, width), bf16),
            pltpu.VMEM((4, width, width), f32),
            pltpu.VMEM((136, width), f32),
        ],
        compiler_params=params,
        name="attention_backward",
    )(x3, g3, meta, w_all, tok, hz, y1, pr, attn, qkv, probs)
    block_output = out3.reshape(rows_here, width).astype(bf16)
    input_grad = dx3.reshape(rows_here, width)

    weights_now = (qkv_weight, proj_weight, router_weight.T, norm_params.T, expert_in[0], expert_out[0])
    firsts_now = (qkv_first, proj_first, router_first.T, norm_first.T, in_first[0], out_first[0])
    seconds_now = (qkv_second, proj_second, router_second.T, norm_second.T, in_second[0], out_second[0])
    state = (*weights_now, *firsts_now, *seconds_now)
    if fast:
        g_exp = pl.pallas_call(
            functools.partial(expert_scatter_kernel, depth),
            in_specs=[anywhere],
            out_specs=vmem,
            out_shape=jax.ShapeDtypeStruct((2, shard, hidden), f32),
            scratch_shapes=Scatter.scratch(depth, hidden, shard),
            compiler_params=remote(2),
            name="expert_scatter",
        )(grads.reshape(experts, 2, depth, 2, shard, hidden))
        shared, small, norms = pl.pallas_call(
            functools.partial(shared_scatter_kernel, depth, experts),
            in_specs=[vmem] * (3 + len(state)),
            out_specs=[vmem] * 3,
            out_shape=[
                jax.ShapeDtypeStruct((4, shard, width), f32),
                jax.ShapeDtypeStruct((16, shard), f32),
                jax.ShapeDtypeStruct((8, 128), f32),
            ],
            scratch_shapes=shared_scatter_scratch(depth, shard, width),
            compiler_params=remote(3),
            name="shared_scatter",
        )(shared_grad.reshape(2, 2, depth, 2, shard, width), small_grad, g_exp, *state)
    else:
        shared = lax.psum(shared_grad.astype(f32), ("expert", "dp"))
        small = lax.psum(small_grad, ("expert", "dp"))
        g_exp = lax.psum(grads.astype(f32), ("expert", "dp"))
        start = lax.axis_index("dp") * shard
        shared = lax.dynamic_slice_in_dim(shared, start, shard, axis=1)
        small = lax.dynamic_slice_in_dim(small, start, shard, axis=1)
        g_exp = lax.dynamic_index_in_dim(g_exp, lax.axis_index("expert"), 0, keepdims=False)
        g_exp = lax.dynamic_slice_in_dim(g_exp, start, shard, axis=1)
        reduced = (
            jnp.concatenate([shared[0], shared[1], shared[2]], axis=1),
            shared[3],
            small[0:experts],
            small[8:12],
            g_exp[0],
            g_exp[1],
        )
        steps_now = [lamb_parts(*entry)[2] for entry in zip(weights_now, reduced, firsts_now, seconds_now)]
        sums = jnp.stack([jnp.sum(v * v) for v in (*weights_now, *steps_now)])
        norms = jnp.broadcast_to(jnp.pad(lax.psum(sums, "dp"), (0, 128 - 12)), (8, 128))
    results = pl.pallas_call(
        functools.partial(update_kernel, experts),
        in_specs=[vmem] * (4 + len(state)),
        out_specs=[vmem] * (len(state) + 1),
        out_shape=[jax.ShapeDtypeStruct(v.shape, f32) for v in weights_now] * 3 + [jax.ShapeDtypeStruct((6, 2), f32)],
        compiler_params=pltpu.CompilerParams(vmem_limit_bytes=VMEM_BYTES),
        name="lamb_update",
    )(shared, small, g_exp, norms, *state)

    def restore(values):
        return (values[0], values[1], values[2].T, values[3].T, values[4][None], values[5][None])

    return (
        block_output,
        input_grad,
        *restore(results[0:6]),
        *restore(results[6:12]),
        *restore(results[12:18]),
        results[18][None],
    )


def solution(mesh):
    tok2 = P(("dp", "expert"), None)
    tok1 = P(("dp", "expert"))
    row = P("dp", None)
    exp = P("expert", "dp", None)
    shared4 = (row, row, row, row)
    placed = (tok2, tok2, tok2, tok1, tok1, *shared4, exp, exp, *shared4, *shared4, exp, exp, exp, exp)
    results = (tok2, tok2, *((*shared4, exp, exp) * 3), P("expert", None, None))
    dims = (mesh.shape["dp"], mesh.shape["expert"])
    return jax.shard_map(
        functools.partial(per_device, dims),
        mesh=mesh,
        in_specs=placed,
        out_specs=results,
        check_vma=False,
    )
```

```python
import functools

import jax
import jax.numpy as jnp
from jax import lax
from jax.experimental import pallas as pl
from jax.experimental.pallas import tpu as pltpu
from jax.sharding import PartitionSpec as P

HEADS = 12
HEAD_DIM = 32
WINDOW = 49
PAD = 64
STEP = 5
TILE = 256
NORM_EPS = 1e-05
MASKED = -1e30
BETA_ONE = 0.9
BETA_TWO = 0.999
ADAM_EPS = 1e-06
DECAY = 0.01
RATE = 0.3
VMEM_BYTES = 60 * 1024 * 1024

f32 = jnp.float32
bf16 = jnp.bfloat16


def dot_nn(a, b):
    return lax.dot_general(a, b, (((1,), (0,)), ((), ())), preferred_element_type=f32)


def dot_nt(a, b):
    return lax.dot_general(a, b, (((1,), (1,)), ((), ())), preferred_element_type=f32)


def dot_tn(a, b):
    return lax.dot_general(a, b, (((0,), (0,)), ((), ())), preferred_element_type=f32)


def norm_stats(v):
    width = v.shape[-1]
    mean = jnp.sum(v, axis=-1, keepdims=True) * (1.0 / width)
    centred = v - mean
    var = jnp.sum(centred * centred, axis=-1, keepdims=True) * (1.0 / width)
    rstd = lax.rsqrt(var + NORM_EPS)
    return centred * rstd, rstd


def norm_back(d, normed, rstd, gain):
    width = d.shape[-1]
    dn = d * gain
    m1 = jnp.sum(dn, axis=-1, keepdims=True) * (1.0 / width)
    m2 = jnp.sum(dn * normed, axis=-1, keepdims=True) * (1.0 / width)
    return rstd * (dn - m1 - normed * m2)


def head_masks():
    lane = lax.broadcasted_iota(jnp.int32, (PAD, 128), 1)
    return [lane // HEAD_DIM == h for h in range(4)]


def spread_heads(v, masks):
    zero = jnp.zeros_like(v)
    return jnp.concatenate([jnp.where(m, v, zero) for m in masks], axis=0)


def gather_heads(v, masks):
    out = jnp.where(masks[0], v[0:PAD], 0.0)
    for h in range(1, 4):
        out = jnp.where(masks[h], v[h * PAD : (h + 1) * PAD], out)
    return out


def weight_part(w_ref, part):
    width = (w_ref.shape[-1] - 128) // 2
    cols = slice((part % 2) * width, (part % 2 + 1) * width)
    if len(w_ref.shape) == 4:
        return w_ref[part // 2, :, :, cols].reshape(width, width)
    return w_ref[part // 2, :, cols]


def small_part(w_ref):
    width = (w_ref.shape[-1] - 128) // 2
    if len(w_ref.shape) == 4:
        return w_ref[0, :, :, 2 * width :].reshape(width, 128)
    return w_ref[0, :, 2 * width :]


def load_windows(src_ref, wide_ref, dst_ref, per_group):
    width = dst_ref.shape[-1]
    wide_ref[...] = src_ref[0].astype(f32)
    for k in range(per_group):
        dst_ref[k * PAD : k * PAD + WINDOW, :] = wide_ref[k * WINDOW : (k + 1) * WINDOW, :]
        dst_ref[k * PAD + WINDOW : (k + 1) * PAD, :] = jnp.zeros((PAD - WINDOW, width), f32)


def store_windows(src_ref, wide_ref, out_ref, per_group):
    for k in range(per_group):
        wide_ref[k * WINDOW : (k + 1) * WINDOW, :] = src_ref[k * PAD : k * PAD + WINDOW, :]
    out_ref[0] = wide_ref[...].astype(out_ref.dtype)


def token_columns(combo_ref, per_group):
    turned = jnp.transpose(combo_ref[...].astype(f32))
    return jnp.concatenate([turned[0:PAD, k : k + 1] for k in range(per_group)], axis=0).astype(jnp.int32)


def route_of(combo):
    return jnp.where(combo >= 512, combo & 15, -1)


def valid_of(combo):
    return ((combo >> 8) & 1).astype(f32)


def run_hooks(plan, step, index):
    for (k, i), jobs in plan.items():
        if i == index:

            @pl.when(step == k)
            def _():
                for job in jobs:
                    job()


def forward_kernel(dims, experts, slots, per_group, fast, *refs):
    depth = dims[0] // 2
    plan = {}
    step = pl.program_id(0)
    if fast:
        x_ref, g_ref, combo_ref, qkv_w, proj_w, router_w, norm_w, in_w, out_w = refs[:9]
        hz_ref, y1_ref, pr_ref, attn_ref, qkv_ref, p_ref, key_ref, keyrow_ref, count_ref, ws_out, we_ref = refs[9:20]
        xp, gp, wide, codes, regions, carry, w_ref, sh, ex, ws_sem = refs[20:30]
        shared_sems, gather_sems = refs[30:37], refs[37:]
        gather = Gather(depth, ex, we_ref, gather_sems)
        shared = SharedGather(depth, sh, w_ref, shared_sems)

        def enter():
            meet(gather.z, gather.x, gather.y, gather.c, depth)
            width = qkv_w.shape[1] // 3
            shard = qkv_w.shape[0]
            small = jnp.concatenate([router_w[...], norm_w[...]], axis=0)
            small = jnp.concatenate([small, jnp.zeros((128 - small.shape[0], shard), f32)], axis=0)
            sh[0, :, 0 : 2 * width] = qkv_w[:, 0 : 2 * width].astype(bf16)
            sh[0, :, 2 * width :] = jnp.transpose(small).astype(bf16)
            sh[1, :, 0:width] = qkv_w[:, 2 * width :].astype(bf16)
            sh[1, :, width : 2 * width] = proj_w[...].astype(bf16)
            sh[1, :, 2 * width :] = jnp.zeros((shard, 128), bf16)
            shared.begin()
            ex[0] = in_w[0].astype(bf16)
            ex[1] = out_w[0].astype(bf16)
            gather.begin()

        def store_shared():
            pltpu.make_async_copy(w_ref, ws_out, ws_sem.at[0]).start()

        def leave():
            gather.finish()
            shared.finish()
            pltpu.make_async_copy(w_ref, ws_out, ws_sem.at[0]).wait()

        g = gather
        plan = {
            (0, 0): [enter],
            (0, 1): [shared.receive, store_shared, lambda: g.turns(0), lambda: g.line(1)],
            (0, 2): [lambda: g.line(2)],
            (0, 3): [lambda: g.turns(1)],
            (0, 4): [lambda: g.line(3)],
            (1, 2): [lambda: g.turns(2)],
            (1, 4): [lambda: g.turns(3)],
            (2, 3): [g.last],
            (2, 4): [leave],
        }
    else:
        x_ref, g_ref, combo_ref, w_ref = refs[:4]
        hz_ref, y1_ref, pr_ref, attn_ref, qkv_ref, p_ref, key_ref, keyrow_ref, count_ref = refs[4:13]
        xp, gp, wide, codes, regions, carry = refs[13:19]
    rows = per_group * PAD
    width = x_ref.shape[-1]
    groups = width // 128
    run_hooks(plan, step, 0)
    load_windows(x_ref, wide, xp, per_group)
    load_windows(g_ref, wide, gp, per_group)

    @pl.when(step == 0)
    def _():
        carry[...] = jnp.zeros_like(carry)

    combo = token_columns(combo_ref, per_group)
    valid = valid_of(combo)
    route = route_of(combo)
    codes[...] = jnp.where((combo >> 8) & 1 == 1, (combo >> 4) & 15, -1)
    flat = combo_ref[...]
    flat = jnp.where(flat >= 512, (flat >> 4) & 15, -3)
    for k in range(per_group):
        regions[k] = jnp.concatenate([flat[k : k + 1, :]] * 2, axis=1)

    normed, _ = norm_stats(xp[...])
    run_hooks(plan, step, 1)
    small = small_part(w_ref)
    small_t = jnp.transpose(small.astype(f32))
    a1, b1, a2, b2 = (small_t[experts + i : experts + i + 1, :] for i in range(4))
    h1 = (normed * a1 + b1).astype(bf16)
    for part in range(3):
        raw = dot_nn(h1, weight_part(w_ref, part))
        if part == 0:
            raw = raw * (HEAD_DIM**-0.5)
        qkv_ref[:, :, part * width : (part + 1) * width] = raw.astype(bf16).reshape(per_group, PAD, width)
    run_hooks(plan, step, 2)

    masks = head_masks()
    key_i = lax.broadcasted_iota(jnp.int32, (PAD, 4 * PAD), 0)
    lane_i = lax.broadcasted_iota(jnp.int32, (PAD, 4 * PAD), 1)
    diagonal = key_i == lax.rem(lane_i, PAD)

    def window(w, _):
        at = pl.ds(pl.multiple_of(w * PAD, PAD), PAD)
        allowed = (codes[at, :] == regions[w]) | diagonal
        for lg in range(groups):
            q = qkv_ref[w, :, lg * 128 : (lg + 1) * 128]
            k = qkv_ref[w, :, width + lg * 128 : width + (lg + 1) * 128]
            v = qkv_ref[w, :, 2 * width + lg * 128 : 2 * width + (lg + 1) * 128]
            s = dot_nt(k, spread_heads(q, masks))
            s = jnp.where(allowed, s, MASKED)
            e = jnp.exp(s - jnp.max(s, axis=0, keepdims=True))
            p = e * (1.0 / jnp.sum(e, axis=0, keepdims=True))
            p_ref[w, lg] = p
            o = dot_tn(p.astype(bf16), v)
            attn_ref[at, lg * 128 : (lg + 1) * 128] = gather_heads(o, masks).astype(bf16)
        return 0

    half = per_group // 2
    lax.fori_loop(0, half, window, 0)
    run_hooks(plan, step, 3)
    lax.fori_loop(half, per_group, window, 0)

    y1 = xp[...] + dot_nn(attn_ref[...], weight_part(w_ref, 3))
    y1_ref[...] = y1
    normed2, _ = norm_stats(y1)
    h2 = (normed2 * a2 + b2).astype(bf16)
    lane = lax.broadcasted_iota(jnp.int32, (rows, 128), 1)
    logits = jnp.where(lane < experts, dot_nn(h2, small), MASKED)
    e = jnp.exp(logits - jnp.max(logits, axis=-1, keepdims=True))
    pr = e * (1.0 / jnp.sum(e, axis=-1, keepdims=True))
    pr_ref[...] = pr
    chosen = lane == route
    gate = jnp.sum(jnp.where(chosen, pr, 0.0), axis=-1, keepdims=True)
    gv = gp[...] * valid
    hz_ref[:, 0:width] = h2
    hz_ref[:, width : 2 * width] = (gate * gv).astype(bf16)

    onehot = jnp.where(chosen, 1.0, 0.0)
    before = lax.broadcasted_iota(jnp.int32, (rows, rows), 1) < lax.broadcasted_iota(jnp.int32, (rows, rows), 0)
    ranks = dot_nn(jnp.where(before, 1.0, 0.0).astype(bf16), onehot.astype(bf16)) + carry[0:1, :]
    slot = jnp.sum(ranks * onehot, axis=-1, keepdims=True)
    seen = jnp.sum(onehot, axis=-1, keepdims=True)
    key = (route.astype(f32) * slots + slot) * seen + (seen - 1.0)
    key = jnp.broadcast_to(key, (rows, 128))
    key_ref[...] = key.astype(jnp.int32)
    keyrow_ref[...] = jnp.transpose(key)[0:1, :].astype(jnp.int32)
    carry[...] = carry[...] + jnp.sum(onehot, axis=0, keepdims=True)
    count_ref[...] = carry[...].astype(jnp.int32)
    run_hooks(plan, step, 4)


def expert_kernel(slots, counts_ref, hz_ref, keyrow_ref, keycol_ref, we_ref, grad_ref, tok_ref, acc):
    e = pl.program_id(0)
    width = hz_ref.shape[-1] // 2
    total = hz_ref.shape[0]

    @pl.when(e == 0)
    def _():
        tok_ref[...] = jnp.zeros_like(tok_ref)

    acc[...] = jnp.zeros_like(acc)
    used = counts_ref[e]

    def tile(t, _):
        base = e * slots + t * TILE
        pick = keyrow_ref[...] == base + lax.broadcasted_iota(jnp.int32, (TILE, total), 0)
        both = dot_nn(jnp.where(pick, 1.0, 0.0).astype(bf16), hz_ref[...]).astype(bf16)
        rows, dz = both[:, 0:width], both[:, width : 2 * width]
        up = dot_nn(rows, we_ref[0, 0])
        cdf = 0.5 * (1.0 + lax.erf(up * 2.0**-0.5))
        hidden = (up * cdf).astype(bf16)
        slope = cdf + up * (jnp.exp(-0.5 * up * up) * (2.0 * jnp.pi) ** -0.5)
        ret = dot_nt(hidden, we_ref[0, 1]).astype(bf16)
        dup = (dot_nn(dz, we_ref[0, 1]) * slope).astype(bf16)
        back = dot_nt(dup, we_ref[0, 0]).astype(bf16)
        acc[1] += dot_tn(dz, hidden)
        acc[0] += dot_tn(rows, dup)
        put = jnp.concatenate([keycol_ref[...]] * (TILE // 128), axis=1) == base + lax.broadcasted_iota(jnp.int32, (total, TILE), 1)
        tok_ref[...] += dot_nn(jnp.where(put, 1.0, 0.0).astype(bf16), jnp.concatenate([ret, back], axis=1))
        return 0

    lax.fori_loop(0, (used + TILE - 1) // TILE, tile, 0)
    grad_ref[0] = acc[...].astype(bf16)


def backward_kernel(dims, experts, per_group, fast, *refs):
    depth = dims[0] // 2
    plan = {}
    step = pl.program_id(0)
    x_ref, g_ref, combo_ref, w_ref, tok_ref, hz_ref, y1_ref, pr_ref, attn_ref, qkv_ref, p_ref = refs[:11]
    refs = refs[11:]
    if fast:
        ge_ref, out_ref, dx_ref, shared_ref, small_ref, gexp_ref = refs[:6]
        xp, gp, wide, outp, dattn, dqkv, acc, acc_s = refs[6:14]
        sc = Scatter(depth, ge_ref, refs[14:19], refs[19:])

        def enter():
            meet(sc.z, sc.x, sc.y, sc.c, depth)
            sc.begin()

        def leave():
            sc.third(depth - 1)
            for s in range(2):
                gexp_ref[s] = sc.result(s)
            sc.finish()

        plan = {
            (0, 0): [enter],
            (0, 1): [lambda: sc.merge(0)],
            (0, 3): [lambda: sc.second(0), lambda: sc.merge(1)],
            (1, 1): [lambda: sc.second(1), lambda: sc.third(0), lambda: sc.merge(2)],
            (2, 0): [lambda: sc.second(2), lambda: sc.third(1), lambda: sc.merge(3)],
            (2, 3): [lambda: sc.second(3), lambda: sc.third(2)],
            (2, 4): [leave],
        }
    else:
        out_ref, dx_ref, shared_ref, small_ref = refs[:4]
        xp, gp, wide, outp, dattn, dqkv, acc, acc_s = refs[4:12]
    rows = per_group * PAD
    width = x_ref.shape[-1]
    groups = width // 128
    scale = HEAD_DIM**-0.5

    @pl.when(step == 0)
    def _():
        acc[...] = jnp.zeros_like(acc)
        acc_s[...] = jnp.zeros_like(acc_s)

    run_hooks(plan, step, 0)
    load_windows(x_ref, wide, xp, per_group)
    load_windows(g_ref, wide, gp, per_group)
    combo = token_columns(combo_ref, per_group)
    valid = valid_of(combo)
    route = route_of(combo)
    small = small_part(w_ref)
    small_t = jnp.transpose(small.astype(f32))
    a1, b1, a2, b2 = (small_t[experts + i : experts + i + 1, :] for i in range(4))
    y1 = y1_ref[...]
    gv = gp[...] * valid
    z = tok_ref[:, 0:width]
    lane = lax.broadcasted_iota(jnp.int32, (rows, 128), 1)
    chosen = lane == route
    pr = pr_ref[...]
    gate = jnp.sum(jnp.where(chosen, pr, 0.0), axis=-1, keepdims=True)
    outp[...] = y1 + gate * z
    store_windows(outp, wide, out_ref, per_group)
    dgate = jnp.sum(gv * z, axis=-1, keepdims=True)
    kept = jnp.where(lane < experts, jnp.where(chosen, 1.0, 0.0) - pr, 0.0)
    dlogits = (dgate * gate * kept).astype(bf16)
    h2 = hz_ref[:, 0:width]
    acc_s[0:128] += dot_tn(dlogits, h2)
    dh2 = dot_nt(dlogits, small) + tok_ref[:, width : 2 * width]
    n2, r2 = norm_stats(y1)
    acc_s[130:131] += jnp.sum(dh2 * n2, axis=0, keepdims=True)
    acc_s[131:132] += jnp.sum(dh2, axis=0, keepdims=True)
    dy1 = gv + norm_back(dh2, n2, r2, a2)
    gp[...] = dy1
    da = dy1.astype(bf16)
    acc[3] += dot_tn(attn_ref[...], da)
    dattn[...] = dot_nt(da, weight_part(w_ref, 3)).astype(bf16)
    run_hooks(plan, step, 1)

    masks = head_masks()

    def window(w, _):
        at = pl.ds(pl.multiple_of(w * PAD, PAD), PAD)
        for lg in range(groups):
            cols = slice(lg * 128, (lg + 1) * 128)
            q = qkv_ref[w, :, lg * 128 : (lg + 1) * 128]
            k = qkv_ref[w, :, width + lg * 128 : width + (lg + 1) * 128]
            v = qkv_ref[w, :, 2 * width + lg * 128 : 2 * width + (lg + 1) * 128]
            d_all = spread_heads(dattn[at, cols], masks)
            q_all = spread_heads(q, masks)
            p = p_ref[w, lg]
            dp = dot_nt(v, d_all)
            ds = (p * (dp - jnp.sum(dp * p, axis=0, keepdims=True))).astype(bf16)
            dv = dot_nn(p.astype(bf16), d_all)
            dk = dot_nn(ds, q_all)
            dq = gather_heads(dot_tn(ds, k), masks) * scale
            dqkv[0, at, cols] = dq.astype(bf16)
            dqkv[1, at, cols] = dk.astype(bf16)
            dqkv[2, at, cols] = dv.astype(bf16)
        return 0

    half = per_group // 2
    lax.fori_loop(0, half, window, 0)
    run_hooks(plan, step, 2)
    lax.fori_loop(half, per_group, window, 0)
    run_hooks(plan, step, 3)

    n1, r1 = norm_stats(xp[...])
    h1 = (n1 * a1 + b1).astype(bf16)
    dh1 = jnp.zeros((rows, width), f32)
    for part in range(3):
        dpart = dqkv[part]
        acc[part] += dot_tn(h1, dpart)
        dh1 = dh1 + dot_nt(dpart, weight_part(w_ref, part))
    acc_s[128:129] += jnp.sum(dh1 * n1, axis=0, keepdims=True)
    acc_s[129:130] += jnp.sum(dh1, axis=0, keepdims=True)
    outp[...] = gp[...] + norm_back(dh1, n1, r1, a1)
    store_windows(outp, wide, dx_ref, per_group)

    @pl.when(step == pl.num_programs(0) - 1)
    def _():
        for part in range(4):
            shared_ref[part] = acc[part].astype(bf16)
        small_ref[0:8] = acc_s[0:8]
        small_ref[8:16] = acc_s[128:136]

    run_hooks(plan, step, 4)


def place():
    dp, ex = lax.axis_index("dp"), lax.axis_index("expert")
    return lax.div(dp, 2), lax.rem(dp, 2), lax.div(ex, 2), lax.rem(ex, 2)


def at(z, x, y, c):
    return (z * 2 + x, y * 2 + c)


def push(src, dst, send_sem, recv_sem, device):
    copy = pltpu.make_async_remote_copy(
        src_ref=src,
        dst_ref=dst,
        send_sem=send_sem,
        recv_sem=recv_sem,
        device_id=device,
        device_id_type=pl.DeviceIdType.MESH,
    )
    return copy


def meet(z, x, y, c, depth):
    barrier = pltpu.get_barrier_semaphore()

    def greet(device):
        pl.semaphore_signal(barrier, inc=1, device_id=device, device_id_type=pl.DeviceIdType.MESH)

    greet(at(z, x, y, 1 - c))
    greet(at(z, 1 - x, y, c))
    greet(at(z, x, 1 - y, c))
    for other in range(depth):
        @pl.when(z != other)
        def _():
            greet(at(other, x, y, c))

    pl.semaphore_wait(barrier, 3 + depth - 1)


class Gather:
    def __init__(self, depth, ex_ref, we_ref, sems):
        self.depth = depth
        self.ex, self.we = ex_ref, we_ref
        (self.loc, self.zs, self.zr, self.xs, self.xr, self.ys, self.yr, self.cs, self.cr) = sems
        self.z, self.x, self.y, self.c = place()

    @staticmethod
    def semaphores(depth):
        dma = pltpu.SemaphoreType.DMA
        return [
            dma((1,)),
            dma((2, depth)),
            dma((depth,)),
            dma((3, depth)),
            dma((3, depth)),
            dma((3, depth)),
            dma((3, depth)),
            dma((7, depth)),
            dma((7, depth)),
        ]

    def local(self):
        return pltpu.make_async_copy(self.ex, self.pair(self.y, self.c, self.z, self.x), self.loc.at[0])

    def block(self, y, c, s, z, x):
        return self.we.at[y * 2 + c, s, z * 2 + x]

    def pair(self, y, c, z, x):
        return self.we.at[y * 2 + c, :, z * 2 + x]

    def z_copy(self, up, zo, first=False):
        mine = self.ex if first else self.pair(self.y, self.c, zo, self.x)
        target = self.z + 1 if up else self.z - 1
        return push(
            mine,
            self.pair(self.y, self.c, zo, self.x),
            self.zs.at[0 if up else 1, zo],
            self.zr.at[zo],
            at(target, self.x, self.y, self.c),
        )

    def x_copy(self, kind, zo, y, first=False):
        s = 0 if kind == 0 else 1
        dst = self.block(y, self.c, s, zo, self.x)
        src = self.ex.at[s] if first else dst
        return push(src, dst, self.xs.at[kind, zo], self.xr.at[kind, zo], at(self.z, 1 - self.x, self.y, self.c))

    def y_copy(self, kind, zo, x, first=False):
        s = 1 if kind == 0 else 0
        dst = self.block(self.y, self.c, s, zo, x)
        src = self.ex.at[s] if first else dst
        return push(src, dst, self.ys.at[kind, zo], self.yr.at[kind, zo], at(self.z, self.x, 1 - self.y, self.c))

    def c_copy(self, kind, zo, c, first=False):
        x, y = self.x, self.y
        if kind == 0:
            dst = self.pair(y, c, zo, x)
        elif kind == 1:
            dst = self.block(y, c, 0, zo, 1 - x)
        elif kind == 2:
            dst = self.block(1 - y, c, 1, zo, x)
        elif kind in (3, 4):
            dst = self.block(1 - y, c, 0, zo, x if kind == 3 else 1 - x)
        else:
            dst = self.block(y if kind == 5 else 1 - y, c, 1, zo, 1 - x)
        src = self.ex if first else dst
        return push(src, dst, self.cs.at[kind, zo], self.cr.at[kind, zo], at(self.z, x, y, 1 - self.c))

    def spread(self, zo, first=False):
        self.x_copy(0, zo, self.y, first).start()
        self.y_copy(0, zo, self.x, first).start()
        self.y_copy(1, zo, self.x, first).start()
        self.x_copy(1, zo, self.y, first).start()
        self.c_copy(0, zo, self.c, first).start()

    def begin(self):
        z = self.z
        self.local().start()

        @pl.when(z < self.depth - 1)
        def _():
            self.z_copy(True, z, True).start()

        @pl.when(z > 0)
        def _():
            self.z_copy(False, z, True).start()

        self.spread(z, True)

    def line(self, s):
        z = self.z

        @pl.when(z - s >= 0)
        def _():
            self.z_copy(True, z - s).wait_recv()

            @pl.when(z < self.depth - 1)
            def _():
                self.z_copy(True, z - s).start()

            self.spread(z - s)

        @pl.when(z + s < self.depth)
        def _():
            self.z_copy(True, z + s).wait_recv()

            @pl.when(z > 0)
            def _():
                self.z_copy(False, z + s).start()

            self.spread(z + s)

    def turn(self, zo):
        self.x_copy(0, zo, self.y).wait_recv()
        self.y_copy(2, zo, 1 - self.x).start()
        self.c_copy(1, zo, self.c).start()
        self.y_copy(0, zo, self.x).wait_recv()
        self.x_copy(2, zo, 1 - self.y).start()
        self.c_copy(2, zo, self.c).start()

    def turns(self, s):
        z = self.z
        if s == 0:
            self.turn(z)
            return

        @pl.when(z - s >= 0)
        def _():
            self.turn(z - s)

        @pl.when(z + s < self.depth)
        def _():
            self.turn(z + s)

    def last(self):
        for zo in range(self.depth):
            for kind, ck in ((1, 3), (2, 4)):
                self.y_copy(kind, zo, self.x).wait_recv()
                self.c_copy(ck, zo, self.c).start()
            for kind, ck in ((1, 5), (2, 6)):
                self.x_copy(kind, zo, self.y).wait_recv()
                self.c_copy(ck, zo, self.c).start()

    def finish(self):
        z = self.z
        for zo in range(self.depth):
            for kind in range(7):
                self.c_copy(kind, zo, 1 - self.c).wait_recv()
        self.local().wait()
        for zo in range(self.depth):
            @pl.when((z < self.depth - 1) & (zo <= z))
            def _():
                self.z_copy(True, zo).wait_send()

            @pl.when((z > 0) & (zo >= z))
            def _():
                self.z_copy(False, zo).wait_send()

            for kind in range(3):
                self.x_copy(kind, zo, self.y).wait_send()
                self.y_copy(kind, zo, self.x).wait_send()
            for kind in range(7):
                self.c_copy(kind, zo, self.c).wait_send()


class SharedGather:
    def __init__(self, depth, sh_ref, ws_ref, sems):
        self.depth, self.sh, self.ws = depth, sh_ref, ws_ref
        self.loc, self.zs, self.zr, self.xs, self.xr, self.cs, self.cr = sems
        self.z, self.x, self.y, self.c = place()

    @staticmethod
    def semaphores(depth):
        dma = pltpu.SemaphoreType.DMA
        return [dma((1,)), dma((depth,)), dma((depth,)), dma((depth,)), dma((depth,)), dma((2, depth)), dma((2, depth))]

    def slot(self, zo, xo):
        return self.ws.at[self.c, zo * 2 + xo]

    def local(self):
        return pltpu.make_async_copy(self.sh.at[self.c], self.slot(self.z, self.x), self.loc.at[0])

    def z_copy(self, target):
        return push(
            self.sh.at[self.c],
            self.slot(self.z, self.x),
            self.zs.at[target],
            self.zr.at[self.z],
            at(target, self.x, self.y, self.c),
        )

    def z_from(self, zo):
        dst = self.slot(zo, self.x)
        return push(dst, dst, self.zs.at[zo], self.zr.at[zo], at(zo, self.x, self.y, self.c))

    def x_copy(self, zo, first=False):
        dst = self.slot(zo, self.x)
        src = self.sh.at[self.c] if first else dst
        return push(src, dst, self.xs.at[zo], self.xr.at[zo], at(self.z, 1 - self.x, self.y, self.c))

    def c_copy(self, zo, xo, first=False):
        dst = self.slot(zo, xo)
        src = self.sh.at[self.c] if first else dst
        return push(src, dst, self.cs.at[xo, zo], self.cr.at[xo, zo], at(self.z, self.x, self.y, 1 - self.c))

    def others(self):
        return [lax.rem(self.z + j, self.depth) for j in range(1, self.depth)]

    def begin(self):
        self.local().start()
        for zo in self.others():
            self.z_copy(zo).start()
        self.x_copy(self.z, True).start()
        self.c_copy(self.z, self.x, True).start()

    def receive(self):
        for zo in self.others():
            self.z_from(zo).wait_recv()
            self.x_copy(zo).start()
            self.c_copy(zo, self.x).start()
        for j in range(self.depth):
            zo = lax.rem(self.z + j, self.depth)
            self.x_copy(zo).wait_recv()
            self.c_copy(zo, 1 - self.x).start()
        for zo in range(self.depth):
            for xo in range(2):
                self.c_copy(zo, xo).wait_recv()
        self.local().wait()

    def finish(self):
        for zo in self.others():
            self.z_copy(zo).wait_send()
        for zo in range(self.depth):
            self.x_copy(zo).wait_send()
            for xo in range(2):
                self.c_copy(zo, xo).wait_send()


class Scatter:
    def __init__(self, depth, ge_ref, bufs, sems):
        self.depth = depth
        self.ge = ge_ref
        self.t, self.rc, self.r1, self.r2, self.r3 = bufs
        (self.ls, self.cs, self.cr, self.s1, self.q1, self.s2, self.q2, self.s3, self.q3) = sems
        self.z, self.x, self.y, self.c = place()

    @staticmethod
    def scratch(depth, cols, shard):
        dma = pltpu.SemaphoreType.DMA
        bufs = [
            pltpu.VMEM((2, 2, depth, 2, shard, cols), bf16),
            pltpu.VMEM((2, 2, depth, 2, shard, cols), bf16),
            pltpu.VMEM((2, depth, 2, shard, cols), bf16),
            pltpu.VMEM((2, depth, shard, cols), bf16),
            pltpu.VMEM((2, depth, shard, cols), bf16),
        ]
        sems = [
            dma((2, 2, depth)),
            dma((2, 2, depth)),
            dma((2, 2, depth)),
            dma((2, depth, 2)),
            dma((2, depth, 2)),
            dma((2, depth)),
            dma((2, depth)),
            dma((2, depth)),
            dma((2, depth)),
        ]
        return bufs + sems

    def local(self, i, s, zo):
        y = self.y if i == 0 else 1 - self.y
        return pltpu.make_async_copy(self.ge.at[y * 2 + self.c, s, zo], self.t.at[i, s, zo], self.ls.at[i, s, zo])

    def core(self, i, s, zo):
        y = self.y if i == 0 else 1 - self.y
        return push(
            self.ge.at[y * 2 + 1 - self.c, s, zo],
            self.rc.at[i, s, zo],
            self.cs.at[i, s, zo],
            self.cr.at[i, s, zo],
            at(self.z, self.x, self.y, 1 - self.c),
        )

    def one(self, s, zo, k):
        if s == 0:
            src, device = self.t.at[1, 0, zo, k], at(self.z, self.x, 1 - self.y, self.c)
        else:
            src, device = self.t.at[k, 1, zo, 1 - self.x], at(self.z, 1 - self.x, self.y, self.c)
        return push(src, self.r1.at[s, zo, k], self.s1.at[s, zo, k], self.q1.at[s, zo, k], device)

    def two(self, s, zo):
        if s == 0:
            src, device = self.t.at[0, 0, zo, 1 - self.x], at(self.z, 1 - self.x, self.y, self.c)
        else:
            src, device = self.t.at[1, 1, zo, self.x], at(self.z, self.x, 1 - self.y, self.c)
        return push(src, self.r2.at[s, zo], self.s2.at[s, zo], self.q2.at[s, zo], device)

    def three(self, s, zo):
        return push(
            self.t.at[0, s, zo, self.x],
            self.r3.at[s, self.z],
            self.s3.at[s, zo],
            self.q3.at[s, self.z],
            at(zo, self.x, self.y, self.c),
        )

    def arrived(self, s, zo):
        return push(
            self.r3.at[s, zo], self.r3.at[s, zo], self.s3.at[s, zo], self.q3.at[s, zo], at(zo, self.x, self.y, self.c)
        )

    def begin(self):
        def body(j, _):
            zo = self.order(j)
            for i, s in ((1, 0), (0, 1), (1, 1), (0, 0)):
                self.core(i, s, zo).start()
                self.local(i, s, zo).start()
            return 0

        lax.fori_loop(0, self.depth, body, 0)

    def order(self, j):
        return lax.rem(self.z + j + 1, self.depth)

    def fold(self, ref, other):
        ref[...] = (ref[...].astype(f32) + other[...].astype(f32)).astype(bf16)

    def merge(self, j):
        zo = self.order(j)
        for i, s in ((1, 0), (0, 1), (1, 1), (0, 0)):
            self.core(i, s, zo).wait_recv()
            self.local(i, s, zo).wait()
            for xo in range(2):
                self.fold(self.t.at[i, s, zo, xo], self.rc.at[i, s, zo, xo])
            if (i, s) == (1, 0):
                self.one(0, zo, 0).start()
                self.one(0, zo, 1).start()
            if s == 1:
                self.one(1, zo, i).start()

    def second(self, j):
        zo = self.order(j)
        for k in range(2):
            self.one(0, zo, k).wait_recv()
            self.fold(self.t.at[0, 0, zo, k], self.r1.at[0, zo, k])
        self.two(0, zo).start()
        for k in range(2):
            self.one(1, zo, k).wait_recv()
            self.fold(self.t.at[k, 1, zo, self.x], self.r1.at[1, zo, k])
        self.two(1, zo).start()

    def third(self, j):
        zo = self.order(j)
        for s in range(2):
            self.two(s, zo).wait_recv()
            self.fold(self.t.at[0, s, zo, self.x], self.r2.at[s, zo])

            @pl.when(zo != self.z)
            def _():
                self.three(s, zo).start()

    def result(self, s):
        total = self.t[0, s, self.z, self.x].astype(f32)
        for j in range(1, self.depth):
            zo = lax.rem(self.z + j, self.depth)
            self.arrived(s, zo).wait_recv()
            total = total + self.r3[s, zo].astype(f32)
        return total

    def finish(self):
        def body(j, _):
            zo = self.order(j)
            for s in range(2):
                for i in range(2):
                    self.core(i, s, zo).wait_send()
                for k in range(2):
                    self.one(s, zo, k).wait_send()
                self.two(s, zo).wait_send()

                @pl.when(zo != self.z)
                def _():
                    self.three(s, zo).wait_send()

            return 0

        lax.fori_loop(0, self.depth, body, 0)


def lamb_parts(weight, grad, first, second):
    first_new = BETA_ONE * first + (1.0 - BETA_ONE) * grad
    second_new = BETA_TWO * second + (1.0 - BETA_TWO) * grad * grad
    first_hat = first_new / (1.0 - BETA_ONE**STEP)
    second_hat = second_new / (1.0 - BETA_TWO**STEP)
    direction = first_hat / (jnp.sqrt(second_hat) + ADAM_EPS) + DECAY * weight
    return first_new, second_new, direction


def row_norms(values, lane0):
    lane = lax.broadcasted_iota(jnp.int32, (1, 128), 1)
    out = jnp.zeros((1, 128), f32)
    for i, v in enumerate(values):
        out = out + jnp.where(lane == lane0 + i, jnp.sum(v * v), 0.0)
    return out


def shared_scatter_kernel(depth, experts, *refs):
    (gs_ref, sm_ref, ge_ref), weights, firsts, seconds = refs[:3], refs[3:9], refs[9:15], refs[15:21]
    fs_ref, gsm_ref, norm_ref = refs[21:24]
    (t, rc, r1, r2, r3, src_c, src_y, src_x, sz, cur, wide, nb) = refs[24:36]
    (ccs, ccr, s1, q1, s2, q2, s3, q3, s4, q4, ms, mr, zs, zr, ns, nr) = refs[36:]
    z, x, y, c = place()
    dp, ex = z * 2 + x, y * 2 + c
    shard = fs_ref.shape[1]
    width = fs_ref.shape[2]

    barrier = pltpu.get_barrier_semaphore()

    def greet(device):
        pl.semaphore_signal(barrier, inc=1, device_id=device, device_id_type=pl.DeviceIdType.MESH)

    def peers(n, me):
        return [lax.rem(me + j, n) for j in range(1, n)]

    n_dp, n_ex = 2 * depth, 4
    for other in peers(n_dp, dp):
        greet((other, ex))
    for other in peers(n_ex, ex):
        greet((dp, other))
    pl.semaphore_wait(barrier, n_dp + n_ex - 2)

    near = [at(z, x, y, 1 - c), at(z, x, 1 - y, c), at(z, 1 - x, y, c)]
    y_of = [y, 1 - y]

    def core(i):
        return push(gs_ref.at[y_of[i], 1 - c], rc.at[i], ccs.at[i], ccr.at[i], near[0])

    def one(zo, k):
        if zo % 2 == 0:
            return push(t.at[1, zo, k], r1.at[zo, k], s1.at[zo, k], q1.at[zo, k], near[1])
        return push(t.at[k, zo, 1 - x], r1.at[zo, k], s1.at[zo, k], q1.at[zo, k], near[2])

    def two(zo):
        if zo % 2 == 0:
            return push(t.at[0, zo, 1 - x], r2.at[zo], s2.at[zo], q2.at[zo], near[2])
        return push(t.at[1, zo, x], r2.at[zo], s2.at[zo], q2.at[zo], near[1])

    def three(zo):
        return push(t.at[0, zo, x], r3.at[z], s3.at[zo], q3.at[z], at(zo, x, y, c))

    def arrived(zo):
        return push(r3.at[zo], r3.at[zo], s3.at[zo], q3.at[zo], at(zo, x, y, c))

    def small_hop(k):
        src = sm_ref if k == 0 else cur.at[k - 1]
        return push(src, (src_c, src_y, src_x)[k], ms.at[k], mr.at[k], near[k])

    def small_z(zo):
        return push(cur.at[2], sz.at[z], zs.at[zo], zr.at[z], at(zo, x, y, c))

    def small_from(zo):
        return push(sz.at[zo], sz.at[zo], zs.at[zo], zr.at[zo], at(zo, x, y, c))

    def fold(ref, a, b):
        ref[...] = (a[...].astype(f32) + b[...].astype(f32)).astype(bf16)

    small_hop(0).start()
    core(1).start()
    core(0).start()
    totals = row_norms([w[...] for w in weights], 0)
    for i in range(2):
        direction = lamb_parts(weights[4 + i][...], ge_ref[i], firsts[4 + i][...], seconds[4 + i][...])[2]
        totals = totals + row_norms([direction], 10 + i)
    small_hop(0).wait_recv()
    cur[0] = sm_ref[...] + src_c[...]
    small_hop(1).start()
    for i in (1, 0):
        core(i).wait_recv()
        for zo in range(depth):
            for k in range(2):
                fold(t.at[i, zo, k], gs_ref.at[y_of[i], c, zo, k], rc.at[i, zo, k])
            if zo % 2 == 0:
                if i == 1:
                    one(zo, 0).start()
                    one(zo, 1).start()
            else:
                one(zo, i).start()
    small_hop(1).wait_recv()
    cur[1] = cur[0] + src_y[...]
    small_hop(2).start()
    for zo in range(depth):
        for k in range(2):
            one(zo, k).wait_recv()
            target = t.at[0, zo, k] if zo % 2 == 0 else t.at[k, zo, x]
            fold(target, target, r1.at[zo, k])
        two(zo).start()
    small_hop(2).wait_recv()
    cur[2] = cur[1] + src_x[...]
    sz[z] = cur[2]
    for zo in range(depth):
        @pl.when(zo != z)
        def _():
            small_z(zo).start()

    for zo in range(depth):
        two(zo).wait_recv()
        target = t.at[0, zo, x]
        fold(target, target, r2.at[zo])

        @pl.when(zo != z)
        def _():
            three(zo).start()

    total = t[0, z, x].astype(f32)
    for zo in peers(depth, z):
        arrived(zo).wait_recv()
        total = total + r3[zo].astype(f32)
    fs_ref[ex] = total

    def four(e):
        return push(fs_ref.at[ex], fs_ref.at[ex], s4.at[e], q4.at[ex], (dp, e))

    def four_from(e):
        return push(fs_ref.at[e], fs_ref.at[e], s4.at[e], q4.at[e], (dp, e))

    for e in peers(n_ex, ex):
        four(e).start()
    for zo in peers(depth, z):
        small_from(zo).wait_recv()
    small = sz[0]
    for zo in range(1, depth):
        small = small + sz[zo]
    wide[...] = jnp.transpose(jnp.concatenate([small, jnp.zeros((128 - 16, small.shape[1]), f32)], axis=0))
    mine = jnp.transpose(wide[pl.ds(pl.multiple_of(dp * shard, 16), shard), :])[0:16]
    gsm_ref[...] = mine
    for i, g in ((2, mine[0:experts]), (3, mine[8:12])):
        direction = lamb_parts(weights[i][...], g, firsts[i][...], seconds[i][...])[2]
        totals = totals + row_norms([direction], 6 + i)
    for e in peers(n_ex, ex):
        four_from(e).wait_recv()
    for part in range(4):
        i = 1 if part == 3 else 0
        cols = slice(0, width) if part == 3 else slice(part * width, (part + 1) * width)
        direction = lamb_parts(weights[i][:, cols], fs_ref[part], firsts[i][:, cols], seconds[i][:, cols])[2]
        totals = totals + row_norms([direction], 6 + i)
    nb[dp] = jnp.broadcast_to(totals, (8, 128))

    def norm_push(r):
        return push(nb.at[dp], nb.at[dp], ns.at[r], nr.at[dp], (r, ex))

    def norm_from(r):
        return push(nb.at[r], nb.at[r], ns.at[r], nr.at[r], (r, ex))

    for r in peers(n_dp, dp):
        norm_push(r).start()
    for r in peers(n_dp, dp):
        norm_from(r).wait_recv()
    summed = nb[0]
    for r in range(1, n_dp):
        summed = summed + nb[r]
    norm_ref[...] = summed

    for r in peers(n_dp, dp):
        norm_push(r).wait_send()
    for e in peers(n_ex, ex):
        four(e).wait_send()
    for i in range(2):
        core(i).wait_send()
    for k in range(3):
        small_hop(k).wait_send()
    for zo in range(depth):
        for k in range(2):
            one(zo, k).wait_send()
        two(zo).wait_send()

        @pl.when(zo != z)
        def _():
            three(zo).wait_send()
            small_z(zo).wait_send()


def shared_scatter_scratch(depth, shard, width):
    dma = pltpu.SemaphoreType.DMA
    return [
        pltpu.VMEM((2, depth, 2, shard, width), bf16),
        pltpu.VMEM((2, depth, 2, shard, width), bf16),
        pltpu.VMEM((depth, 2, shard, width), bf16),
        pltpu.VMEM((depth, shard, width), bf16),
        pltpu.VMEM((depth, shard, width), bf16),
        pltpu.VMEM((16, width), f32),
        pltpu.VMEM((16, width), f32),
        pltpu.VMEM((16, width), f32),
        pltpu.VMEM((depth, 16, width), f32),
        pltpu.VMEM((3, 16, width), f32),
        pltpu.VMEM((width, 128), f32),
        pltpu.VMEM((2 * depth, 8, 128), f32),
        dma((2,)),
        dma((2,)),
        dma((depth, 2)),
        dma((depth, 2)),
        dma((depth,)),
        dma((depth,)),
        dma((depth,)),
        dma((depth,)),
        dma((4,)),
        dma((4,)),
        dma((3,)),
        dma((3,)),
        dma((depth,)),
        dma((depth,)),
        dma((2 * depth,)),
        dma((2 * depth,)),
    ]


def update_kernel(experts, *refs):
    (gsh_ref, gsm_ref, ge_ref, norm_ref), weights, firsts, seconds = refs[:4], refs[4:10], refs[10:16], refs[16:22]
    w_out, m_out, s_out = refs[22:28], refs[28:34], refs[34:40]
    trust_ref = refs[40]
    width = gsh_ref.shape[2]
    totals = norm_ref[0:1, :]
    lane = lax.broadcasted_iota(jnp.int32, (1, 128), 1)

    def pick(i):
        return jnp.sqrt(jnp.sum(jnp.where(lane == i, totals, 0.0), axis=-1, keepdims=True))

    row = lax.broadcasted_iota(jnp.int32, (2, 6), 1)
    col = lax.broadcasted_iota(jnp.int32, (2, 6), 0)
    trust = jnp.zeros((2, 6), f32)
    whole = slice(None)
    jobs = [(0, slice(p * width, (p + 1) * width), lambda p=p: gsh_ref[p]) for p in range(3)]
    jobs += [(1, whole, lambda: gsh_ref[3]), (2, whole, lambda: gsm_ref[0:experts]), (3, whole, lambda: gsm_ref[8:12])]
    jobs += [(4, whole, lambda: ge_ref[0]), (5, whole, lambda: ge_ref[1])]
    ratios = []
    for i in range(6):
        wn, un = pick(i), pick(6 + i)
        ratios.append(wn / (un + 1e-06))
        trust = jnp.where((row == i) & (col == 0), wn, jnp.where((row == i) & (col == 1), un, trust))
    trust_ref[...] = trust
    for i, cols, grad in jobs:
        weight = weights[i][:, cols]
        first, second, direction = lamb_parts(weight, grad(), firsts[i][:, cols], seconds[i][:, cols])
        w_out[i][:, cols] = weight - RATE * ratios[i] * direction
        m_out[i][:, cols] = first
        s_out[i][:, cols] = second


def per_device(
    dims,
    tokens,
    cotangent,
    routes,
    valid_mask,
    shift_region,
    qkv_weight,
    proj_weight,
    router_weight,
    norm_params,
    expert_in,
    expert_out,
    qkv_first,
    qkv_second,
    proj_first,
    proj_second,
    router_first,
    router_second,
    norm_first,
    norm_second,
    in_first,
    in_second,
    out_first,
    out_second,
):
    rows_here, width = tokens.shape
    experts = router_weight.shape[1]
    hidden = expert_in.shape[2]
    shard = qkv_weight.shape[0]
    capacity = 2 * rows_here // experts
    slots = -(-capacity // TILE) * TILE
    windows = rows_here // WINDOW
    per_group = 8
    steps = windows // per_group
    group_rows = per_group * WINDOW
    padded = windows * PAD

    fast = dims == (8, 4)
    depth = dims[0] // 2
    vmem = pl.BlockSpec(memory_space=pltpu.VMEM)
    anywhere = pl.BlockSpec(memory_space=pl.ANY)

    def remote(collective_id):
        return pltpu.CompilerParams(
            vmem_limit_bytes=VMEM_BYTES, collective_id=collective_id, has_side_effects=True
        )

    x3 = tokens.reshape(steps, group_rows, width)
    g3 = cotangent.reshape(steps, group_rows, width)
    combo = (routes[:, 0] + 16 * shift_region + 256 * valid_mask + 512).reshape(windows, WINDOW)
    combo = jnp.tile(jnp.pad(combo, ((0, 0), (0, PAD - WINDOW))), (1, 2))

    rows = per_group * PAD
    params = pltpu.CompilerParams(vmem_limit_bytes=VMEM_BYTES, dimension_semantics=("arbitrary",))

    def by_step(*shape):
        zeros = (0,) * (len(shape) - 1)
        return pl.BlockSpec(shape, lambda i: (i,) + zeros)

    def whole(*shape):
        zeros = (0,) * len(shape)
        return pl.BlockSpec(shape, lambda i, *_: zeros)

    lanes = width // 128
    token_specs = [by_step(1, group_rows, width), by_step(1, group_rows, width), by_step(per_group, 128)]
    forward_out = [
        by_step(rows, 2 * width),
        by_step(rows, width),
        by_step(rows, 128),
        by_step(rows, width),
        by_step(per_group, PAD, 3 * width),
        by_step(per_group, lanes, PAD, 4 * PAD),
        by_step(rows, 128),
        pl.BlockSpec((1, rows), lambda i: (0, i)),
        whole(1, 128),
    ]
    forward_shape = [
        jax.ShapeDtypeStruct((padded, 2 * width), bf16),
        jax.ShapeDtypeStruct((padded, width), f32),
        jax.ShapeDtypeStruct((padded, 128), f32),
        jax.ShapeDtypeStruct((padded, width), bf16),
        jax.ShapeDtypeStruct((windows, PAD, 3 * width), bf16),
        jax.ShapeDtypeStruct((windows, lanes, PAD, 4 * PAD), f32),
        jax.ShapeDtypeStruct((padded, 128), jnp.int32),
        jax.ShapeDtypeStruct((1, padded), jnp.int32),
        jax.ShapeDtypeStruct((1, 128), jnp.int32),
    ]
    forward_scratch = [
        pltpu.VMEM((rows, width), f32),
        pltpu.VMEM((rows, width), f32),
        pltpu.VMEM((group_rows, width), f32),
        pltpu.VMEM((rows, 1), jnp.int32),
        pltpu.VMEM((per_group, 1, 4 * PAD), jnp.int32),
        pltpu.VMEM((1, 128), f32),
    ]
    body = functools.partial(forward_kernel, dims, experts, slots, per_group, fast)
    if fast:
        own = (qkv_weight, proj_weight, router_weight.T, norm_params.T, expert_in, expert_out)
        *forward, w_all, w_exp = pl.pallas_call(
            body,
            grid=(steps,),
            in_specs=token_specs + [whole(*v.shape) for v in own],
            out_specs=forward_out + [anywhere, anywhere],
            out_shape=forward_shape
            + [
                jax.ShapeDtypeStruct((2, 2 * depth, shard, 2 * width + 128), bf16),
                jax.ShapeDtypeStruct((experts, 2, 2 * depth, shard, hidden), bf16),
            ],
            scratch_shapes=forward_scratch
            + [
                pltpu.VMEM((2, 2 * depth, shard, 2 * width + 128), bf16),
                pltpu.VMEM((2, shard, 2 * width + 128), bf16),
                pltpu.VMEM((2, shard, hidden), bf16),
                pltpu.SemaphoreType.DMA((1,)),
            ]
            + SharedGather.semaphores(depth)
            + Gather.semaphores(depth),
            compiler_params=remote(0),
            name="attention_forward",
        )(x3, g3, combo, *own)
    else:
        pack = jnp.concatenate([router_weight, norm_params], axis=1)
        pack = jnp.pad(pack, ((0, 0), (0, 128 - pack.shape[1])))
        shared_shard = jnp.stack(
            [
                jnp.concatenate([qkv_weight[:, : 2 * width], pack], axis=1),
                jnp.concatenate([qkv_weight[:, 2 * width :], proj_weight, pack], axis=1),
            ]
        ).astype(bf16)
        expert_shard = jnp.stack([expert_in[0], expert_out[0]]).astype(bf16)
        w_all = lax.all_gather(shared_shard, "dp", axis=1, tiled=True)
        w_exp = lax.all_gather(lax.all_gather(expert_shard, "dp", axis=1, tiled=True), "expert", axis=0, tiled=False)
        forward = pl.pallas_call(
            body,
            grid=(steps,),
            in_specs=token_specs + [whole(*w_all.shape)],
            out_specs=forward_out,
            out_shape=forward_shape,
            scratch_shapes=forward_scratch,
            compiler_params=params,
            name="attention_forward",
        )(x3, g3, combo, w_all)
    hz, y1, pr, attn, qkv, probs, key, key_row, counts = forward
    w_all = w_all.reshape(2, width, 2 * width + 128)
    w_exp = w_exp.reshape(experts, 2, width, hidden)

    grads, tok = pl.pallas_call(
        functools.partial(expert_kernel, slots),
        grid_spec=pltpu.PrefetchScalarGridSpec(
            num_scalar_prefetch=1,
            grid=(experts,),
            in_specs=[
                whole(padded, 2 * width),
                whole(1, padded),
                whole(padded, 128),
                pl.BlockSpec((1, 2, width, hidden), lambda e, *_: (e, 0, 0, 0)),
            ],
            out_specs=[
                pl.BlockSpec((1, 2, width, hidden), lambda e, *_: (e, 0, 0, 0)),
                whole(padded, 2 * width),
            ],
            scratch_shapes=[pltpu.VMEM((2, width, hidden), f32)],
        ),
        out_shape=[
            jax.ShapeDtypeStruct((experts, 2, width, hidden), bf16),
            jax.ShapeDtypeStruct((padded, 2 * width), f32),
        ],
        compiler_params=params,
        name="experts",
    )(counts[0], hz, key_row, key, w_exp)

    backward_in = (x3, g3, combo, w_all, tok, hz, y1, pr, attn, qkv, probs)
    backward_specs = token_specs + [
        whole(*w_all.shape),
        by_step(rows, 2 * width),
        by_step(rows, 2 * width),
        by_step(rows, width),
        by_step(rows, 128),
        by_step(rows, width),
        by_step(per_group, PAD, 3 * width),
        by_step(per_group, lanes, PAD, 4 * PAD),
    ]
    backward_out = [
        by_step(1, group_rows, width),
        by_step(1, group_rows, width),
        whole(4, width, width),
        whole(16, width),
    ]
    backward_shape = [
        jax.ShapeDtypeStruct((steps, group_rows, width), bf16),
        jax.ShapeDtypeStruct((steps, group_rows, width), f32),
        jax.ShapeDtypeStruct((4, width, width), bf16),
        jax.ShapeDtypeStruct((16, width), f32),
    ]
    backward_scratch = [
        pltpu.VMEM((rows, width), f32),
        pltpu.VMEM((rows, width), f32),
        pltpu.VMEM((group_rows, width), f32),
        pltpu.VMEM((rows, width), f32),
        pltpu.VMEM((rows, width), bf16),
        pltpu.VMEM((3, rows, width), bf16),
        pltpu.VMEM((4, width, width), f32),
        pltpu.VMEM((136, width), f32),
    ]
    body = functools.partial(backward_kernel, dims, experts, per_group, fast)
    if fast:
        out3, dx3, shared_grad, small_grad, g_exp = pl.pallas_call(
            body,
            grid=(steps,),
            in_specs=backward_specs + [anywhere],
            out_specs=backward_out + [whole(2, shard, hidden)],
            out_shape=backward_shape + [jax.ShapeDtypeStruct((2, shard, hidden), f32)],
            scratch_shapes=backward_scratch + Scatter.scratch(depth, hidden, shard),
            compiler_params=remote(1),
            name="attention_backward",
        )(*backward_in, grads.reshape(experts, 2, depth, 2, shard, hidden))
    else:
        out3, dx3, shared_grad, small_grad = pl.pallas_call(
            body,
            grid=(steps,),
            in_specs=backward_specs,
            out_specs=backward_out,
            out_shape=backward_shape,
            scratch_shapes=backward_scratch,
            compiler_params=params,
            name="attention_backward",
        )(*backward_in)
    block_output = out3.reshape(rows_here, width)
    input_grad = dx3.reshape(rows_here, width)

    weights_now = (qkv_weight, proj_weight, router_weight.T, norm_params.T, expert_in[0], expert_out[0])
    firsts_now = (qkv_first, proj_first, router_first.T, norm_first.T, in_first[0], out_first[0])
    seconds_now = (qkv_second, proj_second, router_second.T, norm_second.T, in_second[0], out_second[0])
    state = (*weights_now, *firsts_now, *seconds_now)
    if fast:
        shared, small, norms = pl.pallas_call(
            functools.partial(shared_scatter_kernel, depth, experts),
            in_specs=[vmem] * (3 + len(state)),
            out_specs=[vmem] * 3,
            out_shape=[
                jax.ShapeDtypeStruct((4, shard, width), f32),
                jax.ShapeDtypeStruct((16, shard), f32),
                jax.ShapeDtypeStruct((8, 128), f32),
            ],
            scratch_shapes=shared_scatter_scratch(depth, shard, width),
            compiler_params=remote(2),
            name="shared_scatter",
        )(shared_grad.reshape(2, 2, depth, 2, shard, width), small_grad, g_exp, *state)
    else:
        shared = lax.psum(shared_grad.astype(f32), ("expert", "dp"))
        small = lax.psum(small_grad, ("expert", "dp"))
        g_exp = lax.psum(grads.astype(f32), ("expert", "dp"))
        start = lax.axis_index("dp") * shard
        shared = lax.dynamic_slice_in_dim(shared, start, shard, axis=1)
        small = lax.dynamic_slice_in_dim(small, start, shard, axis=1)
        g_exp = lax.dynamic_index_in_dim(g_exp, lax.axis_index("expert"), 0, keepdims=False)
        g_exp = lax.dynamic_slice_in_dim(g_exp, start, shard, axis=1)
        reduced = (
            jnp.concatenate([shared[0], shared[1], shared[2]], axis=1),
            shared[3],
            small[0:experts],
            small[8:12],
            g_exp[0],
            g_exp[1],
        )
        steps_now = [lamb_parts(*entry)[2] for entry in zip(weights_now, reduced, firsts_now, seconds_now)]
        sums = jnp.stack([jnp.sum(v * v) for v in (*weights_now, *steps_now)])
        norms = jnp.broadcast_to(jnp.pad(lax.psum(sums, "dp"), (0, 128 - 12)), (8, 128))
    results = pl.pallas_call(
        functools.partial(update_kernel, experts),
        in_specs=[vmem] * (4 + len(state)),
        out_specs=[vmem] * (len(state) + 1),
        out_shape=[jax.ShapeDtypeStruct(v.shape, f32) for v in weights_now] * 3 + [jax.ShapeDtypeStruct((2, 6), f32)],
        compiler_params=pltpu.CompilerParams(vmem_limit_bytes=VMEM_BYTES),
        name="lamb_update",
    )(shared, small, g_exp, norms, *state)

    def restore(values):
        return (values[0], values[1], values[2].T, values[3].T, values[4][None], values[5][None])

    return (
        block_output,
        input_grad,
        *restore(results[0:6]),
        *restore(results[6:12]),
        *restore(results[12:18]),
        results[18].T[None],
    )


def solution(mesh):
    tok2 = P(("dp", "expert"), None)
    tok1 = P(("dp", "expert"))
    row = P("dp", None)
    exp = P("expert", "dp", None)
    shared4 = (row, row, row, row)
    placed = (tok2, tok2, tok2, tok1, tok1, *shared4, exp, exp, *shared4, *shared4, exp, exp, exp, exp)
    results = (tok2, tok2, *((*shared4, exp, exp) * 3), P("expert", None, None))
    dims = (mesh.shape["dp"], mesh.shape["expert"])
    return jax.shard_map(
        functools.partial(per_device, dims),
        mesh=mesh,
        in_specs=placed,
        out_specs=results,
        check_vma=False,
    )
```

```python
import functools

import jax
import jax.numpy as jnp
from jax import lax
from jax.experimental import pallas as pl
from jax.experimental.pallas import tpu as pltpu
from jax.sharding import PartitionSpec as P

HEADS = 12
HEAD_DIM = 32
WINDOW = 49
PAD = 64
STEP = 5
TILE = 256
NORM_EPS = 1e-05
MASKED = -1e30
BETA_ONE = 0.9
BETA_TWO = 0.999
ADAM_EPS = 1e-06
DECAY = 0.01
RATE = 0.3
VMEM_BYTES = 60 * 1024 * 1024

f32 = jnp.float32
bf16 = jnp.bfloat16


def dot_nn(a, b):
    return lax.dot_general(a, b, (((1,), (0,)), ((), ())), preferred_element_type=f32)


def dot_nt(a, b):
    return lax.dot_general(a, b, (((1,), (1,)), ((), ())), preferred_element_type=f32)


def dot_tn(a, b):
    return lax.dot_general(a, b, (((0,), (0,)), ((), ())), preferred_element_type=f32)


def norm_stats(v):
    width = v.shape[-1]
    mean = jnp.sum(v, axis=-1, keepdims=True) * (1.0 / width)
    centred = v - mean
    var = jnp.sum(centred * centred, axis=-1, keepdims=True) * (1.0 / width)
    rstd = lax.rsqrt(var + NORM_EPS)
    return centred * rstd, rstd


def norm_back(d, normed, rstd, gain):
    width = d.shape[-1]
    dn = d * gain
    m1 = jnp.sum(dn, axis=-1, keepdims=True) * (1.0 / width)
    m2 = jnp.sum(dn * normed, axis=-1, keepdims=True) * (1.0 / width)
    return rstd * (dn - m1 - normed * m2)


def head_masks():
    lane = lax.broadcasted_iota(jnp.int32, (PAD, 128), 1)
    return [lane // HEAD_DIM == h for h in range(4)]


def spread_heads(v, masks):
    zero = jnp.zeros_like(v)
    return jnp.concatenate([jnp.where(m, v, zero) for m in masks], axis=0)


def gather_heads(v, masks):
    out = jnp.where(masks[0], v[0:PAD], 0.0)
    for h in range(1, 4):
        out = jnp.where(masks[h], v[h * PAD : (h + 1) * PAD], out)
    return out


def weight_part(w_ref, part):
    width = (w_ref.shape[-1] - 128) // 2
    cols = slice((part % 2) * width, (part % 2 + 1) * width)
    if len(w_ref.shape) == 4:
        return w_ref[part // 2, :, :, cols].reshape(width, width)
    return w_ref[part // 2, :, cols]


def small_part(w_ref):
    width = (w_ref.shape[-1] - 128) // 2
    if len(w_ref.shape) == 4:
        return w_ref[0, :, :, 2 * width :].reshape(width, 128)
    return w_ref[0, :, 2 * width :]


def load_windows(src_ref, wide_ref, dst_ref, per_group):
    width = dst_ref.shape[-1]
    wide_ref[...] = src_ref[0].astype(f32)
    for k in range(per_group):
        dst_ref[k * PAD : k * PAD + WINDOW, :] = wide_ref[k * WINDOW : (k + 1) * WINDOW, :]
        dst_ref[k * PAD + WINDOW : (k + 1) * PAD, :] = jnp.zeros((PAD - WINDOW, width), f32)


def store_windows(src_ref, wide_ref, out_ref, per_group):
    for k in range(per_group):
        wide_ref[k * WINDOW : (k + 1) * WINDOW, :] = src_ref[k * PAD : k * PAD + WINDOW, :]
    out_ref[0] = wide_ref[...].astype(out_ref.dtype)


def token_columns(combo_ref, per_group):
    turned = jnp.transpose(combo_ref[...].astype(f32))
    return jnp.concatenate([turned[0:PAD, k : k + 1] for k in range(per_group)], axis=0).astype(jnp.int32)


def route_of(combo):
    return jnp.where(combo >= 512, combo & 15, -1)


def valid_of(combo):
    return ((combo >> 8) & 1).astype(f32)


def run_hooks(plan, step, index, w=None):
    for (k, i), jobs in plan.items():
        if i == index:
            due = step == k if w is None else (step == k) & (w == i)

            @pl.when(due)
            def _():
                for job in jobs:
                    job()


def forward_kernel(dims, experts, slots, per_group, fast, *refs):
    depth = dims[0] // 2
    plan = {}
    step = pl.program_id(0)
    if fast:
        x_ref, g_ref, combo_ref, qkv_w, proj_w, router_w, norm_w, in_w, out_w = refs[:9]
        hz_ref, pr_ref, attn_ref, qkv_ref, p_ref, key_ref, keyrow_ref, count_ref, ws_out, we_ref = refs[9:19]
        xp, gp, wide, codes, regions, carry, w_ref, sh, ex, ws_sem = refs[19:29]
        shared_sems, gather_sems = refs[29:36], refs[36:]
        gather = Gather(depth, ex, we_ref, gather_sems)
        shared = SharedGather(depth, sh, w_ref, shared_sems)

        def enter():
            meet(gather.z, gather.x, gather.y, gather.c, depth)
            width = qkv_w.shape[1] // 3
            shard = qkv_w.shape[0]
            small = jnp.concatenate([router_w[...], norm_w[...]], axis=0)
            small = jnp.concatenate([small, jnp.zeros((128 - small.shape[0], shard), f32)], axis=0)
            sh[0, :, 0 : 2 * width] = qkv_w[:, 0 : 2 * width].astype(bf16)
            sh[0, :, 2 * width :] = jnp.transpose(small).astype(bf16)
            sh[1, :, 0:width] = qkv_w[:, 2 * width :].astype(bf16)
            sh[1, :, width : 2 * width] = proj_w[...].astype(bf16)
            sh[1, :, 2 * width :] = jnp.zeros((shard, 128), bf16)
            shared.begin()
            ex[0] = in_w[0].astype(bf16)
            ex[1] = out_w[0].astype(bf16)
            gather.begin()

        def store_shared():
            pltpu.make_async_copy(w_ref, ws_out, ws_sem.at[0]).start()

        def leave():
            gather.finish()
            shared.finish()
            pltpu.make_async_copy(w_ref, ws_out, ws_sem.at[0]).wait()

        g = gather

        def first_weights():
            shared.along_z()
            gather.turns(0)
            shared.along_x()
            store_shared()
            gather.line(1)

        plan = {
            (0, "start"): [enter],
            (0, "norm"): [first_weights],
            (0, 7): [lambda: g.line(2)],
            (0, "end"): [lambda: g.turns(1)],
            (1, 1): [lambda: g.line(3)],
            (1, 5): [lambda: g.turns(2)],
            (2, "qkv"): [lambda: g.turns(3)],
            (2, "end"): [g.last, leave],
        }
    else:
        x_ref, g_ref, combo_ref, w_ref = refs[:4]
        hz_ref, pr_ref, attn_ref, qkv_ref, p_ref, key_ref, keyrow_ref, count_ref = refs[4:12]
        xp, gp, wide, codes, regions, carry = refs[12:18]
    rows = per_group * PAD
    width = x_ref.shape[-1]
    groups = width // 128
    run_hooks(plan, step, "start")
    load_windows(x_ref, wide, xp, per_group)
    load_windows(g_ref, wide, gp, per_group)

    @pl.when(step == 0)
    def _():
        carry[...] = jnp.zeros_like(carry)

    combo = token_columns(combo_ref, per_group)
    valid = valid_of(combo)
    route = route_of(combo)
    codes[...] = jnp.where((combo >> 8) & 1 == 1, (combo >> 4) & 15, -1)
    flat = combo_ref[...]
    flat = jnp.where(flat >= 512, (flat >> 4) & 15, -3)
    for k in range(per_group):
        regions[k] = jnp.concatenate([flat[k : k + 1, :]] * 2, axis=1)

    normed, _ = norm_stats(xp[...])
    run_hooks(plan, step, "norm")
    small = small_part(w_ref)
    small_t = jnp.transpose(small.astype(f32))
    a1, b1, a2, b2 = (small_t[experts + i : experts + i + 1, :] for i in range(4))
    h1 = (normed * a1 + b1).astype(bf16)
    for part in range(3):
        raw = dot_nn(h1, weight_part(w_ref, part))
        if part == 0:
            raw = raw * (HEAD_DIM**-0.5)
        qkv_ref[:, :, part * width : (part + 1) * width] = raw.astype(bf16).reshape(per_group, PAD, width)
    run_hooks(plan, step, "qkv")

    masks = head_masks()
    key_i = lax.broadcasted_iota(jnp.int32, (PAD, 4 * PAD), 0)
    lane_i = lax.broadcasted_iota(jnp.int32, (PAD, 4 * PAD), 1)
    diagonal = key_i == lax.rem(lane_i, PAD)

    def window(w, _):
        at = pl.ds(pl.multiple_of(w * PAD, PAD), PAD)
        allowed = (codes[at, :] == regions[w]) | diagonal
        for lg in range(groups):
            q = qkv_ref[w, :, lg * 128 : (lg + 1) * 128]
            k = qkv_ref[w, :, width + lg * 128 : width + (lg + 1) * 128]
            v = qkv_ref[w, :, 2 * width + lg * 128 : 2 * width + (lg + 1) * 128]
            s = dot_nt(k, spread_heads(q, masks))
            s = jnp.where(allowed, s, MASKED)
            e = jnp.exp(s - jnp.max(s, axis=0, keepdims=True))
            p = (e * (1.0 / jnp.sum(e, axis=0, keepdims=True))).astype(bf16)
            p_ref[w, lg] = p
            o = dot_tn(p, v)
            attn_ref[at, lg * 128 : (lg + 1) * 128] = gather_heads(o, masks).astype(bf16)
        for i in range(per_group):
            run_hooks(plan, step, i, w)
        return 0

    lax.fori_loop(0, per_group, window, 0)

    y1 = xp[...] + dot_nn(attn_ref[...], weight_part(w_ref, 3))
    normed2, _ = norm_stats(y1)
    h2 = (normed2 * a2 + b2).astype(bf16)
    lane = lax.broadcasted_iota(jnp.int32, (rows, 128), 1)
    logits = jnp.where(lane < experts, dot_nn(h2, small), MASKED)
    e = jnp.exp(logits - jnp.max(logits, axis=-1, keepdims=True))
    pr = e * (1.0 / jnp.sum(e, axis=-1, keepdims=True))
    pr_ref[...] = pr
    chosen = lane == route
    gate = jnp.sum(jnp.where(chosen, pr, 0.0), axis=-1, keepdims=True)
    gv = gp[...] * valid
    hz_ref[:, 0:width] = h2
    hz_ref[:, width : 2 * width] = (gate * gv).astype(bf16)

    onehot = jnp.where(chosen, 1.0, 0.0)
    before = lax.broadcasted_iota(jnp.int32, (rows, rows), 1) < lax.broadcasted_iota(jnp.int32, (rows, rows), 0)
    ranks = dot_nn(jnp.where(before, 1.0, 0.0).astype(bf16), onehot.astype(bf16)) + carry[0:1, :]
    slot = jnp.sum(ranks * onehot, axis=-1, keepdims=True)
    seen = jnp.sum(onehot, axis=-1, keepdims=True)
    key = (route.astype(f32) * slots + slot) * seen + (seen - 1.0)
    key = jnp.broadcast_to(key, (rows, 128))
    key_ref[...] = key.astype(jnp.int32)
    keyrow_ref[...] = jnp.transpose(key)[0:1, :].astype(jnp.int32)
    carry[...] = carry[...] + jnp.sum(onehot, axis=0, keepdims=True)
    count_ref[...] = carry[...].astype(jnp.int32)
    run_hooks(plan, step, "end")


def expert_kernel(slots, counts_ref, hz_ref, keyrow_ref, keycol_ref, we_ref, grad_ref, tok_ref, acc, tok_acc):
    e = pl.program_id(0)
    width = hz_ref.shape[-1] // 2
    total = hz_ref.shape[0]

    @pl.when(e == 0)
    def _():
        tok_acc[...] = jnp.zeros_like(tok_acc)

    acc[...] = jnp.zeros_like(acc)
    used = counts_ref[e]

    def tile(offset, size):
        base = e * slots + offset
        pick = keyrow_ref[...] == base + lax.broadcasted_iota(jnp.int32, (size, total), 0)
        both = dot_nn(jnp.where(pick, 1.0, 0.0).astype(bf16), hz_ref[...]).astype(bf16)
        rows, dz = both[:, 0:width], both[:, width : 2 * width]
        up = dot_nn(rows, we_ref[0, 0])
        cdf = 0.5 * (1.0 + lax.erf(up * 2.0**-0.5))
        hidden = (up * cdf).astype(bf16)
        slope = cdf + up * (jnp.exp(-0.5 * up * up) * (2.0 * jnp.pi) ** -0.5)
        ret = dot_nt(hidden, we_ref[0, 1]).astype(bf16)
        dup = (dot_nn(dz, we_ref[0, 1]) * slope).astype(bf16)
        back = dot_nt(dup, we_ref[0, 0]).astype(bf16)
        acc[1] += dot_tn(dz, hidden)
        acc[0] += dot_tn(rows, dup)
        keys = jnp.concatenate([keycol_ref[...]] * (size // 128), axis=1)
        put = keys == base + lax.broadcasted_iota(jnp.int32, (total, size), 1)
        tok_acc[...] += dot_nn(jnp.where(put, 1.0, 0.0).astype(bf16), jnp.concatenate([ret, back], axis=1))

    def large(t, _):
        tile(t * TILE, TILE)
        return 0

    count = (used + TILE // 2 - 1) // TILE
    lax.fori_loop(0, count, large, 0)

    @pl.when(used > count * TILE)
    def _():
        tile(count * TILE, TILE // 2)

    grad_ref[0] = acc[...].astype(bf16)

    @pl.when(e == pl.num_programs(0) - 1)
    def _():
        tok_ref[...] = tok_acc[...].astype(bf16)


def backward_kernel(dims, experts, per_group, fast, *refs):
    depth = dims[0] // 2
    plan = {}
    step = pl.program_id(0)
    combo_ref, sources, refs = refs[0], refs[1:9], refs[9:]
    if fast:
        ge_ref, state_hbm = refs[0], refs[1:19]
        out_ref, dx_ref, gexp_ref = refs[19:22]
        results = refs[22:25]
        refs = refs[25:]
    else:
        out_ref, dx_ref, shared_ref, small_ref = refs[:4]
        refs = refs[4:]
    xp, gp, wide, outp, dattn, dqkv, acc, acc_s = refs[:8]
    buffers, in_sem = refs[8:16], refs[16]
    w_ref = buffers[0]
    x_all, g_all, tok_all, pr_all, attn_all, qkv_all, p_all = buffers[1:]

    def fetch(i, k):
        if i == 0:
            return pltpu.make_async_copy(sources[0], w_ref, in_sem.at[0, 0])
        return pltpu.make_async_copy(sources[i].at[k], buffers[i].at[k], in_sem.at[i, k])

    def fetch_all():
        fetch(0, 0).start()
        for k in range(x_all.shape[0]):
            for i in range(1, 8):
                fetch(i, k).start()

    if fast:
        sc = Scatter(depth, ge_ref, refs[17:22], refs[22:31])
        state, state_sem, shared_ref, small_ref = refs[31:49], refs[49], refs[50], refs[51]

        def load_state(i):
            return pltpu.make_async_copy(state_hbm[i], state[i], state_sem.at[i])

        def enter():
            meet_all(depth, sc.z, sc.x, sc.y, sc.c)
            sc.begin()
            fetch_all()
            sc.merge(0)

        def start_state():
            for i in range(18):
                load_state(i).start()

        def meanwhile():
            for s in range(2):
                gexp_ref[s] = sc.result(s)
            for i in range(18):
                load_state(i).wait()

        def leave():
            for part in range(4):
                shape = shared_ref.shape[2:]
                shared_ref[part // 2, part % 2] = acc[part].astype(bf16).reshape(shape)
            small_ref[0:8] = acc_s[0:8]
            small_ref[8:16] = acc_s[128:136]
            shared_scatter(
                depth, experts, meanwhile, (shared_ref, small_ref, gexp_ref), state, results, refs[52:]
            )
            sc.finish()

        plan = {
            (0, "start"): [enter],
            (0, "pre"): [lambda: sc.merge(1)],
            (0, 3): [lambda: sc.second(0)],
            (1, "start"): [lambda: sc.merge(2), lambda: sc.second(1)],
            (1, "pre"): [lambda: sc.third(0), start_state],
            (1, 3): [lambda: sc.second(2), lambda: sc.merge(3)],
            (1, 7): [lambda: sc.third(1)],
            (2, "start"): [lambda: sc.third(2)],
            (2, "pre"): [lambda: sc.second(3)],
            (2, 4): [lambda: sc.third(3)],
            (2, "end"): [leave],
        }
    else:
        plan = {(0, "start"): [fetch_all]}
    rows = per_group * PAD
    width = x_all.shape[-1]
    groups = width // 128
    scale = HEAD_DIM**-0.5

    @pl.when(step == 0)
    def _():
        acc[...] = jnp.zeros_like(acc)
        acc_s[...] = jnp.zeros_like(acc_s)

    run_hooks(plan, step, "start")

    @pl.when(step == 0)
    def _():
        fetch(0, 0).wait()

    for i in range(1, 8):
        fetch(i, step).wait()
    load_windows(x_all.at[pl.ds(step, 1)], wide, xp, per_group)
    load_windows(g_all.at[pl.ds(step, 1)], wide, gp, per_group)
    combo = token_columns(combo_ref, per_group)
    valid = valid_of(combo)
    route = route_of(combo)
    small = small_part(w_ref)
    small_t = jnp.transpose(small.astype(f32))
    a1, b1, a2, b2 = (small_t[experts + i : experts + i + 1, :] for i in range(4))
    y1 = xp[...] + dot_nn(attn_all[step], weight_part(w_ref, 3))
    gv = gp[...] * valid
    z = tok_all[step, :, 0:width].astype(f32)
    lane = lax.broadcasted_iota(jnp.int32, (rows, 128), 1)
    chosen = lane == route
    pr = pr_all[step]
    gate = jnp.sum(jnp.where(chosen, pr, 0.0), axis=-1, keepdims=True)
    outp[...] = y1 + gate * z
    store_windows(outp, wide, out_ref, per_group)
    dgate = jnp.sum(gv * z, axis=-1, keepdims=True)
    kept = jnp.where(lane < experts, jnp.where(chosen, 1.0, 0.0) - pr, 0.0)
    dlogits = (dgate * gate * kept).astype(bf16)
    n2, r2 = norm_stats(y1)
    h2 = (n2 * a2 + b2).astype(bf16)
    acc_s[0:128] += dot_tn(dlogits, h2)
    dh2 = dot_nt(dlogits, small) + tok_all[step, :, width : 2 * width].astype(f32)
    acc_s[130:131] += jnp.sum(dh2 * n2, axis=0, keepdims=True)
    acc_s[131:132] += jnp.sum(dh2, axis=0, keepdims=True)
    dy1 = gv + norm_back(dh2, n2, r2, a2)
    gp[...] = dy1
    da = dy1.astype(bf16)
    acc[3] += dot_tn(attn_all[step], da)
    dattn[...] = dot_nt(da, weight_part(w_ref, 3)).astype(bf16)
    run_hooks(plan, step, "pre")

    masks = head_masks()

    def window(w, _):
        at = pl.ds(pl.multiple_of(w * PAD, PAD), PAD)
        for lg in range(groups):
            cols = slice(lg * 128, (lg + 1) * 128)
            q = qkv_all[step, w, :, lg * 128 : (lg + 1) * 128]
            k = qkv_all[step, w, :, width + lg * 128 : width + (lg + 1) * 128]
            v = qkv_all[step, w, :, 2 * width + lg * 128 : 2 * width + (lg + 1) * 128]
            d_all = spread_heads(dattn[at, cols], masks)
            q_all = spread_heads(q, masks)
            p_low = p_all[step, w, lg]
            p = p_low.astype(f32)
            dp = dot_nt(v, d_all)
            ds = (p * (dp - jnp.sum(dp * p, axis=0, keepdims=True))).astype(bf16)
            dv = dot_nn(p_low, d_all)
            dk = dot_nn(ds, q_all)
            dq = gather_heads(dot_tn(ds, k), masks) * scale
            dqkv[0, at, cols] = dq.astype(bf16)
            dqkv[1, at, cols] = dk.astype(bf16)
            dqkv[2, at, cols] = dv.astype(bf16)
        for i in range(per_group):
            run_hooks(plan, step, i, w)
        return 0

    lax.fori_loop(0, per_group, window, 0)

    n1, r1 = norm_stats(xp[...])
    h1 = (n1 * a1 + b1).astype(bf16)
    dh1 = jnp.zeros((rows, width), f32)
    for part in range(3):
        dpart = dqkv[part]
        acc[part] += dot_tn(h1, dpart)
        dh1 = dh1 + dot_nt(dpart, weight_part(w_ref, part))
    acc_s[128:129] += jnp.sum(dh1 * n1, axis=0, keepdims=True)
    acc_s[129:130] += jnp.sum(dh1, axis=0, keepdims=True)
    outp[...] = gp[...] + norm_back(dh1, n1, r1, a1)
    store_windows(outp, wide, dx_ref, per_group)

    if not fast:

        @pl.when(step == pl.num_programs(0) - 1)
        def _():
            for part in range(4):
                shared_ref[part] = acc[part].astype(bf16)
            small_ref[0:8] = acc_s[0:8]
            small_ref[8:16] = acc_s[128:136]

    run_hooks(plan, step, "end")


def place():
    dp, ex = lax.axis_index("dp"), lax.axis_index("expert")
    return lax.div(dp, 2), lax.rem(dp, 2), lax.div(ex, 2), lax.rem(ex, 2)


def at(z, x, y, c):
    return (z * 2 + x, y * 2 + c)


def push(src, dst, send_sem, recv_sem, device):
    copy = pltpu.make_async_remote_copy(
        src_ref=src,
        dst_ref=dst,
        send_sem=send_sem,
        recv_sem=recv_sem,
        device_id=device,
        device_id_type=pl.DeviceIdType.MESH,
    )
    return copy


def meet(z, x, y, c, depth):
    barrier = pltpu.get_barrier_semaphore()

    def greet(device):
        pl.semaphore_signal(barrier, inc=1, device_id=device, device_id_type=pl.DeviceIdType.MESH)

    greet(at(z, x, y, 1 - c))
    greet(at(z, 1 - x, y, c))
    greet(at(z, x, 1 - y, c))
    for other in range(depth):
        @pl.when(z != other)
        def _():
            greet(at(other, x, y, c))

    pl.semaphore_wait(barrier, 3 + depth - 1)


class Gather:
    def __init__(self, depth, ex_ref, we_ref, sems):
        self.depth = depth
        self.ex, self.we = ex_ref, we_ref
        (self.loc, self.zs, self.zr, self.xs, self.xr, self.ys, self.yr, self.cs, self.cr) = sems
        self.z, self.x, self.y, self.c = place()

    @staticmethod
    def semaphores(depth):
        dma = pltpu.SemaphoreType.DMA
        return [
            dma((1,)),
            dma((2, depth)),
            dma((depth,)),
            dma((3, depth)),
            dma((3, depth)),
            dma((3, depth)),
            dma((3, depth)),
            dma((7, depth)),
            dma((7, depth)),
        ]

    def local(self):
        return pltpu.make_async_copy(self.ex, self.pair(self.y, self.c, self.z, self.x), self.loc.at[0])

    def block(self, y, c, s, z, x):
        return self.we.at[y * 2 + c, s, z * 2 + x]

    def pair(self, y, c, z, x):
        return self.we.at[y * 2 + c, :, z * 2 + x]

    def z_copy(self, up, zo, first=False):
        mine = self.ex if first else self.pair(self.y, self.c, zo, self.x)
        target = self.z + 1 if up else self.z - 1
        return push(
            mine,
            self.pair(self.y, self.c, zo, self.x),
            self.zs.at[0 if up else 1, zo],
            self.zr.at[zo],
            at(target, self.x, self.y, self.c),
        )

    def x_copy(self, kind, zo, y, first=False):
        s = 0 if kind == 0 else 1
        dst = self.block(y, self.c, s, zo, self.x)
        src = self.ex.at[s] if first else dst
        return push(src, dst, self.xs.at[kind, zo], self.xr.at[kind, zo], at(self.z, 1 - self.x, self.y, self.c))

    def y_copy(self, kind, zo, x, first=False):
        s = 1 if kind == 0 else 0
        dst = self.block(self.y, self.c, s, zo, x)
        src = self.ex.at[s] if first else dst
        return push(src, dst, self.ys.at[kind, zo], self.yr.at[kind, zo], at(self.z, self.x, 1 - self.y, self.c))

    def c_copy(self, kind, zo, c, first=False):
        x, y = self.x, self.y
        if kind == 0:
            dst = self.pair(y, c, zo, x)
        elif kind == 1:
            dst = self.block(y, c, 0, zo, 1 - x)
        elif kind == 2:
            dst = self.block(1 - y, c, 1, zo, x)
        elif kind in (3, 4):
            dst = self.block(1 - y, c, 0, zo, x if kind == 3 else 1 - x)
        else:
            dst = self.block(y if kind == 5 else 1 - y, c, 1, zo, 1 - x)
        src = self.ex if first else dst
        return push(src, dst, self.cs.at[kind, zo], self.cr.at[kind, zo], at(self.z, x, y, 1 - self.c))

    def spread(self, zo, first=False):
        self.x_copy(0, zo, self.y, first).start()
        self.y_copy(0, zo, self.x, first).start()
        self.y_copy(1, zo, self.x, first).start()
        self.x_copy(1, zo, self.y, first).start()
        self.c_copy(0, zo, self.c, first).start()

    def begin(self):
        z = self.z
        self.local().start()

        @pl.when(z < self.depth - 1)
        def _():
            self.z_copy(True, z, True).start()

        @pl.when(z > 0)
        def _():
            self.z_copy(False, z, True).start()

        self.spread(z, True)

    def line(self, s):
        z = self.z

        @pl.when(z - s >= 0)
        def _():
            self.z_copy(True, z - s).wait_recv()

            @pl.when(z < self.depth - 1)
            def _():
                self.z_copy(True, z - s).start()

            self.spread(z - s)

        @pl.when(z + s < self.depth)
        def _():
            self.z_copy(True, z + s).wait_recv()

            @pl.when(z > 0)
            def _():
                self.z_copy(False, z + s).start()

            self.spread(z + s)

    def turn(self, zo):
        self.x_copy(0, zo, self.y).wait_recv()
        self.y_copy(2, zo, 1 - self.x).start()
        self.c_copy(1, zo, self.c).start()
        self.y_copy(0, zo, self.x).wait_recv()
        self.x_copy(2, zo, 1 - self.y).start()
        self.c_copy(2, zo, self.c).start()

    def turns(self, s):
        z = self.z
        if s == 0:
            self.turn(z)
            return

        @pl.when(z - s >= 0)
        def _():
            self.turn(z - s)

        @pl.when(z + s < self.depth)
        def _():
            self.turn(z + s)

    def last(self):
        for zo in range(self.depth):
            for kind, ck in ((1, 3), (2, 4)):
                self.y_copy(kind, zo, self.x).wait_recv()
                self.c_copy(ck, zo, self.c).start()
            for kind, ck in ((1, 5), (2, 6)):
                self.x_copy(kind, zo, self.y).wait_recv()
                self.c_copy(ck, zo, self.c).start()

    def finish(self):
        z = self.z
        for zo in range(self.depth):
            for kind in range(7):
                self.c_copy(kind, zo, 1 - self.c).wait_recv()
        self.local().wait()
        for zo in range(self.depth):
            @pl.when((z < self.depth - 1) & (zo <= z))
            def _():
                self.z_copy(True, zo).wait_send()

            @pl.when((z > 0) & (zo >= z))
            def _():
                self.z_copy(False, zo).wait_send()

            for kind in range(3):
                self.x_copy(kind, zo, self.y).wait_send()
                self.y_copy(kind, zo, self.x).wait_send()
            for kind in range(7):
                self.c_copy(kind, zo, self.c).wait_send()


class SharedGather:
    def __init__(self, depth, sh_ref, ws_ref, sems):
        self.depth, self.sh, self.ws = depth, sh_ref, ws_ref
        self.loc, self.zs, self.zr, self.xs, self.xr, self.cs, self.cr = sems
        self.z, self.x, self.y, self.c = place()

    @staticmethod
    def semaphores(depth):
        dma = pltpu.SemaphoreType.DMA
        return [dma((1,)), dma((depth,)), dma((depth,)), dma((depth,)), dma((depth,)), dma((2, depth)), dma((2, depth))]

    def slot(self, zo, xo):
        return self.ws.at[self.c, zo * 2 + xo]

    def local(self):
        return pltpu.make_async_copy(self.sh.at[self.c], self.slot(self.z, self.x), self.loc.at[0])

    def z_copy(self, target):
        return push(
            self.sh.at[self.c],
            self.slot(self.z, self.x),
            self.zs.at[target],
            self.zr.at[self.z],
            at(target, self.x, self.y, self.c),
        )

    def z_from(self, zo):
        dst = self.slot(zo, self.x)
        return push(dst, dst, self.zs.at[zo], self.zr.at[zo], at(zo, self.x, self.y, self.c))

    def x_copy(self, zo, first=False):
        dst = self.slot(zo, self.x)
        src = self.sh.at[self.c] if first else dst
        return push(src, dst, self.xs.at[zo], self.xr.at[zo], at(self.z, 1 - self.x, self.y, self.c))

    def c_copy(self, zo, xo, first=False):
        dst = self.slot(zo, xo)
        src = self.sh.at[self.c] if first else dst
        return push(src, dst, self.cs.at[xo, zo], self.cr.at[xo, zo], at(self.z, self.x, self.y, 1 - self.c))

    def others(self):
        return [lax.rem(self.z + j, self.depth) for j in range(1, self.depth)]

    def begin(self):
        self.local().start()
        for zo in self.others():
            self.z_copy(zo).start()
        self.x_copy(self.z, True).start()
        self.c_copy(self.z, self.x, True).start()

    def along_z(self):
        for zo in self.others():
            self.z_from(zo).wait_recv()
            self.x_copy(zo).start()
            self.c_copy(zo, self.x).start()

    def along_x(self):
        for j in range(self.depth):
            zo = lax.rem(self.z + j, self.depth)
            self.x_copy(zo).wait_recv()
            self.c_copy(zo, 1 - self.x).start()
        for zo in range(self.depth):
            for xo in range(2):
                self.c_copy(zo, xo).wait_recv()
        self.local().wait()

    def finish(self):
        for zo in self.others():
            self.z_copy(zo).wait_send()
        for zo in range(self.depth):
            self.x_copy(zo).wait_send()
            for xo in range(2):
                self.c_copy(zo, xo).wait_send()


class Scatter:
    def __init__(self, depth, ge_ref, bufs, sems):
        self.depth = depth
        self.ge = ge_ref
        self.t, self.rc, self.r1, self.r2, self.r3 = bufs
        (self.ls, self.cs, self.cr, self.s1, self.q1, self.s2, self.q2, self.s3, self.q3) = sems
        self.z, self.x, self.y, self.c = place()

    @staticmethod
    def scratch(depth, cols, shard):
        dma = pltpu.SemaphoreType.DMA
        bufs = [
            pltpu.VMEM((2, 2, depth, 2, shard, cols), bf16),
            pltpu.VMEM((2, 2, depth, 2, shard, cols), bf16),
            pltpu.VMEM((2, depth, 2, shard, cols), bf16),
            pltpu.VMEM((2, depth, shard, cols), bf16),
            pltpu.VMEM((2, depth, shard, cols), bf16),
        ]
        sems = [
            dma((2, 2, depth)),
            dma((2, 2, depth)),
            dma((2, 2, depth)),
            dma((2, depth, 2)),
            dma((2, depth, 2)),
            dma((2, depth)),
            dma((2, depth)),
            dma((2, depth)),
            dma((2, depth)),
        ]
        return bufs + sems

    def local(self, i, s, zo):
        y = self.y if i == 0 else 1 - self.y
        return pltpu.make_async_copy(self.ge.at[y * 2 + self.c, s, zo], self.t.at[i, s, zo], self.ls.at[i, s, zo])

    def core(self, i, s, zo):
        y = self.y if i == 0 else 1 - self.y
        return push(
            self.ge.at[y * 2 + 1 - self.c, s, zo],
            self.rc.at[i, s, zo],
            self.cs.at[i, s, zo],
            self.cr.at[i, s, zo],
            at(self.z, self.x, self.y, 1 - self.c),
        )

    def one(self, s, zo, k):
        if s == 0:
            src, device = self.t.at[1, 0, zo, k], at(self.z, self.x, 1 - self.y, self.c)
        else:
            src, device = self.t.at[k, 1, zo, 1 - self.x], at(self.z, 1 - self.x, self.y, self.c)
        return push(src, self.r1.at[s, zo, k], self.s1.at[s, zo, k], self.q1.at[s, zo, k], device)

    def two(self, s, zo):
        if s == 0:
            src, device = self.t.at[0, 0, zo, 1 - self.x], at(self.z, 1 - self.x, self.y, self.c)
        else:
            src, device = self.t.at[1, 1, zo, self.x], at(self.z, self.x, 1 - self.y, self.c)
        return push(src, self.r2.at[s, zo], self.s2.at[s, zo], self.q2.at[s, zo], device)

    def three(self, s, zo):
        return push(
            self.t.at[0, s, zo, self.x],
            self.r3.at[s, self.z],
            self.s3.at[s, zo],
            self.q3.at[s, self.z],
            at(zo, self.x, self.y, self.c),
        )

    def arrived(self, s, zo):
        return push(
            self.r3.at[s, zo], self.r3.at[s, zo], self.s3.at[s, zo], self.q3.at[s, zo], at(zo, self.x, self.y, self.c)
        )

    def begin(self):
        def body(j, _):
            zo = self.order(j)
            for i, s in ((1, 0), (0, 1), (1, 1), (0, 0)):
                self.core(i, s, zo).start()
                self.local(i, s, zo).start()
            return 0

        lax.fori_loop(0, self.depth, body, 0)

    def order(self, j):
        return lax.rem(self.z + j + 1, self.depth)

    def fold(self, ref, other):
        ref[...] = (ref[...].astype(f32) + other[...].astype(f32)).astype(bf16)

    def merge(self, j):
        zo = self.order(j)
        for i, s in ((1, 0), (0, 1), (1, 1), (0, 0)):
            self.core(i, s, zo).wait_recv()
            self.local(i, s, zo).wait()
            for xo in range(2):
                self.fold(self.t.at[i, s, zo, xo], self.rc.at[i, s, zo, xo])
            if (i, s) == (1, 0):
                self.one(0, zo, 0).start()
                self.one(0, zo, 1).start()
            if s == 1:
                self.one(1, zo, i).start()

    def second(self, j):
        zo = self.order(j)
        for k in range(2):
            self.one(0, zo, k).wait_recv()
            self.fold(self.t.at[0, 0, zo, k], self.r1.at[0, zo, k])
        self.two(0, zo).start()
        for k in range(2):
            self.one(1, zo, k).wait_recv()
            self.fold(self.t.at[k, 1, zo, self.x], self.r1.at[1, zo, k])
        self.two(1, zo).start()

    def third(self, j):
        zo = self.order(j)
        for s in range(2):
            self.two(s, zo).wait_recv()
            self.fold(self.t.at[0, s, zo, self.x], self.r2.at[s, zo])

            @pl.when(zo != self.z)
            def _():
                self.three(s, zo).start()

    def result(self, s):
        total = self.t[0, s, self.z, self.x].astype(f32)
        for j in range(1, self.depth):
            zo = lax.rem(self.z + j, self.depth)
            self.arrived(s, zo).wait_recv()
            total = total + self.r3[s, zo].astype(f32)
        return total

    def finish(self):
        def body(j, _):
            zo = self.order(j)
            for s in range(2):
                for i in range(2):
                    self.core(i, s, zo).wait_send()
                for k in range(2):
                    self.one(s, zo, k).wait_send()
                self.two(s, zo).wait_send()

                @pl.when(zo != self.z)
                def _():
                    self.three(s, zo).wait_send()

            return 0

        lax.fori_loop(0, self.depth, body, 0)


def lamb_parts(weight, grad, first, second):
    first_new = BETA_ONE * first + (1.0 - BETA_ONE) * grad
    second_new = BETA_TWO * second + (1.0 - BETA_TWO) * grad * grad
    first_hat = first_new / (1.0 - BETA_ONE**STEP)
    second_hat = second_new / (1.0 - BETA_TWO**STEP)
    direction = first_hat / (jnp.sqrt(second_hat) + ADAM_EPS) + DECAY * weight
    return first_new, second_new, direction


def row_norms(values, lane0):
    lane = lax.broadcasted_iota(jnp.int32, (1, 128), 1)
    out = jnp.zeros((1, 128), f32)
    for i, v in enumerate(values):
        out = out + jnp.where(lane == lane0 + i, jnp.sum(v * v), 0.0)
    return out


def peers(n, me):
    return [lax.rem(me + j, n) for j in range(1, n)]


def meet_all(depth, z, x, y, c):
    barrier = pltpu.get_barrier_semaphore()
    dp, ex = z * 2 + x, y * 2 + c
    n_dp, n_ex = 2 * depth, 4
    for other in peers(n_dp, dp):
        pl.semaphore_signal(barrier, inc=1, device_id=(other, ex), device_id_type=pl.DeviceIdType.MESH)
    for other in peers(n_ex, ex):
        pl.semaphore_signal(barrier, inc=1, device_id=(dp, other), device_id_type=pl.DeviceIdType.MESH)
    pl.semaphore_wait(barrier, n_dp + n_ex - 2)


def shared_scatter(depth, experts, meanwhile, operands, state, outputs, scratch):
    gs_ref, sm_ref, ge_ref = operands
    weights, firsts, seconds = state[0:6], state[6:12], state[12:18]
    fs_out, gsm_ref, norm_ref = outputs
    (t, rc, r1, r2, r3, src_c, src_y, src_x, sz, cur, wide, nb, nq, fs_ref) = scratch[:14]
    (ccs, ccr, s1, q1, s2, q2, s3, q3, s4, q4, ms, mr, zs, zr, ns, nr, es, er) = scratch[14:]
    z, x, y, c = place()
    dp, ex = z * 2 + x, y * 2 + c
    n_dp, n_ex = 2 * depth, 4
    shard = fs_ref.shape[1]
    width = fs_ref.shape[2]

    near = [at(z, x, y, 1 - c), at(z, x, 1 - y, c), at(z, 1 - x, y, c)]
    y_of = [y, 1 - y]

    def core(i):
        return push(gs_ref.at[y_of[i], 1 - c], rc.at[i], ccs.at[i], ccr.at[i], near[0])

    def one(zo, k):
        if zo % 2 == 0:
            return push(t.at[1, zo, k], r1.at[zo, k], s1.at[zo, k], q1.at[zo, k], near[1])
        return push(t.at[k, zo, 1 - x], r1.at[zo, k], s1.at[zo, k], q1.at[zo, k], near[2])

    def two(zo):
        if zo % 2 == 0:
            return push(t.at[0, zo, 1 - x], r2.at[zo], s2.at[zo], q2.at[zo], near[2])
        return push(t.at[1, zo, x], r2.at[zo], s2.at[zo], q2.at[zo], near[1])

    def three(zo):
        return push(t.at[0, zo, x], r3.at[z], s3.at[zo], q3.at[z], at(zo, x, y, c))

    def arrived(zo):
        return push(r3.at[zo], r3.at[zo], s3.at[zo], q3.at[zo], at(zo, x, y, c))

    def small_hop(k):
        src = sm_ref if k == 0 else cur.at[k - 1]
        return push(src, (src_c, src_y, src_x)[k], ms.at[k], mr.at[k], near[k])

    def small_z(zo):
        return push(cur.at[2], sz.at[z], zs.at[zo], zr.at[z], at(zo, x, y, c))

    def small_from(zo):
        return push(sz.at[zo], sz.at[zo], zs.at[zo], zr.at[zo], at(zo, x, y, c))

    def fold(ref, a, b):
        ref[...] = (a[...].astype(f32) + b[...].astype(f32)).astype(bf16)

    small_hop(0).start()
    core(1).start()
    core(0).start()
    meanwhile()
    totals = row_norms([w[...] for w in weights], 0)
    for i in range(2):
        direction = lamb_parts(weights[4 + i][...], ge_ref[i], firsts[4 + i][...], seconds[4 + i][...])[2]
        totals = totals + row_norms([direction], 10 + i)
    small_hop(0).wait_recv()
    cur[0] = sm_ref[...] + src_c[...]
    small_hop(1).start()
    for i in (1, 0):
        core(i).wait_recv()
        for zo in range(depth):
            for k in range(2):
                fold(t.at[i, zo, k], gs_ref.at[y_of[i], c, zo, k], rc.at[i, zo, k])
            if zo % 2 == 0:
                if i == 1:
                    one(zo, 0).start()
                    one(zo, 1).start()
            else:
                one(zo, i).start()
    small_hop(1).wait_recv()
    cur[1] = cur[0] + src_y[...]
    small_hop(2).start()
    for zo in range(depth):
        for k in range(2):
            one(zo, k).wait_recv()
            target = t.at[0, zo, k] if zo % 2 == 0 else t.at[k, zo, x]
            fold(target, target, r1.at[zo, k])
        two(zo).start()
    small_hop(2).wait_recv()
    cur[2] = cur[1] + src_x[...]
    sz[z] = cur[2]
    for zo in range(depth):
        @pl.when(zo != z)
        def _():
            small_z(zo).start()

    for zo in range(depth):
        two(zo).wait_recv()
        target = t.at[0, zo, x]
        fold(target, target, r2.at[zo])

        @pl.when(zo != z)
        def _():
            three(zo).start()

    total = t[0, z, x].astype(f32)
    for zo in peers(depth, z):
        arrived(zo).wait_recv()
        total = total + r3[zo].astype(f32)
    fs_ref[ex] = total

    def four(e):
        return push(fs_ref.at[ex], fs_ref.at[ex], s4.at[e], q4.at[ex], (dp, e))

    def four_from(e):
        return push(fs_ref.at[e], fs_ref.at[e], s4.at[e], q4.at[e], (dp, e))

    def quarter(e):
        return push(nq.at[ex], nq.at[ex], es.at[e], er.at[ex], (dp, e))

    def quarter_from(e):
        return push(nq.at[e], nq.at[e], es.at[e], er.at[e], (dp, e))

    def part_of(refs):
        out = refs[1][...]
        for p in range(3):
            out = jnp.where(ex == p, refs[0][:, p * width : (p + 1) * width], out)
        return out

    direction = lamb_parts(part_of(weights), total, part_of(firsts), part_of(seconds))[2]
    lane = lax.broadcasted_iota(jnp.int32, (8, 128), 1)
    nq[ex] = jnp.where(lane == jnp.where(ex == 3, 7, 6), jnp.sum(direction * direction), 0.0)
    for e in peers(n_ex, ex):
        quarter(e).start()
    for e in peers(n_ex, ex):
        four(e).start()
    for zo in peers(depth, z):
        small_from(zo).wait_recv()
    small = sz[0]
    for zo in range(1, depth):
        small = small + sz[zo]
    wide[...] = jnp.transpose(jnp.concatenate([small, jnp.zeros((128 - 16, small.shape[1]), f32)], axis=0))
    mine = jnp.transpose(wide[pl.ds(pl.multiple_of(dp * shard, 16), shard), :])[0:16]
    gsm_ref[...] = mine
    for i, g in ((2, mine[0:experts]), (3, mine[8:12])):
        direction = lamb_parts(weights[i][...], g, firsts[i][...], seconds[i][...])[2]
        totals = totals + row_norms([direction], 6 + i)
    for e in peers(n_ex, ex):
        quarter_from(e).wait_recv()
    combined = jnp.broadcast_to(totals, (8, 128))
    for e in range(n_ex):
        combined = combined + nq[e]
    nb[dp] = combined

    def norm_push(r):
        return push(nb.at[dp], nb.at[dp], ns.at[r], nr.at[dp], (r, ex))

    def norm_from(r):
        return push(nb.at[r], nb.at[r], ns.at[r], nr.at[r], (r, ex))

    for r in peers(n_dp, dp):
        norm_push(r).start()
    for e in peers(n_ex, ex):
        four_from(e).wait_recv()
    fs_out[...] = fs_ref[...]
    for r in peers(n_dp, dp):
        norm_from(r).wait_recv()
    summed = nb[0]
    for r in range(1, n_dp):
        summed = summed + nb[r]
    norm_ref[...] = summed
    for e in peers(n_ex, ex):
        quarter(e).wait_send()

    for r in peers(n_dp, dp):
        norm_push(r).wait_send()
    for e in peers(n_ex, ex):
        four(e).wait_send()
    for i in range(2):
        core(i).wait_send()
    for k in range(3):
        small_hop(k).wait_send()
    for zo in range(depth):
        for k in range(2):
            one(zo, k).wait_send()
        two(zo).wait_send()

        @pl.when(zo != z)
        def _():
            three(zo).wait_send()
            small_z(zo).wait_send()


def shared_scatter_scratch(depth, shard, width):
    dma = pltpu.SemaphoreType.DMA
    return [
        pltpu.VMEM((2, depth, 2, shard, width), bf16),
        pltpu.VMEM((2, depth, 2, shard, width), bf16),
        pltpu.VMEM((depth, 2, shard, width), bf16),
        pltpu.VMEM((depth, shard, width), bf16),
        pltpu.VMEM((depth, shard, width), bf16),
        pltpu.VMEM((16, width), f32),
        pltpu.VMEM((16, width), f32),
        pltpu.VMEM((16, width), f32),
        pltpu.VMEM((depth, 16, width), f32),
        pltpu.VMEM((3, 16, width), f32),
        pltpu.VMEM((width, 128), f32),
        pltpu.VMEM((2 * depth, 8, 128), f32),
        pltpu.VMEM((4, 8, 128), f32),
        pltpu.VMEM((4, shard, width), f32),
        dma((2,)),
        dma((2,)),
        dma((depth, 2)),
        dma((depth, 2)),
        dma((depth,)),
        dma((depth,)),
        dma((depth,)),
        dma((depth,)),
        dma((4,)),
        dma((4,)),
        dma((3,)),
        dma((3,)),
        dma((depth,)),
        dma((depth,)),
        dma((2 * depth,)),
        dma((2 * depth,)),
        dma((4,)),
        dma((4,)),
    ]


def update_kernel(experts, *refs):
    (gsh_ref, gsm_ref, ge_ref, norm_ref), weights, firsts, seconds = refs[:4], refs[4:10], refs[10:16], refs[16:22]
    w_out, m_out, s_out = refs[22:28], refs[28:34], refs[34:40]
    trust_ref = refs[40]
    width = gsh_ref.shape[2]
    totals = norm_ref[0:1, :]
    lane = lax.broadcasted_iota(jnp.int32, (1, 128), 1)

    def pick(i):
        return jnp.sqrt(jnp.sum(jnp.where(lane == i, totals, 0.0), axis=-1, keepdims=True))

    row = lax.broadcasted_iota(jnp.int32, (2, 6), 1)
    col = lax.broadcasted_iota(jnp.int32, (2, 6), 0)
    trust = jnp.zeros((2, 6), f32)
    whole = slice(None)
    jobs = [(0, slice(p * width, (p + 1) * width), lambda p=p: gsh_ref[p]) for p in range(3)]
    jobs += [(1, whole, lambda: gsh_ref[3]), (2, whole, lambda: gsm_ref[0:experts]), (3, whole, lambda: gsm_ref[8:12])]
    jobs += [(4, whole, lambda: ge_ref[0]), (5, whole, lambda: ge_ref[1])]
    ratios = []
    for i in range(6):
        wn, un = pick(i), pick(6 + i)
        ratios.append(wn / (un + 1e-06))
        trust = jnp.where((row == i) & (col == 0), wn, jnp.where((row == i) & (col == 1), un, trust))
    trust_ref[...] = trust
    for i, cols, grad in jobs:
        weight = weights[i][:, cols]
        first, second, direction = lamb_parts(weight, grad(), firsts[i][:, cols], seconds[i][:, cols])
        w_out[i][:, cols] = weight - RATE * ratios[i] * direction
        m_out[i][:, cols] = first
        s_out[i][:, cols] = second


def per_device(
    dims,
    tokens,
    cotangent,
    routes,
    valid_mask,
    shift_region,
    qkv_weight,
    proj_weight,
    router_weight,
    norm_params,
    expert_in,
    expert_out,
    qkv_first,
    qkv_second,
    proj_first,
    proj_second,
    router_first,
    router_second,
    norm_first,
    norm_second,
    in_first,
    in_second,
    out_first,
    out_second,
):
    rows_here, width = tokens.shape
    experts = router_weight.shape[1]
    hidden = expert_in.shape[2]
    shard = qkv_weight.shape[0]
    capacity = 2 * rows_here // experts
    slots = -(-capacity // TILE) * TILE
    windows = rows_here // WINDOW
    per_group = 8
    steps = windows // per_group
    group_rows = per_group * WINDOW
    padded = windows * PAD

    fast = dims == (8, 4)
    depth = dims[0] // 2
    vmem = pl.BlockSpec(memory_space=pltpu.VMEM)
    anywhere = pl.BlockSpec(memory_space=pl.ANY)

    def remote(collective_id):
        return pltpu.CompilerParams(
            vmem_limit_bytes=VMEM_BYTES, collective_id=collective_id, has_side_effects=True
        )

    x3 = tokens.reshape(steps, group_rows, width)
    g3 = cotangent.reshape(steps, group_rows, width)
    combo = (routes[:, 0] + 16 * shift_region + 256 * valid_mask + 512).reshape(windows, WINDOW)
    combo = jnp.tile(jnp.pad(combo, ((0, 0), (0, PAD - WINDOW))), (1, 2))

    rows = per_group * PAD
    params = pltpu.CompilerParams(vmem_limit_bytes=VMEM_BYTES, dimension_semantics=("arbitrary",))

    def by_step(*shape):
        zeros = (0,) * (len(shape) - 1)
        return pl.BlockSpec(shape, lambda i: (i,) + zeros)

    def whole(*shape):
        zeros = (0,) * len(shape)
        return pl.BlockSpec(shape, lambda i, *_: zeros)

    lanes = width // 128
    token_specs = [by_step(1, group_rows, width), by_step(1, group_rows, width), by_step(per_group, 128)]
    forward_out = [
        by_step(rows, 2 * width),
        by_step(rows, 128),
        by_step(rows, width),
        by_step(per_group, PAD, 3 * width),
        by_step(per_group, lanes, PAD, 4 * PAD),
        by_step(rows, 128),
        pl.BlockSpec((1, rows), lambda i: (0, i)),
        whole(1, 128),
    ]
    forward_shape = [
        jax.ShapeDtypeStruct((padded, 2 * width), bf16),
        jax.ShapeDtypeStruct((padded, 128), f32),
        jax.ShapeDtypeStruct((padded, width), bf16),
        jax.ShapeDtypeStruct((windows, PAD, 3 * width), bf16),
        jax.ShapeDtypeStruct((windows, lanes, PAD, 4 * PAD), bf16),
        jax.ShapeDtypeStruct((padded, 128), jnp.int32),
        jax.ShapeDtypeStruct((1, padded), jnp.int32),
        jax.ShapeDtypeStruct((1, 128), jnp.int32),
    ]
    forward_scratch = [
        pltpu.VMEM((rows, width), f32),
        pltpu.VMEM((rows, width), f32),
        pltpu.VMEM((group_rows, width), f32),
        pltpu.VMEM((rows, 1), jnp.int32),
        pltpu.VMEM((per_group, 1, 4 * PAD), jnp.int32),
        pltpu.VMEM((1, 128), f32),
    ]
    body = functools.partial(forward_kernel, dims, experts, slots, per_group, fast)
    if fast:
        own = (qkv_weight, proj_weight, router_weight.T, norm_params.T, expert_in, expert_out)
        *forward, w_all, w_exp = pl.pallas_call(
            body,
            grid=(steps,),
            in_specs=token_specs + [whole(*v.shape) for v in own],
            out_specs=forward_out + [anywhere, anywhere],
            out_shape=forward_shape
            + [
                jax.ShapeDtypeStruct((2, 2 * depth, shard, 2 * width + 128), bf16),
                jax.ShapeDtypeStruct((experts, 2, 2 * depth, shard, hidden), bf16),
            ],
            scratch_shapes=forward_scratch
            + [
                pltpu.VMEM((2, 2 * depth, shard, 2 * width + 128), bf16),
                pltpu.VMEM((2, shard, 2 * width + 128), bf16),
                pltpu.VMEM((2, shard, hidden), bf16),
                pltpu.SemaphoreType.DMA((1,)),
            ]
            + SharedGather.semaphores(depth)
            + Gather.semaphores(depth),
            compiler_params=remote(0),
            name="attention_forward",
        )(x3, g3, combo, *own)
    else:
        pack = jnp.concatenate([router_weight, norm_params], axis=1)
        pack = jnp.pad(pack, ((0, 0), (0, 128 - pack.shape[1])))
        shared_shard = jnp.stack(
            [
                jnp.concatenate([qkv_weight[:, : 2 * width], pack], axis=1),
                jnp.concatenate([qkv_weight[:, 2 * width :], proj_weight, pack], axis=1),
            ]
        ).astype(bf16)
        expert_shard = jnp.stack([expert_in[0], expert_out[0]]).astype(bf16)
        w_all = lax.all_gather(shared_shard, "dp", axis=1, tiled=True)
        w_exp = lax.all_gather(lax.all_gather(expert_shard, "dp", axis=1, tiled=True), "expert", axis=0, tiled=False)
        forward = pl.pallas_call(
            body,
            grid=(steps,),
            in_specs=token_specs + [whole(*w_all.shape)],
            out_specs=forward_out,
            out_shape=forward_shape,
            scratch_shapes=forward_scratch,
            compiler_params=params,
            name="attention_forward",
        )(x3, g3, combo, w_all)
    hz, pr, attn, qkv, probs, key, key_row, counts = forward
    w_all = w_all.reshape(2, width, 2 * width + 128)
    w_exp = w_exp.reshape(experts, 2, width, hidden)

    grads, tok = pl.pallas_call(
        functools.partial(expert_kernel, slots),
        grid_spec=pltpu.PrefetchScalarGridSpec(
            num_scalar_prefetch=1,
            grid=(experts,),
            in_specs=[
                whole(padded, 2 * width),
                whole(1, padded),
                whole(padded, 128),
                pl.BlockSpec((1, 2, width, hidden), lambda e, *_: (e, 0, 0, 0)),
            ],
            out_specs=[
                pl.BlockSpec((1, 2, width, hidden), lambda e, *_: (e, 0, 0, 0)),
                whole(padded, 2 * width),
            ],
            scratch_shapes=[pltpu.VMEM((2, width, hidden), f32), pltpu.VMEM((padded, 2 * width), f32)],
        ),
        out_shape=[
            jax.ShapeDtypeStruct((experts, 2, width, hidden), bf16),
            jax.ShapeDtypeStruct((padded, 2 * width), bf16),
        ],
        compiler_params=params,
        name="experts",
    )(counts[0], hz, key_row, key, w_exp)

    staged = (
        w_all,
        x3,
        g3,
        tok.reshape(steps, rows, 2 * width),
        pr.reshape(steps, rows, 128),
        attn.reshape(steps, rows, width),
        qkv.reshape(steps, per_group, PAD, 3 * width),
        probs.reshape(steps, per_group, lanes, PAD, 4 * PAD),
    )
    backward_in = (combo, *staged)
    backward_specs = [by_step(per_group, 128)] + [anywhere] * len(staged)
    backward_out = [
        by_step(1, group_rows, width),
        by_step(1, group_rows, width),
        whole(4, width, width),
        whole(16, width),
    ]
    backward_shape = [
        jax.ShapeDtypeStruct((steps, group_rows, width), bf16),
        jax.ShapeDtypeStruct((steps, group_rows, width), f32),
        jax.ShapeDtypeStruct((4, width, width), bf16),
        jax.ShapeDtypeStruct((16, width), f32),
    ]
    backward_scratch = [
        pltpu.VMEM((rows, width), f32),
        pltpu.VMEM((rows, width), f32),
        pltpu.VMEM((group_rows, width), f32),
        pltpu.VMEM((rows, width), f32),
        pltpu.VMEM((rows, width), bf16),
        pltpu.VMEM((3, rows, width), bf16),
        pltpu.VMEM((4, width, width), f32),
        pltpu.VMEM((136, width), f32),
        *[pltpu.VMEM(v.shape, v.dtype) for v in staged],
        pltpu.SemaphoreType.DMA((8, steps)),
    ]
    weights_now = (qkv_weight, proj_weight, router_weight.T, norm_params.T, expert_in[0], expert_out[0])
    firsts_now = (qkv_first, proj_first, router_first.T, norm_first.T, in_first[0], out_first[0])
    seconds_now = (qkv_second, proj_second, router_second.T, norm_second.T, in_second[0], out_second[0])
    state = (*weights_now, *firsts_now, *seconds_now)
    body = functools.partial(backward_kernel, dims, experts, per_group, fast)
    if fast:
        finals = [
            jax.ShapeDtypeStruct((2, shard, hidden), f32),
            jax.ShapeDtypeStruct((4, shard, width), f32),
            jax.ShapeDtypeStruct((16, shard), f32),
            jax.ShapeDtypeStruct((8, 128), f32),
        ]
        out3, dx3, g_exp, shared, small, norms = pl.pallas_call(
            body,
            grid=(steps,),
            in_specs=backward_specs + [anywhere] * (1 + len(state)),
            out_specs=backward_out[:2] + [whole(*v.shape) for v in finals],
            out_shape=backward_shape[:2] + finals,
            scratch_shapes=backward_scratch
            + Scatter.scratch(depth, hidden, shard)
            + [pltpu.VMEM(v.shape, v.dtype) for v in state]
            + [
                pltpu.SemaphoreType.DMA((len(state),)),
                pltpu.VMEM((2, 2, depth, 2, shard, width), bf16),
                pltpu.VMEM((16, width), f32),
            ]
            + shared_scatter_scratch(depth, shard, width),
            compiler_params=remote(1),
            name="attention_backward",
        )(*backward_in, grads.reshape(experts, 2, depth, 2, shard, hidden), *state)
    else:
        out3, dx3, shared_grad, small_grad = pl.pallas_call(
            body,
            grid=(steps,),
            in_specs=backward_specs,
            out_specs=backward_out,
            out_shape=backward_shape,
            scratch_shapes=backward_scratch,
            compiler_params=params,
            name="attention_backward",
        )(*backward_in)
    block_output = out3.reshape(rows_here, width)
    input_grad = dx3.reshape(rows_here, width)

    if not fast:
        shared = lax.psum(shared_grad.astype(f32), ("expert", "dp"))
        small = lax.psum(small_grad, ("expert", "dp"))
        g_exp = lax.psum(grads.astype(f32), ("expert", "dp"))
        start = lax.axis_index("dp") * shard
        shared = lax.dynamic_slice_in_dim(shared, start, shard, axis=1)
        small = lax.dynamic_slice_in_dim(small, start, shard, axis=1)
        g_exp = lax.dynamic_index_in_dim(g_exp, lax.axis_index("expert"), 0, keepdims=False)
        g_exp = lax.dynamic_slice_in_dim(g_exp, start, shard, axis=1)
        reduced = (
            jnp.concatenate([shared[0], shared[1], shared[2]], axis=1),
            shared[3],
            small[0:experts],
            small[8:12],
            g_exp[0],
            g_exp[1],
        )
        steps_now = [lamb_parts(*entry)[2] for entry in zip(weights_now, reduced, firsts_now, seconds_now)]
        sums = jnp.stack([jnp.sum(v * v) for v in (*weights_now, *steps_now)])
        norms = jnp.broadcast_to(jnp.pad(lax.psum(sums, "dp"), (0, 128 - 12)), (8, 128))
    results = pl.pallas_call(
        functools.partial(update_kernel, experts),
        in_specs=[vmem] * (4 + len(state)),
        out_specs=[vmem] * (len(state) + 1),
        out_shape=[jax.ShapeDtypeStruct(v.shape, f32) for v in weights_now] * 3 + [jax.ShapeDtypeStruct((2, 6), f32)],
        compiler_params=pltpu.CompilerParams(vmem_limit_bytes=VMEM_BYTES),
        name="lamb_update",
    )(shared, small, g_exp, norms, *state)

    def restore(values):
        return (values[0], values[1], values[2].T, values[3].T, values[4][None], values[5][None])

    return (
        block_output,
        input_grad,
        *restore(results[0:6]),
        *restore(results[6:12]),
        *restore(results[12:18]),
        results[18].T[None],
    )


def solution(mesh):
    tok2 = P(("dp", "expert"), None)
    tok1 = P(("dp", "expert"))
    row = P("dp", None)
    exp = P("expert", "dp", None)
    shared4 = (row, row, row, row)
    placed = (tok2, tok2, tok2, tok1, tok1, *shared4, exp, exp, *shared4, *shared4, exp, exp, exp, exp)
    results = (tok2, tok2, *((*shared4, exp, exp) * 3), P("expert", None, None))
    dims = (mesh.shape["dp"], mesh.shape["expert"])
    return jax.shard_map(
        functools.partial(per_device, dims),
        mesh=mesh,
        in_specs=placed,
        out_specs=results,
        check_vma=False,
    )
```

```python
import functools

import jax
import jax.numpy as jnp
from jax import lax
from jax.experimental import pallas as pl
from jax.experimental.pallas import tpu as pltpu
from jax.sharding import PartitionSpec as P

HEADS = 12
HEAD_DIM = 32
WINDOW = 49
PAD = 64
STEP = 5
TILE = 256
GROUP = 4
NORM_EPS = 1e-05
MASKED = -1e30
BETA_ONE = 0.9
BETA_TWO = 0.999
ADAM_EPS = 1e-06
DECAY = 0.01
RATE = 0.3
VMEM_BYTES = 60 * 1024 * 1024

f32 = jnp.float32
bf16 = jnp.bfloat16


def dot_nn(a, b):
    return lax.dot_general(a, b, (((1,), (0,)), ((), ())), preferred_element_type=f32)


def dot_nt(a, b):
    return lax.dot_general(a, b, (((1,), (1,)), ((), ())), preferred_element_type=f32)


def dot_tn(a, b):
    return lax.dot_general(a, b, (((0,), (0,)), ((), ())), preferred_element_type=f32)


def norm_stats(v):
    width = v.shape[-1]
    mean = jnp.sum(v, axis=-1, keepdims=True) * (1.0 / width)
    centred = v - mean
    var = jnp.sum(centred * centred, axis=-1, keepdims=True) * (1.0 / width)
    rstd = lax.rsqrt(var + NORM_EPS)
    return centred * rstd, rstd


def norm_back(d, normed, rstd, gain):
    width = d.shape[-1]
    dn = d * gain
    m1 = jnp.sum(dn, axis=-1, keepdims=True) * (1.0 / width)
    m2 = jnp.sum(dn * normed, axis=-1, keepdims=True) * (1.0 / width)
    return rstd * (dn - m1 - normed * m2)


def head_masks():
    lane = lax.broadcasted_iota(jnp.int32, (PAD, 128), 1)
    return [lane // HEAD_DIM == h for h in range(4)]


def spread_heads(v, masks):
    zero = jnp.zeros_like(v)
    return jnp.concatenate([jnp.where(m, v, zero) for m in masks], axis=0)


def gather_heads(v, masks):
    out = jnp.where(masks[0], v[0:PAD], 0.0)
    for h in range(1, 4):
        out = jnp.where(masks[h], v[h * PAD : (h + 1) * PAD], out)
    return out


def weight_part(w_ref, part):
    width = (w_ref.shape[-1] - 128) // 2
    cols = slice((part % 2) * width, (part % 2 + 1) * width)
    if len(w_ref.shape) == 4:
        return w_ref[part // 2, :, :, cols].reshape(width, width)
    return w_ref[part // 2, :, cols]


def small_part(w_ref):
    width = (w_ref.shape[-1] - 128) // 2
    if len(w_ref.shape) == 4:
        return w_ref[0, :, :, 2 * width :].reshape(width, 128)
    return w_ref[0, :, 2 * width :]


def load_windows(src_ref, wide_ref, dst_ref, per_group):
    width = dst_ref.shape[-1]
    wide_ref[...] = src_ref[0].astype(f32)
    for k in range(per_group):
        dst_ref[k * PAD : k * PAD + WINDOW, :] = wide_ref[k * WINDOW : (k + 1) * WINDOW, :]
        dst_ref[k * PAD + WINDOW : (k + 1) * PAD, :] = jnp.zeros((PAD - WINDOW, width), f32)


def store_windows(src_ref, wide_ref, out_ref, per_group):
    for k in range(per_group):
        wide_ref[k * WINDOW : (k + 1) * WINDOW, :] = src_ref[k * PAD : k * PAD + WINDOW, :]
    out_ref[0] = wide_ref[...].astype(out_ref.dtype)


def token_columns(combo_ref, per_group):
    turned = jnp.transpose(combo_ref[...].astype(f32))
    return jnp.concatenate([turned[0:PAD, k : k + 1] for k in range(per_group)], axis=0).astype(jnp.int32)


def route_of(combo):
    return jnp.where(combo >= 512, combo & 15, -1)


def valid_of(combo):
    return ((combo >> 8) & 1).astype(f32)


def run_hooks(plan, step, index, w=None):
    for (k, i), jobs in plan.items():
        if i == index:
            due = step == k if w is None else (step == k) & (w == i)

            @pl.when(due)
            def _():
                for job in jobs:
                    job()


def forward_kernel(dims, experts, slots, per_group, fast, *refs):
    depth = dims[0] // 2
    plan = {}
    step = pl.program_id(0)
    if fast:
        x_ref, g_ref, *token_rows = refs[:5]
        qkv_w, proj_w, router_w, norm_w, in_w, out_w = refs[5:11]
        hz_ref, pr_ref, attn_ref, qkv_ref, p_ref, key_ref, keyrow_ref, count_ref, combo_ref, ws_out, we_ref = refs[11:22]
        combos, xp, gp, wide, codes, regions, carry, w_ref, sh, ex, ws_sem = refs[22:33]
        shared_sems, gather_sems = refs[33:40], refs[40:]
        gather = Gather(depth, ex, we_ref, gather_sems)
        shared = SharedGather(depth, sh, w_ref, shared_sems)

        def enter():
            meet(gather.z, gather.x, gather.y, gather.c, depth)
            width = qkv_w.shape[1] // 3
            shard = qkv_w.shape[0]
            small = jnp.concatenate([router_w[...], norm_w[...]], axis=0)
            small = jnp.concatenate([small, jnp.zeros((128 - small.shape[0], shard), f32)], axis=0)
            sh[0, :, 0 : 2 * width] = qkv_w[:, 0 : 2 * width].astype(bf16)
            sh[0, :, 2 * width :] = jnp.transpose(small).astype(bf16)
            sh[1, :, 0:width] = qkv_w[:, 2 * width :].astype(bf16)
            sh[1, :, width : 2 * width] = proj_w[...].astype(bf16)
            sh[1, :, 2 * width :] = jnp.zeros((shard, 128), bf16)
            shared.begin()
            ex[0] = in_w[0].astype(bf16)
            ex[1] = out_w[0].astype(bf16)
            gather.begin()

        def store_shared():
            pltpu.make_async_copy(w_ref, ws_out, ws_sem.at[0]).start()

        def leave():
            gather.finish()
            shared.finish()
            pltpu.make_async_copy(w_ref, ws_out, ws_sem.at[0]).wait()

        g = gather

        def first_weights():
            shared.along_z()
            gather.turns(0)
            shared.along_x()
            store_shared()
            gather.line(1)

        plan = {
            (0, "start"): [enter],
            (0, "norm"): [first_weights],
            (0, 7): [lambda: g.line(2)],
            (0, "end"): [lambda: g.turns(1)],
            (1, 3): [lambda: g.line(3)],
            (1, 7): [lambda: g.turns(2)],
            (2, "qkv"): [lambda: g.turns(3)],
            (2, "end"): [g.last, leave],
        }
    else:
        x_ref, g_ref, *token_rows = refs[:5]
        w_ref = refs[5]
        hz_ref, pr_ref, attn_ref, qkv_ref, p_ref, key_ref, keyrow_ref, count_ref, combo_ref = refs[6:15]
        combos, xp, gp, wide, codes, regions, carry = refs[15:22]
    rows = per_group * PAD
    width = x_ref.shape[-1]
    groups = width // 128
    run_hooks(plan, step, "start")
    load_windows(x_ref, wide, xp, per_group)
    load_windows(g_ref, wide, gp, per_group)

    @pl.when(step == 0)
    def _():
        carry[...] = jnp.zeros_like(carry)
        packed = (16 * token_rows[1][...] + 256 * token_rows[2][...] + 512).reshape(1, -1) + token_rows[0][...]
        combos[...] = jnp.zeros_like(combos)
        for k in range(combos.shape[0]):
            piece = packed[:, k * WINDOW : (k + 1) * WINDOW]
            combos[k : k + 1, 0:WINDOW] = piece
            combos[k : k + 1, PAD : PAD + WINDOW] = piece

    combo_ref[...] = combos[pl.ds(pl.multiple_of(step * per_group, per_group), per_group), :]
    combo = token_columns(combo_ref, per_group)
    valid = valid_of(combo)
    route = route_of(combo)
    codes[...] = jnp.where((combo >> 8) & 1 == 1, (combo >> 4) & 15, -1)
    flat = combo_ref[...]
    flat = jnp.where(flat >= 512, (flat >> 4) & 15, -3)
    for k in range(per_group):
        regions[k] = jnp.concatenate([flat[k : k + 1, :]] * 2, axis=1)

    normed, _ = norm_stats(xp[...])
    run_hooks(plan, step, "norm")
    small = small_part(w_ref)
    small_t = jnp.transpose(small.astype(f32))
    a1, b1, a2, b2 = (small_t[experts + i : experts + i + 1, :] for i in range(4))
    h1 = (normed * a1 + b1).astype(bf16)
    for part in range(3):
        raw = dot_nn(h1, weight_part(w_ref, part))
        if part == 0:
            raw = raw * (HEAD_DIM**-0.5)
        qkv_ref[:, :, part * width : (part + 1) * width] = raw.astype(bf16).reshape(per_group, PAD, width)
    run_hooks(plan, step, "qkv")

    masks = head_masks()
    key_i = lax.broadcasted_iota(jnp.int32, (PAD, 4 * PAD), 0)
    lane_i = lax.broadcasted_iota(jnp.int32, (PAD, 4 * PAD), 1)
    diagonal = key_i == lax.rem(lane_i, PAD)

    def window(w):
        at = pl.ds(pl.multiple_of(w * PAD, PAD), PAD)
        allowed = (codes[at, :] == regions[w]) | diagonal
        for lg in range(groups):
            q = qkv_ref[w, :, lg * 128 : (lg + 1) * 128]
            k = qkv_ref[w, :, width + lg * 128 : width + (lg + 1) * 128]
            v = qkv_ref[w, :, 2 * width + lg * 128 : 2 * width + (lg + 1) * 128]
            s = dot_nt(k, spread_heads(q, masks))
            s = jnp.where(allowed, s, MASKED)
            e = jnp.exp(s - jnp.max(s, axis=0, keepdims=True))
            p = (e * (1.0 / jnp.sum(e, axis=0, keepdims=True))).astype(bf16)
            p_ref[w, lg] = p
            o = dot_tn(p, v)
            attn_ref[at, lg * 128 : (lg + 1) * 128] = gather_heads(o, masks).astype(bf16)

    def windows(j, _):
        for k in range(GROUP):
            window(j * GROUP + k)
        for i in range(per_group):
            run_hooks(plan, step, i, j * GROUP + GROUP - 1)
        return 0

    lax.fori_loop(0, per_group // GROUP, windows, 0)

    y1 = xp[...] + dot_nn(attn_ref[...], weight_part(w_ref, 3))
    normed2, _ = norm_stats(y1)
    h2 = (normed2 * a2 + b2).astype(bf16)
    lane = lax.broadcasted_iota(jnp.int32, (rows, 128), 1)
    logits = jnp.where(lane < experts, dot_nn(h2, small), MASKED)
    e = jnp.exp(logits - jnp.max(logits, axis=-1, keepdims=True))
    pr = e * (1.0 / jnp.sum(e, axis=-1, keepdims=True))
    pr_ref[...] = pr
    chosen = lane == route
    gate = jnp.sum(jnp.where(chosen, pr, 0.0), axis=-1, keepdims=True)
    gv = gp[...] * valid
    hz_ref[:, 0:width] = h2
    hz_ref[:, width : 2 * width] = (gate * gv).astype(bf16)

    onehot = jnp.where(chosen, 1.0, 0.0)
    before = lax.broadcasted_iota(jnp.int32, (rows, rows), 1) < lax.broadcasted_iota(jnp.int32, (rows, rows), 0)
    ranks = dot_nn(jnp.where(before, 1.0, 0.0).astype(bf16), onehot.astype(bf16)) + carry[0:1, :]
    slot = jnp.sum(ranks * onehot, axis=-1, keepdims=True)
    seen = jnp.sum(onehot, axis=-1, keepdims=True)
    key = (route.astype(f32) * slots + slot) * seen + (seen - 1.0)
    key = jnp.broadcast_to(key, (rows, 128))
    key_ref[...] = key.astype(jnp.int32)
    keyrow_ref[...] = jnp.transpose(key)[0:1, :].astype(jnp.int32)
    carry[...] = carry[...] + jnp.sum(onehot, axis=0, keepdims=True)
    count_ref[...] = carry[...].astype(jnp.int32)
    run_hooks(plan, step, "end")


def expert_kernel(slots, counts_ref, hz_ref, keyrow_ref, keycol_ref, we_ref, grad_ref, tok_ref, acc, tok_acc):
    e = pl.program_id(0)
    width = hz_ref.shape[-1] // 2
    total = hz_ref.shape[0]

    @pl.when(e == 0)
    def _():
        tok_acc[...] = jnp.zeros_like(tok_acc)

    acc[...] = jnp.zeros_like(acc)
    used = counts_ref[e]

    def tile(offset, size):
        base = e * slots + offset
        pick = keyrow_ref[...] == base + lax.broadcasted_iota(jnp.int32, (size, total), 0)
        both = dot_nn(jnp.where(pick, 1.0, 0.0).astype(bf16), hz_ref[...]).astype(bf16)
        rows, dz = both[:, 0:width], both[:, width : 2 * width]
        up = dot_nn(rows, we_ref[0, 0])
        cdf = 0.5 * (1.0 + lax.erf(up * 2.0**-0.5))
        hidden = (up * cdf).astype(bf16)
        slope = cdf + up * (jnp.exp(-0.5 * up * up) * (2.0 * jnp.pi) ** -0.5)
        ret = dot_nt(hidden, we_ref[0, 1]).astype(bf16)
        dup = (dot_nn(dz, we_ref[0, 1]) * slope).astype(bf16)
        back = dot_nt(dup, we_ref[0, 0]).astype(bf16)
        acc[1] += dot_tn(dz, hidden)
        acc[0] += dot_tn(rows, dup)
        keys = jnp.concatenate([keycol_ref[...]] * (size // 128), axis=1)
        put = keys == base + lax.broadcasted_iota(jnp.int32, (total, size), 1)
        tok_acc[...] += dot_nn(jnp.where(put, 1.0, 0.0).astype(bf16), jnp.concatenate([ret, back], axis=1))

    def large(t, _):
        tile(t * TILE, TILE)
        return 0

    count = (used + TILE // 2 - 1) // TILE
    lax.fori_loop(0, count, large, 0)

    @pl.when(used > count * TILE)
    def _():
        tile(count * TILE, TILE // 2)

    grad_ref[0] = acc[...].astype(bf16)

    @pl.when(e == pl.num_programs(0) - 1)
    def _():
        tok_ref[...] = tok_acc[...].astype(bf16)


def backward_kernel(dims, experts, per_group, fast, *refs):
    depth = dims[0] // 2
    plan = {}
    step = pl.program_id(0)
    combo_ref, sources, refs = refs[0], refs[1:9], refs[9:]
    if fast:
        ge_ref, state_hbm = refs[0], refs[1:19]
        out_ref, dx_ref, gexp_ref = refs[19:22]
        results = refs[22:25]
        refs = refs[25:]
    else:
        out_ref, dx_ref, shared_ref, small_ref = refs[:4]
        refs = refs[4:]
    xp, gp, wide, outp, dattn, dqkv, acc, acc_s = refs[:8]
    buffers, in_sem = refs[8:16], refs[16]
    w_ref = buffers[0]
    x_all, g_all, tok_all, pr_all, attn_all, qkv_all, p_all = buffers[1:]

    def fetch(i, k):
        if i == 0:
            return pltpu.make_async_copy(sources[0], w_ref, in_sem.at[0, 0])
        return pltpu.make_async_copy(sources[i].at[k], buffers[i].at[k], in_sem.at[i, k])

    def fetch_all():
        fetch(0, 0).start()
        for k in range(x_all.shape[0]):
            for i in range(1, 8):
                fetch(i, k).start()

    if fast:
        sc = Scatter(depth, ge_ref, refs[17:22], refs[22:31])
        state, state_sem, shared_ref, small_ref = refs[31:49], refs[49], refs[50], refs[51]

        def load_state(i):
            return pltpu.make_async_copy(state_hbm[i], state[i], state_sem.at[i])

        def enter():
            meet_all(depth, sc.z, sc.x, sc.y, sc.c)
            sc.begin()
            fetch_all()
            sc.merge(0)

        def start_state():
            for i in range(18):
                load_state(i).start()

        def early():
            sc.second(depth - 1)
            sc.third(depth - 2)

        def middle():
            sc.third(depth - 1)

        def meanwhile():
            for s in range(2):
                gexp_ref[s] = sc.result(s)
            for i in range(18):
                load_state(i).wait()

        def leave():
            for part in range(4):
                shape = shared_ref.shape[2:]
                shared_ref[part // 2, part % 2] = acc[part].astype(bf16).reshape(shape)
            small_ref[0:8] = acc_s[0:8]
            small_ref[8:16] = acc_s[128:136]
            shared_scatter(
                depth, experts, early, middle, meanwhile, (shared_ref, small_ref, gexp_ref), state, results, refs[52:]
            )
            sc.finish()

        plan = {
            (0, "start"): [enter],
            (0, "pre"): [lambda: sc.merge(1)],
            (0, 7): [lambda: sc.second(0)],
            (1, "start"): [lambda: sc.merge(2)],
            (1, "pre"): [lambda: sc.second(1), start_state],
            (1, 3): [lambda: sc.merge(3), lambda: sc.third(0)],
            (1, "end"): [lambda: sc.second(2)],
            (2, "pre"): [lambda: sc.third(1)],
            (2, "end"): [leave],
        }
    else:
        plan = {(0, "start"): [fetch_all]}
    rows = per_group * PAD
    width = x_all.shape[-1]
    groups = width // 128
    scale = HEAD_DIM**-0.5

    @pl.when(step == 0)
    def _():
        acc[...] = jnp.zeros_like(acc)
        acc_s[...] = jnp.zeros_like(acc_s)

    run_hooks(plan, step, "start")

    @pl.when(step == 0)
    def _():
        fetch(0, 0).wait()

    for i in range(1, 8):
        fetch(i, step).wait()
    load_windows(x_all.at[pl.ds(step, 1)], wide, xp, per_group)
    load_windows(g_all.at[pl.ds(step, 1)], wide, gp, per_group)
    combo = token_columns(combo_ref, per_group)
    valid = valid_of(combo)
    route = route_of(combo)
    small = small_part(w_ref)
    small_t = jnp.transpose(small.astype(f32))
    a1, b1, a2, b2 = (small_t[experts + i : experts + i + 1, :] for i in range(4))
    y1 = xp[...] + dot_nn(attn_all[step], weight_part(w_ref, 3))
    gv = gp[...] * valid
    z = tok_all[step, :, 0:width].astype(f32)
    lane = lax.broadcasted_iota(jnp.int32, (rows, 128), 1)
    chosen = lane == route
    pr = pr_all[step]
    gate = jnp.sum(jnp.where(chosen, pr, 0.0), axis=-1, keepdims=True)
    outp[...] = y1 + gate * z
    store_windows(outp, wide, out_ref, per_group)
    dgate = jnp.sum(gv * z, axis=-1, keepdims=True)
    kept = jnp.where(lane < experts, jnp.where(chosen, 1.0, 0.0) - pr, 0.0)
    dlogits = (dgate * gate * kept).astype(bf16)
    n2, r2 = norm_stats(y1)
    h2 = (n2 * a2 + b2).astype(bf16)
    acc_s[0:128] += dot_tn(dlogits, h2)
    dh2 = dot_nt(dlogits, small) + tok_all[step, :, width : 2 * width].astype(f32)
    acc_s[130:131] += jnp.sum(dh2 * n2, axis=0, keepdims=True)
    acc_s[131:132] += jnp.sum(dh2, axis=0, keepdims=True)
    dy1 = gv + norm_back(dh2, n2, r2, a2)
    gp[...] = dy1
    da = dy1.astype(bf16)
    acc[3] += dot_tn(attn_all[step], da)
    dattn[...] = dot_nt(da, weight_part(w_ref, 3)).astype(bf16)
    run_hooks(plan, step, "pre")

    masks = head_masks()

    def window(w):
        at = pl.ds(pl.multiple_of(w * PAD, PAD), PAD)
        for lg in range(groups):
            cols = slice(lg * 128, (lg + 1) * 128)
            q = qkv_all[step, w, :, lg * 128 : (lg + 1) * 128]
            k = qkv_all[step, w, :, width + lg * 128 : width + (lg + 1) * 128]
            v = qkv_all[step, w, :, 2 * width + lg * 128 : 2 * width + (lg + 1) * 128]
            d_all = spread_heads(dattn[at, cols], masks)
            q_all = spread_heads(q, masks)
            p_low = p_all[step, w, lg]
            p = p_low.astype(f32)
            dp = dot_nt(v, d_all)
            ds = (p * (dp - jnp.sum(dp * p, axis=0, keepdims=True))).astype(bf16)
            dv = dot_nn(p_low, d_all)
            dk = dot_nn(ds, q_all)
            dq = gather_heads(dot_tn(ds, k), masks) * scale
            dqkv[0, at, cols] = dq.astype(bf16)
            dqkv[1, at, cols] = dk.astype(bf16)
            dqkv[2, at, cols] = dv.astype(bf16)

    def windows(j, _):
        for k in range(GROUP):
            window(j * GROUP + k)
        for i in range(per_group):
            run_hooks(plan, step, i, j * GROUP + GROUP - 1)
        return 0

    lax.fori_loop(0, per_group // GROUP, windows, 0)

    n1, r1 = norm_stats(xp[...])
    h1 = (n1 * a1 + b1).astype(bf16)
    dh1 = jnp.zeros((rows, width), f32)
    for part in range(3):
        dpart = dqkv[part]
        acc[part] += dot_tn(h1, dpart)
        dh1 = dh1 + dot_nt(dpart, weight_part(w_ref, part))
    acc_s[128:129] += jnp.sum(dh1 * n1, axis=0, keepdims=True)
    acc_s[129:130] += jnp.sum(dh1, axis=0, keepdims=True)
    outp[...] = gp[...] + norm_back(dh1, n1, r1, a1)
    store_windows(outp, wide, dx_ref, per_group)

    if not fast:

        @pl.when(step == pl.num_programs(0) - 1)
        def _():
            for part in range(4):
                shared_ref[part] = acc[part].astype(bf16)
            small_ref[0:8] = acc_s[0:8]
            small_ref[8:16] = acc_s[128:136]

    run_hooks(plan, step, "end")


def place():
    dp, ex = lax.axis_index("dp"), lax.axis_index("expert")
    return lax.div(dp, 2), lax.rem(dp, 2), lax.div(ex, 2), lax.rem(ex, 2)


def at(z, x, y, c):
    return (z * 2 + x, y * 2 + c)


def push(src, dst, send_sem, recv_sem, device):
    copy = pltpu.make_async_remote_copy(
        src_ref=src,
        dst_ref=dst,
        send_sem=send_sem,
        recv_sem=recv_sem,
        device_id=device,
        device_id_type=pl.DeviceIdType.MESH,
    )
    return copy


def meet(z, x, y, c, depth):
    barrier = pltpu.get_barrier_semaphore()

    def greet(device):
        pl.semaphore_signal(barrier, inc=1, device_id=device, device_id_type=pl.DeviceIdType.MESH)

    greet(at(z, x, y, 1 - c))
    greet(at(z, 1 - x, y, c))
    greet(at(z, x, 1 - y, c))
    for other in range(depth):
        @pl.when(z != other)
        def _():
            greet(at(other, x, y, c))

    pl.semaphore_wait(barrier, 3 + depth - 1)


class Gather:
    def __init__(self, depth, ex_ref, we_ref, sems):
        self.depth = depth
        self.ex, self.we = ex_ref, we_ref
        (self.loc, self.zs, self.zr, self.xs, self.xr, self.ys, self.yr, self.cs, self.cr) = sems
        self.z, self.x, self.y, self.c = place()

    @staticmethod
    def semaphores(depth):
        dma = pltpu.SemaphoreType.DMA
        return [
            dma((1,)),
            dma((2, depth)),
            dma((depth,)),
            dma((3, depth)),
            dma((3, depth)),
            dma((3, depth)),
            dma((3, depth)),
            dma((7, depth)),
            dma((7, depth)),
        ]

    def local(self):
        return pltpu.make_async_copy(self.ex, self.pair(self.y, self.c, self.z, self.x), self.loc.at[0])

    def block(self, y, c, s, z, x):
        return self.we.at[y * 2 + c, s, z * 2 + x]

    def pair(self, y, c, z, x):
        return self.we.at[y * 2 + c, :, z * 2 + x]

    def z_copy(self, up, zo, first=False):
        mine = self.ex if first else self.pair(self.y, self.c, zo, self.x)
        target = self.z + 1 if up else self.z - 1
        return push(
            mine,
            self.pair(self.y, self.c, zo, self.x),
            self.zs.at[0 if up else 1, zo],
            self.zr.at[zo],
            at(target, self.x, self.y, self.c),
        )

    def x_copy(self, kind, zo, y, first=False):
        s = 0 if kind == 0 else 1
        dst = self.block(y, self.c, s, zo, self.x)
        src = self.ex.at[s] if first else dst
        return push(src, dst, self.xs.at[kind, zo], self.xr.at[kind, zo], at(self.z, 1 - self.x, self.y, self.c))

    def y_copy(self, kind, zo, x, first=False):
        s = 1 if kind == 0 else 0
        dst = self.block(self.y, self.c, s, zo, x)
        src = self.ex.at[s] if first else dst
        return push(src, dst, self.ys.at[kind, zo], self.yr.at[kind, zo], at(self.z, self.x, 1 - self.y, self.c))

    def c_copy(self, kind, zo, c, first=False):
        x, y = self.x, self.y
        if kind == 0:
            dst = self.pair(y, c, zo, x)
        elif kind == 1:
            dst = self.block(y, c, 0, zo, 1 - x)
        elif kind == 2:
            dst = self.block(1 - y, c, 1, zo, x)
        elif kind in (3, 4):
            dst = self.block(1 - y, c, 0, zo, x if kind == 3 else 1 - x)
        else:
            dst = self.block(y if kind == 5 else 1 - y, c, 1, zo, 1 - x)
        src = self.ex if first else dst
        return push(src, dst, self.cs.at[kind, zo], self.cr.at[kind, zo], at(self.z, x, y, 1 - self.c))

    def spread(self, zo, first=False):
        self.x_copy(0, zo, self.y, first).start()
        self.y_copy(0, zo, self.x, first).start()
        self.y_copy(1, zo, self.x, first).start()
        self.x_copy(1, zo, self.y, first).start()
        self.c_copy(0, zo, self.c, first).start()

    def begin(self):
        z = self.z
        self.local().start()

        @pl.when(z < self.depth - 1)
        def _():
            self.z_copy(True, z, True).start()

        @pl.when(z > 0)
        def _():
            self.z_copy(False, z, True).start()

        self.spread(z, True)

    def line(self, s):
        z = self.z

        @pl.when(z - s >= 0)
        def _():
            self.z_copy(True, z - s).wait_recv()

            @pl.when(z < self.depth - 1)
            def _():
                self.z_copy(True, z - s).start()

            self.spread(z - s)

        @pl.when(z + s < self.depth)
        def _():
            self.z_copy(True, z + s).wait_recv()

            @pl.when(z > 0)
            def _():
                self.z_copy(False, z + s).start()

            self.spread(z + s)

    def turn(self, zo):
        self.x_copy(0, zo, self.y).wait_recv()
        self.y_copy(2, zo, 1 - self.x).start()
        self.c_copy(1, zo, self.c).start()
        self.y_copy(0, zo, self.x).wait_recv()
        self.x_copy(2, zo, 1 - self.y).start()
        self.c_copy(2, zo, self.c).start()

    def turns(self, s):
        z = self.z
        if s == 0:
            self.turn(z)
            return

        @pl.when(z - s >= 0)
        def _():
            self.turn(z - s)

        @pl.when(z + s < self.depth)
        def _():
            self.turn(z + s)

    def last(self):
        for zo in range(self.depth):
            for kind, ck in ((1, 3), (2, 4)):
                self.y_copy(kind, zo, self.x).wait_recv()
                self.c_copy(ck, zo, self.c).start()
            for kind, ck in ((1, 5), (2, 6)):
                self.x_copy(kind, zo, self.y).wait_recv()
                self.c_copy(ck, zo, self.c).start()

    def finish(self):
        z = self.z
        for zo in range(self.depth):
            for kind in range(7):
                self.c_copy(kind, zo, 1 - self.c).wait_recv()
        self.local().wait()
        for zo in range(self.depth):
            @pl.when((z < self.depth - 1) & (zo <= z))
            def _():
                self.z_copy(True, zo).wait_send()

            @pl.when((z > 0) & (zo >= z))
            def _():
                self.z_copy(False, zo).wait_send()

            for kind in range(3):
                self.x_copy(kind, zo, self.y).wait_send()
                self.y_copy(kind, zo, self.x).wait_send()
            for kind in range(7):
                self.c_copy(kind, zo, self.c).wait_send()


class SharedGather:
    def __init__(self, depth, sh_ref, ws_ref, sems):
        self.depth, self.sh, self.ws = depth, sh_ref, ws_ref
        self.loc, self.zs, self.zr, self.xs, self.xr, self.cs, self.cr = sems
        self.z, self.x, self.y, self.c = place()

    @staticmethod
    def semaphores(depth):
        dma = pltpu.SemaphoreType.DMA
        return [dma((1,)), dma((depth,)), dma((depth,)), dma((depth,)), dma((depth,)), dma((2, depth)), dma((2, depth))]

    def slot(self, zo, xo):
        return self.ws.at[self.c, zo * 2 + xo]

    def local(self):
        return pltpu.make_async_copy(self.sh.at[self.c], self.slot(self.z, self.x), self.loc.at[0])

    def z_copy(self, target):
        return push(
            self.sh.at[self.c],
            self.slot(self.z, self.x),
            self.zs.at[target],
            self.zr.at[self.z],
            at(target, self.x, self.y, self.c),
        )

    def z_from(self, zo):
        dst = self.slot(zo, self.x)
        return push(dst, dst, self.zs.at[zo], self.zr.at[zo], at(zo, self.x, self.y, self.c))

    def x_copy(self, zo, first=False):
        dst = self.slot(zo, self.x)
        src = self.sh.at[self.c] if first else dst
        return push(src, dst, self.xs.at[zo], self.xr.at[zo], at(self.z, 1 - self.x, self.y, self.c))

    def c_copy(self, zo, xo, first=False):
        dst = self.slot(zo, xo)
        src = self.sh.at[self.c] if first else dst
        return push(src, dst, self.cs.at[xo, zo], self.cr.at[xo, zo], at(self.z, self.x, self.y, 1 - self.c))

    def others(self):
        return [lax.rem(self.z + j, self.depth) for j in range(1, self.depth)]

    def begin(self):
        self.local().start()
        for zo in self.others():
            self.z_copy(zo).start()
        self.x_copy(self.z, True).start()
        self.c_copy(self.z, self.x, True).start()

    def along_z(self):
        for zo in self.others():
            self.z_from(zo).wait_recv()
            self.x_copy(zo).start()
            self.c_copy(zo, self.x).start()

    def along_x(self):
        for j in range(self.depth):
            zo = lax.rem(self.z + j, self.depth)
            self.x_copy(zo).wait_recv()
            self.c_copy(zo, 1 - self.x).start()
        for zo in range(self.depth):
            for xo in range(2):
                self.c_copy(zo, xo).wait_recv()
        self.local().wait()

    def finish(self):
        for zo in self.others():
            self.z_copy(zo).wait_send()
        for zo in range(self.depth):
            self.x_copy(zo).wait_send()
            for xo in range(2):
                self.c_copy(zo, xo).wait_send()


class Scatter:
    def __init__(self, depth, ge_ref, bufs, sems):
        self.depth = depth
        self.ge = ge_ref
        self.t, self.rc, self.r1, self.r2, self.r3 = bufs
        (self.ls, self.cs, self.cr, self.s1, self.q1, self.s2, self.q2, self.s3, self.q3) = sems
        self.z, self.x, self.y, self.c = place()

    @staticmethod
    def scratch(depth, cols, shard):
        dma = pltpu.SemaphoreType.DMA
        bufs = [
            pltpu.VMEM((2, 2, depth, 2, shard, cols), bf16),
            pltpu.VMEM((2, 2, depth, 2, shard, cols), bf16),
            pltpu.VMEM((2, depth, 2, shard, cols), bf16),
            pltpu.VMEM((2, depth, shard, cols), bf16),
            pltpu.VMEM((2, depth, shard, cols), bf16),
        ]
        sems = [
            dma((2, 2, depth)),
            dma((2, 2, depth)),
            dma((2, 2, depth)),
            dma((2, depth, 2)),
            dma((2, depth, 2)),
            dma((2, depth)),
            dma((2, depth)),
            dma((2, depth)),
            dma((2, depth)),
        ]
        return bufs + sems

    def local(self, i, s, zo):
        y = self.y if i == 0 else 1 - self.y
        return pltpu.make_async_copy(self.ge.at[y * 2 + self.c, s, zo], self.t.at[i, s, zo], self.ls.at[i, s, zo])

    def core(self, i, s, zo):
        y = self.y if i == 0 else 1 - self.y
        return push(
            self.ge.at[y * 2 + 1 - self.c, s, zo],
            self.rc.at[i, s, zo],
            self.cs.at[i, s, zo],
            self.cr.at[i, s, zo],
            at(self.z, self.x, self.y, 1 - self.c),
        )

    def one(self, s, zo, k):
        if s == 0:
            src, device = self.t.at[1, 0, zo, k], at(self.z, self.x, 1 - self.y, self.c)
        else:
            src, device = self.t.at[k, 1, zo, 1 - self.x], at(self.z, 1 - self.x, self.y, self.c)
        return push(src, self.r1.at[s, zo, k], self.s1.at[s, zo, k], self.q1.at[s, zo, k], device)

    def two(self, s, zo):
        if s == 0:
            src, device = self.t.at[0, 0, zo, 1 - self.x], at(self.z, 1 - self.x, self.y, self.c)
        else:
            src, device = self.t.at[1, 1, zo, self.x], at(self.z, self.x, 1 - self.y, self.c)
        return push(src, self.r2.at[s, zo], self.s2.at[s, zo], self.q2.at[s, zo], device)

    def three(self, s, zo):
        return push(
            self.t.at[0, s, zo, self.x],
            self.r3.at[s, self.z],
            self.s3.at[s, zo],
            self.q3.at[s, self.z],
            at(zo, self.x, self.y, self.c),
        )

    def arrived(self, s, zo):
        return push(
            self.r3.at[s, zo], self.r3.at[s, zo], self.s3.at[s, zo], self.q3.at[s, zo], at(zo, self.x, self.y, self.c)
        )

    def begin(self):
        def body(j, _):
            zo = self.order(j)
            for i, s in ((1, 0), (0, 1), (1, 1), (0, 0)):
                self.core(i, s, zo).start()
                self.local(i, s, zo).start()
            return 0

        lax.fori_loop(0, self.depth, body, 0)

    def order(self, j):
        return lax.rem(self.z + j + 1, self.depth)

    def fold(self, ref, other):
        ref[...] = (ref[...].astype(f32) + other[...].astype(f32)).astype(bf16)

    def merge(self, j):
        zo = self.order(j)
        for i, s in ((1, 0), (0, 1), (1, 1), (0, 0)):
            self.core(i, s, zo).wait_recv()
            self.local(i, s, zo).wait()
            for xo in range(2):
                self.fold(self.t.at[i, s, zo, xo], self.rc.at[i, s, zo, xo])
            if (i, s) == (1, 0):
                self.one(0, zo, 0).start()
                self.one(0, zo, 1).start()
            if s == 1:
                self.one(1, zo, i).start()

    def second(self, j):
        zo = self.order(j)
        for k in range(2):
            self.one(0, zo, k).wait_recv()
            self.fold(self.t.at[0, 0, zo, k], self.r1.at[0, zo, k])
        self.two(0, zo).start()
        for k in range(2):
            self.one(1, zo, k).wait_recv()
            self.fold(self.t.at[k, 1, zo, self.x], self.r1.at[1, zo, k])
        self.two(1, zo).start()

    def third(self, j):
        zo = self.order(j)
        for s in range(2):
            self.two(s, zo).wait_recv()
            self.fold(self.t.at[0, s, zo, self.x], self.r2.at[s, zo])

            @pl.when(zo != self.z)
            def _():
                self.three(s, zo).start()

    def result(self, s):
        total = self.t[0, s, self.z, self.x].astype(f32)
        for j in range(1, self.depth):
            zo = lax.rem(self.z + j, self.depth)
            self.arrived(s, zo).wait_recv()
            total = total + self.r3[s, zo].astype(f32)
        return total

    def finish(self):
        def body(j, _):
            zo = self.order(j)
            for s in range(2):
                for i in range(2):
                    self.core(i, s, zo).wait_send()
                for k in range(2):
                    self.one(s, zo, k).wait_send()
                self.two(s, zo).wait_send()

                @pl.when(zo != self.z)
                def _():
                    self.three(s, zo).wait_send()

            return 0

        lax.fori_loop(0, self.depth, body, 0)


def lamb_parts(weight, grad, first, second):
    first_new = BETA_ONE * first + (1.0 - BETA_ONE) * grad
    second_new = BETA_TWO * second + (1.0 - BETA_TWO) * grad * grad
    first_hat = first_new / (1.0 - BETA_ONE**STEP)
    second_hat = second_new / (1.0 - BETA_TWO**STEP)
    direction = first_hat / (jnp.sqrt(second_hat) + ADAM_EPS) + DECAY * weight
    return first_new, second_new, direction


def row_norms(values, lane0):
    lane = lax.broadcasted_iota(jnp.int32, (1, 128), 1)
    out = jnp.zeros((1, 128), f32)
    for i, v in enumerate(values):
        out = out + jnp.where(lane == lane0 + i, jnp.sum(v * v), 0.0)
    return out


def peers(n, me):
    return [lax.rem(me + j, n) for j in range(1, n)]


def meet_all(depth, z, x, y, c):
    barrier = pltpu.get_barrier_semaphore()
    dp, ex = z * 2 + x, y * 2 + c
    n_dp, n_ex = 2 * depth, 4
    for other in peers(n_dp, dp):
        pl.semaphore_signal(barrier, inc=1, device_id=(other, ex), device_id_type=pl.DeviceIdType.MESH)
    for other in peers(n_ex, ex):
        pl.semaphore_signal(barrier, inc=1, device_id=(dp, other), device_id_type=pl.DeviceIdType.MESH)
    pl.semaphore_wait(barrier, n_dp + n_ex - 2)


def shared_scatter(depth, experts, early, middle, meanwhile, operands, state, outputs, scratch):
    gs_ref, sm_ref, ge_ref = operands
    weights, firsts, seconds = state[0:6], state[6:12], state[12:18]
    fs_out, gsm_ref, norm_ref = outputs
    (t, rc, r1, r2, r3, src_c, src_y, src_x, sz, cur, wide, nb, nq, fs_ref) = scratch[:14]
    (ccs, ccr, s1, q1, s2, q2, s3, q3, s4, q4, ms, mr, zs, zr, ns, nr, es, er) = scratch[14:]
    z, x, y, c = place()
    dp, ex = z * 2 + x, y * 2 + c
    n_dp, n_ex = 2 * depth, 4
    shard = fs_ref.shape[1]
    width = fs_ref.shape[2]

    near = [at(z, x, y, 1 - c), at(z, x, 1 - y, c), at(z, 1 - x, y, c)]
    y_of = [y, 1 - y]

    def core(i):
        return push(gs_ref.at[y_of[i], 1 - c], rc.at[i], ccs.at[i], ccr.at[i], near[0])

    order = [lax.rem(z + 1 + j, depth) for j in range(depth)]

    def one(j, k):
        zo = order[j]
        if j % 2 == 0:
            return push(t.at[1, zo, k], r1.at[zo, k], s1.at[zo, k], q1.at[zo, k], near[1])
        return push(t.at[k, zo, 1 - x], r1.at[zo, k], s1.at[zo, k], q1.at[zo, k], near[2])

    def two(j):
        zo = order[j]
        if j % 2 == 0:
            return push(t.at[0, zo, 1 - x], r2.at[zo], s2.at[zo], q2.at[zo], near[2])
        return push(t.at[1, zo, x], r2.at[zo], s2.at[zo], q2.at[zo], near[1])

    def three(zo):
        return push(t.at[0, zo, x], r3.at[z], s3.at[zo], q3.at[z], at(zo, x, y, c))

    def arrived(zo):
        return push(r3.at[zo], r3.at[zo], s3.at[zo], q3.at[zo], at(zo, x, y, c))

    def small_hop(k):
        src = sm_ref if k == 0 else cur.at[k - 1]
        return push(src, (src_c, src_y, src_x)[k], ms.at[k], mr.at[k], near[k])

    def small_z(zo):
        return push(cur.at[2], sz.at[z], zs.at[zo], zr.at[z], at(zo, x, y, c))

    def small_from(zo):
        return push(sz.at[zo], sz.at[zo], zs.at[zo], zr.at[zo], at(zo, x, y, c))

    def fold(ref, a, b):
        ref[...] = (a[...].astype(f32) + b[...].astype(f32)).astype(bf16)

    small_hop(0).start()
    core(1).start()
    core(0).start()
    early()
    small_hop(0).wait_recv()
    cur[0] = sm_ref[...] + src_c[...]
    small_hop(1).start()
    for i in (1, 0):
        core(i).wait_recv()
        for j, zo in enumerate(order):
            for k in range(2):
                fold(t.at[i, zo, k], gs_ref.at[y_of[i], c, zo, k], rc.at[i, zo, k])
            if j % 2 == 0:
                if i == 1:
                    one(j, 0).start()
                    one(j, 1).start()
            else:
                one(j, i).start()
    middle()
    small_hop(1).wait_recv()
    cur[1] = cur[0] + src_y[...]
    small_hop(2).start()
    for j, zo in enumerate(order):
        for k in range(2):
            one(j, k).wait_recv()
            target = t.at[0, zo, k] if j % 2 == 0 else t.at[k, zo, x]
            fold(target, target, r1.at[zo, k])
        two(j).start()
    small_hop(2).wait_recv()
    cur[2] = cur[1] + src_x[...]
    sz[z] = cur[2]
    for zo in range(depth):
        @pl.when(zo != z)
        def _():
            small_z(zo).start()

    for j, zo in enumerate(order):
        two(j).wait_recv()
        target = t.at[0, zo, x]
        fold(target, target, r2.at[zo])
        if j < depth - 1:
            three(zo).start()

    meanwhile()
    totals = row_norms([w[...] for w in weights], 0)
    for i in range(2):
        direction = lamb_parts(weights[4 + i][...], ge_ref[i], firsts[4 + i][...], seconds[4 + i][...])[2]
        totals = totals + row_norms([direction], 10 + i)
    total = t[0, z, x].astype(f32)
    for zo in peers(depth, z):
        arrived(zo).wait_recv()
        total = total + r3[zo].astype(f32)
    fs_ref[ex] = total

    def four(e):
        return push(fs_ref.at[ex], fs_ref.at[ex], s4.at[e], q4.at[ex], (dp, e))

    def four_from(e):
        return push(fs_ref.at[e], fs_ref.at[e], s4.at[e], q4.at[e], (dp, e))

    def quarter(e):
        return push(nq.at[ex], nq.at[ex], es.at[e], er.at[ex], (dp, e))

    def quarter_from(e):
        return push(nq.at[e], nq.at[e], es.at[e], er.at[e], (dp, e))

    def part_of(refs):
        out = refs[1][...]
        for p in range(3):
            out = jnp.where(ex == p, refs[0][:, p * width : (p + 1) * width], out)
        return out

    direction = lamb_parts(part_of(weights), total, part_of(firsts), part_of(seconds))[2]
    lane = lax.broadcasted_iota(jnp.int32, (8, 128), 1)
    nq[ex] = jnp.where(lane == jnp.where(ex == 3, 7, 6), jnp.sum(direction * direction), 0.0)
    for e in peers(n_ex, ex):
        quarter(e).start()
    for e in peers(n_ex, ex):
        four(e).start()
    for zo in peers(depth, z):
        small_from(zo).wait_recv()
    small = sz[0]
    for zo in range(1, depth):
        small = small + sz[zo]
    wide[...] = jnp.transpose(jnp.concatenate([small, jnp.zeros((128 - 16, small.shape[1]), f32)], axis=0))
    mine = jnp.transpose(wide[pl.ds(pl.multiple_of(dp * shard, 16), shard), :])[0:16]
    gsm_ref[...] = mine
    for i, g in ((2, mine[0:experts]), (3, mine[8:12])):
        direction = lamb_parts(weights[i][...], g, firsts[i][...], seconds[i][...])[2]
        totals = totals + row_norms([direction], 6 + i)
    for e in peers(n_ex, ex):
        quarter_from(e).wait_recv()
    combined = jnp.broadcast_to(totals, (8, 128))
    for e in range(n_ex):
        combined = combined + nq[e]
    nb[dp] = combined

    def norm_push(r):
        return push(nb.at[dp], nb.at[dp], ns.at[r], nr.at[dp], (r, ex))

    def norm_from(r):
        return push(nb.at[r], nb.at[r], ns.at[r], nr.at[r], (r, ex))

    for r in peers(n_dp, dp):
        norm_push(r).start()
    for e in peers(n_ex, ex):
        four_from(e).wait_recv()
    fs_out[...] = fs_ref[...]
    for r in peers(n_dp, dp):
        norm_from(r).wait_recv()
    summed = nb[0]
    for r in range(1, n_dp):
        summed = summed + nb[r]
    norm_ref[...] = summed
    for e in peers(n_ex, ex):
        quarter(e).wait_send()

    for r in peers(n_dp, dp):
        norm_push(r).wait_send()
    for e in peers(n_ex, ex):
        four(e).wait_send()
    for i in range(2):
        core(i).wait_send()
    for k in range(3):
        small_hop(k).wait_send()
    for j, zo in enumerate(order):
        for k in range(2):
            one(j, k).wait_send()
        two(j).wait_send()
        if j < depth - 1:
            three(zo).wait_send()
            small_z(zo).wait_send()


def shared_scatter_scratch(depth, shard, width):
    dma = pltpu.SemaphoreType.DMA
    return [
        pltpu.VMEM((2, depth, 2, shard, width), bf16),
        pltpu.VMEM((2, depth, 2, shard, width), bf16),
        pltpu.VMEM((depth, 2, shard, width), bf16),
        pltpu.VMEM((depth, shard, width), bf16),
        pltpu.VMEM((depth, shard, width), bf16),
        pltpu.VMEM((16, width), f32),
        pltpu.VMEM((16, width), f32),
        pltpu.VMEM((16, width), f32),
        pltpu.VMEM((depth, 16, width), f32),
        pltpu.VMEM((3, 16, width), f32),
        pltpu.VMEM((width, 128), f32),
        pltpu.VMEM((2 * depth, 8, 128), f32),
        pltpu.VMEM((4, 8, 128), f32),
        pltpu.VMEM((4, shard, width), f32),
        dma((2,)),
        dma((2,)),
        dma((depth, 2)),
        dma((depth, 2)),
        dma((depth,)),
        dma((depth,)),
        dma((depth,)),
        dma((depth,)),
        dma((4,)),
        dma((4,)),
        dma((3,)),
        dma((3,)),
        dma((depth,)),
        dma((depth,)),
        dma((2 * depth,)),
        dma((2 * depth,)),
        dma((4,)),
        dma((4,)),
    ]


def update_kernel(experts, *refs):
    (gsh_ref, gsm_ref, ge_ref, norm_ref), weights, firsts, seconds = refs[:4], refs[4:10], refs[10:16], refs[16:22]
    w_out, m_out, s_out = refs[22:28], refs[28:34], refs[34:40]
    trust_ref = refs[40]
    width = gsh_ref.shape[2]
    totals = norm_ref[0:1, :]
    lane = lax.broadcasted_iota(jnp.int32, (1, 128), 1)

    def pick(i):
        return jnp.sqrt(jnp.sum(jnp.where(lane == i, totals, 0.0), axis=-1, keepdims=True))

    row = lax.broadcasted_iota(jnp.int32, (2, 6), 1)
    col = lax.broadcasted_iota(jnp.int32, (2, 6), 0)
    trust = jnp.zeros((2, 6), f32)
    whole = slice(None)
    jobs = [(0, slice(p * width, (p + 1) * width), lambda p=p: gsh_ref[p]) for p in range(3)]
    jobs += [(1, whole, lambda: gsh_ref[3]), (2, whole, lambda: gsm_ref[0:experts]), (3, whole, lambda: gsm_ref[8:12])]
    jobs += [(4, whole, lambda: ge_ref[0]), (5, whole, lambda: ge_ref[1])]
    ratios = []
    for i in range(6):
        wn, un = pick(i), pick(6 + i)
        ratios.append(wn / (un + 1e-06))
        trust = jnp.where((row == i) & (col == 0), wn, jnp.where((row == i) & (col == 1), un, trust))
    trust_ref[...] = trust
    for i, cols, grad in jobs:
        weight = weights[i][:, cols]
        first, second, direction = lamb_parts(weight, grad(), firsts[i][:, cols], seconds[i][:, cols])
        w_out[i][:, cols] = weight - RATE * ratios[i] * direction
        m_out[i][:, cols] = first
        s_out[i][:, cols] = second


def per_device(
    dims,
    tokens,
    cotangent,
    routes,
    valid_mask,
    shift_region,
    qkv_weight,
    proj_weight,
    router_weight,
    norm_params,
    expert_in,
    expert_out,
    qkv_first,
    qkv_second,
    proj_first,
    proj_second,
    router_first,
    router_second,
    norm_first,
    norm_second,
    in_first,
    in_second,
    out_first,
    out_second,
):
    rows_here, width = tokens.shape
    experts = router_weight.shape[1]
    hidden = expert_in.shape[2]
    shard = qkv_weight.shape[0]
    capacity = 2 * rows_here // experts
    slots = -(-capacity // TILE) * TILE
    windows = rows_here // WINDOW
    per_group = 8
    steps = windows // per_group
    group_rows = per_group * WINDOW
    padded = windows * PAD

    fast = dims == (8, 4)
    depth = dims[0] // 2
    vmem = pl.BlockSpec(memory_space=pltpu.VMEM)
    anywhere = pl.BlockSpec(memory_space=pl.ANY)

    def remote(collective_id):
        return pltpu.CompilerParams(
            vmem_limit_bytes=VMEM_BYTES, collective_id=collective_id, has_side_effects=True
        )

    x3 = tokens.reshape(steps, group_rows, width)
    g3 = cotangent.reshape(steps, group_rows, width)
    token_rows = (routes.reshape(1, rows_here), shift_region, valid_mask)

    rows = per_group * PAD
    params = pltpu.CompilerParams(vmem_limit_bytes=VMEM_BYTES, dimension_semantics=("arbitrary",))

    def by_step(*shape):
        zeros = (0,) * (len(shape) - 1)
        return pl.BlockSpec(shape, lambda i: (i,) + zeros)

    def whole(*shape):
        zeros = (0,) * len(shape)
        return pl.BlockSpec(shape, lambda i, *_: zeros)

    lanes = width // 128
    token_specs = [by_step(1, group_rows, width), by_step(1, group_rows, width)] + [whole(1, rows_here), whole(rows_here), whole(rows_here)]
    forward_out = [
        by_step(rows, 2 * width),
        by_step(rows, 128),
        by_step(rows, width),
        by_step(per_group, PAD, 3 * width),
        by_step(per_group, lanes, PAD, 4 * PAD),
        by_step(rows, 128),
        pl.BlockSpec((1, rows), lambda i: (0, i)),
        whole(1, 128),
        by_step(per_group, 128),
    ]
    forward_shape = [
        jax.ShapeDtypeStruct((padded, 2 * width), bf16),
        jax.ShapeDtypeStruct((padded, 128), f32),
        jax.ShapeDtypeStruct((padded, width), bf16),
        jax.ShapeDtypeStruct((windows, PAD, 3 * width), bf16),
        jax.ShapeDtypeStruct((windows, lanes, PAD, 4 * PAD), bf16),
        jax.ShapeDtypeStruct((padded, 128), jnp.int32),
        jax.ShapeDtypeStruct((1, padded), jnp.int32),
        jax.ShapeDtypeStruct((1, 128), jnp.int32),
        jax.ShapeDtypeStruct((windows, 128), jnp.int32),
    ]
    forward_scratch = [
        pltpu.VMEM((windows, 128), jnp.int32),
        pltpu.VMEM((rows, width), f32),
        pltpu.VMEM((rows, width), f32),
        pltpu.VMEM((group_rows, width), f32),
        pltpu.VMEM((rows, 1), jnp.int32),
        pltpu.VMEM((per_group, 1, 4 * PAD), jnp.int32),
        pltpu.VMEM((1, 128), f32),
    ]
    body = functools.partial(forward_kernel, dims, experts, slots, per_group, fast)
    if fast:
        own = (qkv_weight, proj_weight, router_weight.T, norm_params.T, expert_in, expert_out)
        *forward, w_all, w_exp = pl.pallas_call(
            body,
            grid=(steps,),
            in_specs=token_specs + [whole(*v.shape) for v in own],
            out_specs=forward_out + [anywhere, anywhere],
            out_shape=forward_shape
            + [
                jax.ShapeDtypeStruct((2, 2 * depth, shard, 2 * width + 128), bf16),
                jax.ShapeDtypeStruct((experts, 2, 2 * depth, shard, hidden), bf16),
            ],
            scratch_shapes=forward_scratch
            + [
                pltpu.VMEM((2, 2 * depth, shard, 2 * width + 128), bf16),
                pltpu.VMEM((2, shard, 2 * width + 128), bf16),
                pltpu.VMEM((2, shard, hidden), bf16),
                pltpu.SemaphoreType.DMA((1,)),
            ]
            + SharedGather.semaphores(depth)
            + Gather.semaphores(depth),
            compiler_params=remote(0),
            name="attention_forward",
        )(x3, g3, *token_rows, *own)
    else:
        pack = jnp.concatenate([router_weight, norm_params], axis=1)
        pack = jnp.pad(pack, ((0, 0), (0, 128 - pack.shape[1])))
        shared_shard = jnp.stack(
            [
                jnp.concatenate([qkv_weight[:, : 2 * width], pack], axis=1),
                jnp.concatenate([qkv_weight[:, 2 * width :], proj_weight, pack], axis=1),
            ]
        ).astype(bf16)
        expert_shard = jnp.stack([expert_in[0], expert_out[0]]).astype(bf16)
        w_all = lax.all_gather(shared_shard, "dp", axis=1, tiled=True)
        w_exp = lax.all_gather(lax.all_gather(expert_shard, "dp", axis=1, tiled=True), "expert", axis=0, tiled=False)
        forward = pl.pallas_call(
            body,
            grid=(steps,),
            in_specs=token_specs + [whole(*w_all.shape)],
            out_specs=forward_out,
            out_shape=forward_shape,
            scratch_shapes=forward_scratch,
            compiler_params=params,
            name="attention_forward",
        )(x3, g3, *token_rows, w_all)
    hz, pr, attn, qkv, probs, key, key_row, counts, combo = forward
    w_all = w_all.reshape(2, width, 2 * width + 128)
    w_exp = w_exp.reshape(experts, 2, width, hidden)

    grads, tok = pl.pallas_call(
        functools.partial(expert_kernel, slots),
        grid_spec=pltpu.PrefetchScalarGridSpec(
            num_scalar_prefetch=1,
            grid=(experts,),
            in_specs=[
                whole(padded, 2 * width),
                whole(1, padded),
                whole(padded, 128),
                pl.BlockSpec((1, 2, width, hidden), lambda e, *_: (e, 0, 0, 0)),
            ],
            out_specs=[
                pl.BlockSpec((1, 2, width, hidden), lambda e, *_: (e, 0, 0, 0)),
                whole(padded, 2 * width),
            ],
            scratch_shapes=[pltpu.VMEM((2, width, hidden), f32), pltpu.VMEM((padded, 2 * width), f32)],
        ),
        out_shape=[
            jax.ShapeDtypeStruct((experts, 2, width, hidden), bf16),
            jax.ShapeDtypeStruct((padded, 2 * width), bf16),
        ],
        compiler_params=params,
        name="experts",
    )(counts[0], hz, key_row, key, w_exp)

    staged = (
        w_all,
        x3,
        g3,
        tok.reshape(steps, rows, 2 * width),
        pr.reshape(steps, rows, 128),
        attn.reshape(steps, rows, width),
        qkv.reshape(steps, per_group, PAD, 3 * width),
        probs.reshape(steps, per_group, lanes, PAD, 4 * PAD),
    )
    backward_in = (combo, *staged)
    backward_specs = [by_step(per_group, 128)] + [anywhere] * len(staged)
    backward_out = [
        by_step(1, group_rows, width),
        by_step(1, group_rows, width),
        whole(4, width, width),
        whole(16, width),
    ]
    backward_shape = [
        jax.ShapeDtypeStruct((steps, group_rows, width), bf16),
        jax.ShapeDtypeStruct((steps, group_rows, width), f32),
        jax.ShapeDtypeStruct((4, width, width), bf16),
        jax.ShapeDtypeStruct((16, width), f32),
    ]
    backward_scratch = [
        pltpu.VMEM((rows, width), f32),
        pltpu.VMEM((rows, width), f32),
        pltpu.VMEM((group_rows, width), f32),
        pltpu.VMEM((rows, width), f32),
        pltpu.VMEM((rows, width), bf16),
        pltpu.VMEM((3, rows, width), bf16),
        pltpu.VMEM((4, width, width), f32),
        pltpu.VMEM((136, width), f32),
        *[pltpu.VMEM(v.shape, v.dtype) for v in staged],
        pltpu.SemaphoreType.DMA((8, steps)),
    ]
    weights_now = (qkv_weight, proj_weight, router_weight.T, norm_params.T, expert_in[0], expert_out[0])
    firsts_now = (qkv_first, proj_first, router_first.T, norm_first.T, in_first[0], out_first[0])
    seconds_now = (qkv_second, proj_second, router_second.T, norm_second.T, in_second[0], out_second[0])
    state = (*weights_now, *firsts_now, *seconds_now)
    body = functools.partial(backward_kernel, dims, experts, per_group, fast)
    if fast:
        finals = [
            jax.ShapeDtypeStruct((2, shard, hidden), f32),
            jax.ShapeDtypeStruct((4, shard, width), f32),
            jax.ShapeDtypeStruct((16, shard), f32),
            jax.ShapeDtypeStruct((8, 128), f32),
        ]
        out3, dx3, g_exp, shared, small, norms = pl.pallas_call(
            body,
            grid=(steps,),
            in_specs=backward_specs + [anywhere] * (1 + len(state)),
            out_specs=backward_out[:2] + [whole(*v.shape) for v in finals],
            out_shape=backward_shape[:2] + finals,
            scratch_shapes=backward_scratch
            + Scatter.scratch(depth, hidden, shard)
            + [pltpu.VMEM(v.shape, v.dtype) for v in state]
            + [
                pltpu.SemaphoreType.DMA((len(state),)),
                pltpu.VMEM((2, 2, depth, 2, shard, width), bf16),
                pltpu.VMEM((16, width), f32),
            ]
            + shared_scatter_scratch(depth, shard, width),
            compiler_params=remote(1),
            name="attention_backward",
        )(*backward_in, grads.reshape(experts, 2, depth, 2, shard, hidden), *state)
    else:
        out3, dx3, shared_grad, small_grad = pl.pallas_call(
            body,
            grid=(steps,),
            in_specs=backward_specs,
            out_specs=backward_out,
            out_shape=backward_shape,
            scratch_shapes=backward_scratch,
            compiler_params=params,
            name="attention_backward",
        )(*backward_in)
    block_output = out3.reshape(rows_here, width)
    input_grad = dx3.reshape(rows_here, width)

    if not fast:
        shared = lax.psum(shared_grad.astype(f32), ("expert", "dp"))
        small = lax.psum(small_grad, ("expert", "dp"))
        g_exp = lax.psum(grads.astype(f32), ("expert", "dp"))
        start = lax.axis_index("dp") * shard
        shared = lax.dynamic_slice_in_dim(shared, start, shard, axis=1)
        small = lax.dynamic_slice_in_dim(small, start, shard, axis=1)
        g_exp = lax.dynamic_index_in_dim(g_exp, lax.axis_index("expert"), 0, keepdims=False)
        g_exp = lax.dynamic_slice_in_dim(g_exp, start, shard, axis=1)
        reduced = (
            jnp.concatenate([shared[0], shared[1], shared[2]], axis=1),
            shared[3],
            small[0:experts],
            small[8:12],
            g_exp[0],
            g_exp[1],
        )
        steps_now = [lamb_parts(*entry)[2] for entry in zip(weights_now, reduced, firsts_now, seconds_now)]
        sums = jnp.stack([jnp.sum(v * v) for v in (*weights_now, *steps_now)])
        norms = jnp.broadcast_to(jnp.pad(lax.psum(sums, "dp"), (0, 128 - 12)), (8, 128))
    cuts, part = 1, shard

    def rows_of(v):
        if v.shape[-2] != shard:
            return whole(*v.shape)
        lead = v.shape[:-2]
        return pl.BlockSpec((*lead, part, v.shape[-1]), lambda i: (0,) * len(lead) + (i, 0))

    grads_now = (shared, small, g_exp, norms)
    results = pl.pallas_call(
        functools.partial(update_kernel, experts),
        grid=(cuts,),
        in_specs=[rows_of(v) for v in (*grads_now, *state)],
        out_specs=[rows_of(v) for v in weights_now] * 3 + [whole(2, 6)],
        out_shape=[jax.ShapeDtypeStruct(v.shape, f32) for v in weights_now] * 3
        + [jax.ShapeDtypeStruct((2, 6), f32)],
        compiler_params=params,
        name="lamb_update",
    )(*grads_now, *state)

    def restore(values):
        return (values[0], values[1], values[2].T, values[3].T, values[4][None], values[5][None])

    return (
        block_output,
        input_grad,
        *restore(results[0:6]),
        *restore(results[6:12]),
        *restore(results[12:18]),
        results[18].T[None],
    )


def solution(mesh):
    tok2 = P(("dp", "expert"), None)
    tok1 = P(("dp", "expert"))
    row = P("dp", None)
    exp = P("expert", "dp", None)
    shared4 = (row, row, row, row)
    placed = (tok2, tok2, tok2, tok1, tok1, *shared4, exp, exp, *shared4, *shared4, exp, exp, exp, exp)
    results = (tok2, tok2, *((*shared4, exp, exp) * 3), P("expert", None, None))
    dims = (mesh.shape["dp"], mesh.shape["expert"])
    return jax.shard_map(
        functools.partial(per_device, dims),
        mesh=mesh,
        in_specs=placed,
        out_specs=results,
        check_vma=False,
    )
```

```python
import functools

import jax
import jax.numpy as jnp
from jax import lax
from jax.experimental import pallas as pl
from jax.experimental.pallas import tpu as pltpu
from jax.sharding import PartitionSpec as P

HEADS = 12
HEAD_DIM = 32
WINDOW = 49
PAD = 64
STEP = 5
TILE = 256
GROUP = 4
NORM_EPS = 1e-05
MASKED = -1e30
BETA_ONE = 0.9
BETA_TWO = 0.999
ADAM_EPS = 1e-06
DECAY = 0.01
RATE = 0.3
VMEM_BYTES = 60 * 1024 * 1024

f32 = jnp.float32
bf16 = jnp.bfloat16


def dot_nn(a, b):
    return lax.dot_general(a, b, (((1,), (0,)), ((), ())), preferred_element_type=f32)


def dot_nt(a, b):
    return lax.dot_general(a, b, (((1,), (1,)), ((), ())), preferred_element_type=f32)


def dot_tn(a, b):
    return lax.dot_general(a, b, (((0,), (0,)), ((), ())), preferred_element_type=f32)


def norm_stats(v):
    width = v.shape[-1]
    mean = jnp.sum(v, axis=-1, keepdims=True) * (1.0 / width)
    centred = v - mean
    var = jnp.sum(centred * centred, axis=-1, keepdims=True) * (1.0 / width)
    rstd = lax.rsqrt(var + NORM_EPS)
    return centred * rstd, rstd


def norm_back(d, normed, rstd, gain):
    width = d.shape[-1]
    dn = d * gain
    m1 = jnp.sum(dn, axis=-1, keepdims=True) * (1.0 / width)
    m2 = jnp.sum(dn * normed, axis=-1, keepdims=True) * (1.0 / width)
    return rstd * (dn - m1 - normed * m2)


def head_masks():
    lane = lax.broadcasted_iota(jnp.int32, (PAD, 128), 1)
    return [lane // HEAD_DIM == h for h in range(4)]


def spread_heads(v, masks):
    zero = jnp.zeros_like(v)
    return jnp.concatenate([jnp.where(m, v, zero) for m in masks], axis=0)


def gather_heads(v, masks):
    out = jnp.where(masks[0], v[0:PAD], 0.0)
    for h in range(1, 4):
        out = jnp.where(masks[h], v[h * PAD : (h + 1) * PAD], out)
    return out


def weight_part(w_ref, part):
    width = (w_ref.shape[-1] - 128) // 2
    cols = slice((part % 2) * width, (part % 2 + 1) * width)
    if len(w_ref.shape) == 4:
        return w_ref[part // 2, :, :, cols].reshape(width, width)
    return w_ref[part // 2, :, cols]


def small_part(w_ref):
    width = (w_ref.shape[-1] - 128) // 2
    if len(w_ref.shape) == 4:
        return w_ref[0, :, :, 2 * width :].reshape(width, 128)
    return w_ref[0, :, 2 * width :]


def load_windows(src_ref, wide_ref, dst_ref, per_group):
    width = dst_ref.shape[-1]
    wide_ref[...] = src_ref[0].astype(f32)
    for k in range(per_group):
        dst_ref[k * PAD : k * PAD + WINDOW, :] = wide_ref[k * WINDOW : (k + 1) * WINDOW, :]
        dst_ref[k * PAD + WINDOW : (k + 1) * PAD, :] = jnp.zeros((PAD - WINDOW, width), f32)


def store_windows(src_ref, wide_ref, out_ref, per_group):
    for k in range(per_group):
        wide_ref[k * WINDOW : (k + 1) * WINDOW, :] = src_ref[k * PAD : k * PAD + WINDOW, :]
    out_ref[0] = wide_ref[...].astype(out_ref.dtype)


def token_columns(combo_ref, per_group):
    turned = jnp.transpose(combo_ref[...].astype(f32))
    return jnp.concatenate([turned[0:PAD, k : k + 1] for k in range(per_group)], axis=0).astype(jnp.int32)


def route_of(combo):
    return jnp.where(combo >= 512, combo & 15, -1)


def valid_of(combo):
    return ((combo >> 8) & 1).astype(f32)


def run_hooks(plan, step, index, w=None):
    for (k, i), jobs in plan.items():
        if i == index:
            due = step == k if w is None else (step == k) & (w == i)

            @pl.when(due)
            def _():
                for job in jobs:
                    job()


def forward_kernel(dims, experts, slots, per_group, fast, *refs):
    depth = dims[0] // 2
    plan = {}
    step = pl.program_id(0)
    if fast:
        x_ref, g_ref, *token_rows = refs[:5]
        qkv_w, proj_w, router_w, norm_w, in_w, out_w = refs[5:11]
        hz_ref, pr_ref, attn_ref, qkv_ref, p_ref, key_ref, keyrow_ref, count_ref, combo_ref, ws_out, we_ref = refs[11:22]
        combos, xp_all, gp_all, normed_all, xb, gb, in_sem, wide, codes, regions, carry, w_ref, sh, ex, ws_sem = refs[22:37]
        shared_sems, gather_sems = refs[37:44], refs[44:]
        gather = Gather(depth, ex, we_ref, gather_sems)
        shared = SharedGather(depth, sh, w_ref, shared_sems)

        def enter():
            meet(gather.z, gather.x, gather.y, gather.c, depth)
            width = qkv_w.shape[1] // 3
            shard = qkv_w.shape[0]
            small = jnp.concatenate([router_w[...], norm_w[...]], axis=0)
            small = jnp.concatenate([small, jnp.zeros((128 - small.shape[0], shard), f32)], axis=0)
            sh[0, :, 0 : 2 * width] = qkv_w[:, 0 : 2 * width].astype(bf16)
            sh[0, :, 2 * width :] = jnp.transpose(small).astype(bf16)
            sh[1, :, 0:width] = qkv_w[:, 2 * width :].astype(bf16)
            sh[1, :, width : 2 * width] = proj_w[...].astype(bf16)
            sh[1, :, 2 * width :] = jnp.zeros((shard, 128), bf16)
            shared.begin()
            ex[0] = in_w[0].astype(bf16)
            ex[1] = out_w[0].astype(bf16)
            gather.begin()

        def store_shared():
            pltpu.make_async_copy(w_ref, ws_out, ws_sem.at[0]).start()

        def leave():
            gather.finish()
            shared.finish()
            pltpu.make_async_copy(w_ref, ws_out, ws_sem.at[0]).wait()

        g = gather

        def from_z():
            shared.along_z()
            gather.turns(0)

        def first_weights():
            gather.line(1)
            shared.along_x()
            store_shared()

        plan = {
            (0, "start"): [enter],
            (0, "prepared"): [from_z],
            (0, "norm"): [first_weights],
            (0, 7): [lambda: g.line(2)],
            (0, "end"): [lambda: g.turns(1)],
            (1, 3): [lambda: g.line(3)],
            (1, 7): [lambda: g.turns(2)],
            (2, "qkv"): [lambda: g.turns(3)],
            (2, 7): [lambda: g.last(0, 2)],
            (2, "end"): [lambda: g.last(2, depth), leave],
        }
    else:
        x_ref, g_ref, *token_rows = refs[:5]
        w_ref = refs[5]
        hz_ref, pr_ref, attn_ref, qkv_ref, p_ref, key_ref, keyrow_ref, count_ref, combo_ref = refs[6:15]
        combos, xp_all, gp_all, normed_all, xb, gb, in_sem, wide, codes, regions, carry = refs[15:26]
    rows = per_group * PAD
    width = x_ref.shape[-1]
    groups = width // 128
    steps = xb.shape[0]
    run_hooks(plan, step, "start")

    def fetch(k):
        return (
            pltpu.make_async_copy(x_ref.at[k], xb.at[k], in_sem.at[0, k]),
            pltpu.make_async_copy(g_ref.at[k], gb.at[k], in_sem.at[1, k]),
        )

    @pl.when(step == 0)
    def _():
        for k in range(steps):
            for copy in fetch(k):
                copy.start()

        def prepare(k, _):
            for copy in fetch(k):
                copy.wait()
            load_windows(xb.at[pl.ds(k, 1)], wide, xp_all.at[k], per_group)
            load_windows(gb.at[pl.ds(k, 1)], wide, gp_all.at[k], per_group)
            normed_all[k] = norm_stats(xp_all[k])[0]
            return 0

        lax.fori_loop(0, steps, prepare, 0)

    run_hooks(plan, step, "prepared")

    @pl.when(step == 0)
    def _():
        carry[...] = jnp.zeros_like(carry)
        packed = (16 * token_rows[1][...] + 256 * token_rows[2][...] + 512).reshape(1, -1) + token_rows[0][...]
        combos[...] = jnp.zeros_like(combos)
        for k in range(combos.shape[0]):
            piece = packed[:, k * WINDOW : (k + 1) * WINDOW]
            combos[k : k + 1, 0:WINDOW] = piece
            combos[k : k + 1, PAD : PAD + WINDOW] = piece
        lane = lax.broadcasted_iota(jnp.int32, (rows, 128), 1)
        before = lax.broadcasted_iota(jnp.int32, (rows, rows), 1) < lax.broadcasted_iota(jnp.int32, (rows, rows), 0)
        before = jnp.where(before, 1.0, 0.0).astype(bf16)
        for k in range(steps):
            route = route_of(token_columns(combos.at[k * per_group : (k + 1) * per_group], per_group))
            onehot = jnp.where(lane == route, 1.0, 0.0)
            ranks = dot_nn(before, onehot.astype(bf16)) + carry[0:1, :]
            slot = jnp.sum(ranks * onehot, axis=-1, keepdims=True)
            seen = jnp.sum(onehot, axis=-1, keepdims=True)
            key = (route.astype(f32) * slots + slot) * seen + (seen - 1.0)
            key = jnp.broadcast_to(key, (rows, 128))
            key_ref[k * rows : (k + 1) * rows, :] = key.astype(jnp.int32)
            keyrow_ref[:, k * rows : (k + 1) * rows] = jnp.transpose(key)[0:1, :].astype(jnp.int32)
            carry[...] = carry[...] + jnp.sum(onehot, axis=0, keepdims=True)
        count_ref[...] = carry[...].astype(jnp.int32)

    combo_ref[...] = combos[pl.ds(pl.multiple_of(step * per_group, per_group), per_group), :]
    combo = token_columns(combo_ref, per_group)
    valid = valid_of(combo)
    route = route_of(combo)
    codes[...] = jnp.where((combo >> 8) & 1 == 1, (combo >> 4) & 15, -1)
    flat = combo_ref[...]
    flat = jnp.where(flat >= 512, (flat >> 4) & 15, -3)
    for k in range(per_group):
        regions[k] = jnp.concatenate([flat[k : k + 1, :]] * 2, axis=1)

    run_hooks(plan, step, "norm")
    normed = normed_all[step]
    small = small_part(w_ref)
    small_t = jnp.transpose(small.astype(f32))
    a1, b1, a2, b2 = (small_t[experts + i : experts + i + 1, :] for i in range(4))
    h1 = (normed * a1 + b1).astype(bf16)
    for part in range(3):
        raw = dot_nn(h1, weight_part(w_ref, part))
        if part == 0:
            raw = raw * (HEAD_DIM**-0.5)
        qkv_ref[:, :, part * width : (part + 1) * width] = raw.astype(bf16).reshape(per_group, PAD, width)
    run_hooks(plan, step, "qkv")

    masks = head_masks()
    key_i = lax.broadcasted_iota(jnp.int32, (PAD, 4 * PAD), 0)
    lane_i = lax.broadcasted_iota(jnp.int32, (PAD, 4 * PAD), 1)
    diagonal = key_i == lax.rem(lane_i, PAD)

    def window(w):
        at = pl.ds(pl.multiple_of(w * PAD, PAD), PAD)
        allowed = (codes[at, :] == regions[w]) | diagonal
        for lg in range(groups):
            q = qkv_ref[w, :, lg * 128 : (lg + 1) * 128]
            k = qkv_ref[w, :, width + lg * 128 : width + (lg + 1) * 128]
            v = qkv_ref[w, :, 2 * width + lg * 128 : 2 * width + (lg + 1) * 128]
            s = dot_nt(k, spread_heads(q, masks))
            s = jnp.where(allowed, s, MASKED)
            e = jnp.exp(s - jnp.max(s, axis=0, keepdims=True))
            p = (e * (1.0 / jnp.sum(e, axis=0, keepdims=True))).astype(bf16)
            p_ref[w, lg] = p
            o = dot_tn(p, v)
            attn_ref[at, lg * 128 : (lg + 1) * 128] = gather_heads(o, masks).astype(bf16)

    def windows(j, _):
        for k in range(GROUP):
            window(j * GROUP + k)
        for i in range(per_group):
            run_hooks(plan, step, i, j * GROUP + GROUP - 1)
        return 0

    lax.fori_loop(0, per_group // GROUP, windows, 0)

    y1 = xp_all[step] + dot_nn(attn_ref[...], weight_part(w_ref, 3))
    normed2, _ = norm_stats(y1)
    h2 = (normed2 * a2 + b2).astype(bf16)
    lane = lax.broadcasted_iota(jnp.int32, (rows, 128), 1)
    logits = jnp.where(lane < experts, dot_nn(h2, small), MASKED)
    e = jnp.exp(logits - jnp.max(logits, axis=-1, keepdims=True))
    pr = e * (1.0 / jnp.sum(e, axis=-1, keepdims=True))
    pr_ref[...] = pr
    chosen = lane == route
    gate = jnp.sum(jnp.where(chosen, pr, 0.0), axis=-1, keepdims=True)
    gv = gp_all[step] * valid
    hz_ref[:, 0:width] = h2
    hz_ref[:, width : 2 * width] = (gate * gv).astype(bf16)

    run_hooks(plan, step, "end")


def expert_kernel(slots, counts_ref, hz_ref, keyrow_ref, keycol_ref, we_ref, grad_ref, tok_ref, acc, tok_acc):
    e = pl.program_id(0)
    width = hz_ref.shape[-1] // 2
    total = hz_ref.shape[0]

    @pl.when(e == 0)
    def _():
        tok_acc[...] = jnp.zeros_like(tok_acc)

    acc[...] = jnp.zeros_like(acc)
    used = counts_ref[e]

    def tile(offset, size):
        base = e * slots + offset
        pick = keyrow_ref[...] == base + lax.broadcasted_iota(jnp.int32, (size, total), 0)
        both = dot_nn(jnp.where(pick, 1.0, 0.0).astype(bf16), hz_ref[...]).astype(bf16)
        rows, dz = both[:, 0:width], both[:, width : 2 * width]
        up = dot_nn(rows, we_ref[0, 0])
        cdf = 0.5 * (1.0 + lax.erf(up * 2.0**-0.5))
        hidden = (up * cdf).astype(bf16)
        slope = cdf + up * (jnp.exp(-0.5 * up * up) * (2.0 * jnp.pi) ** -0.5)
        ret = dot_nt(hidden, we_ref[0, 1]).astype(bf16)
        dup = (dot_nn(dz, we_ref[0, 1]) * slope).astype(bf16)
        back = dot_nt(dup, we_ref[0, 0]).astype(bf16)
        acc[1] += dot_tn(dz, hidden)
        acc[0] += dot_tn(rows, dup)
        keys = jnp.concatenate([keycol_ref[...]] * (size // 128), axis=1)
        put = keys == base + lax.broadcasted_iota(jnp.int32, (total, size), 1)
        tok_acc[...] += dot_nn(jnp.where(put, 1.0, 0.0).astype(bf16), jnp.concatenate([ret, back], axis=1))

    def large(t, _):
        tile(t * TILE, TILE)
        return 0

    count = (used + TILE // 2 - 1) // TILE
    lax.fori_loop(0, count, large, 0)

    @pl.when(used > count * TILE)
    def _():
        tile(count * TILE, TILE // 2)

    grad_ref[0] = acc[...].astype(bf16)

    @pl.when(e == pl.num_programs(0) - 1)
    def _():
        tok_ref[...] = tok_acc[...].astype(bf16)


def backward_kernel(dims, experts, per_group, fast, *refs):
    depth = dims[0] // 2
    plan = {}
    step = pl.program_id(0)
    combo_ref, sources, refs = refs[0], refs[1:9], refs[9:]
    if fast:
        ge_ref, state_hbm = refs[0], refs[1:19]
        out_ref, dx_ref, gexp_ref = refs[19:22]
        results = refs[22:25]
        refs = refs[25:]
    else:
        out_ref, dx_ref, shared_ref, small_ref = refs[:4]
        refs = refs[4:]
    xp, gp, wide, outp, dattn, dqkv, acc, acc_s = refs[:8]
    buffers, in_sem = refs[8:16], refs[16]
    w_ref = buffers[0]
    x_all, g_all, tok_all, pr_all, attn_all, qkv_all, p_all = buffers[1:]

    def fetch(i, k):
        if i == 0:
            return pltpu.make_async_copy(sources[0], w_ref, in_sem.at[0, 0])
        return pltpu.make_async_copy(sources[i].at[k], buffers[i].at[k], in_sem.at[i, k])

    def fetch_all():
        fetch(0, 0).start()
        for k in range(x_all.shape[0]):
            for i in range(1, 8):
                fetch(i, k).start()

    if fast:
        sc = Scatter(depth, ge_ref, refs[17:22], refs[22:31])
        state, state_sem, shared_ref, small_ref = refs[31:49], refs[49], refs[50], refs[51]

        def load_state(i):
            return pltpu.make_async_copy(state_hbm[i], state[i], state_sem.at[i])

        def enter():
            meet_all(depth, sc.z, sc.x, sc.y, sc.c)
            sc.begin()
            fetch_all()
            sc.merge(0)

        def start_state():
            for i in range(18):
                load_state(i).start()

        def early():
            sc.second(depth - 1)
            sc.third(depth - 2)

        def middle():
            sc.third(depth - 1)

        def meanwhile():
            for s in range(2):
                gexp_ref[s] = sc.result(s)
            for i in range(18):
                load_state(i).wait()

        def leave():
            for part in range(4):
                shape = shared_ref.shape[2:]
                shared_ref[part // 2, part % 2] = acc[part].astype(bf16).reshape(shape)
            small_ref[0:8] = acc_s[0:8]
            small_ref[8:16] = acc_s[128:136]
            shared_scatter(
                depth, experts, early, middle, meanwhile, (shared_ref, small_ref, gexp_ref), state, results, refs[52:]
            )
            sc.finish()

        plan = {
            (0, "start"): [enter],
            (0, "pre"): [lambda: sc.merge(1)],
            (0, 7): [lambda: sc.second(0)],
            (1, "start"): [lambda: sc.merge(2)],
            (1, "pre"): [lambda: sc.second(1), start_state],
            (1, 3): [lambda: sc.merge(3), lambda: sc.third(0)],
            (1, "end"): [lambda: sc.second(2)],
            (2, "pre"): [lambda: sc.third(1)],
            (2, "end"): [leave],
        }
    else:
        plan = {(0, "start"): [fetch_all]}
    rows = per_group * PAD
    width = x_all.shape[-1]
    groups = width // 128
    scale = HEAD_DIM**-0.5

    @pl.when(step == 0)
    def _():
        acc[...] = jnp.zeros_like(acc)
        acc_s[...] = jnp.zeros_like(acc_s)

    run_hooks(plan, step, "start")

    @pl.when(step == 0)
    def _():
        fetch(0, 0).wait()

    for i in range(1, 8):
        fetch(i, step).wait()
    load_windows(x_all.at[pl.ds(step, 1)], wide, xp, per_group)
    load_windows(g_all.at[pl.ds(step, 1)], wide, gp, per_group)
    combo = token_columns(combo_ref, per_group)
    valid = valid_of(combo)
    route = route_of(combo)
    small = small_part(w_ref)
    small_t = jnp.transpose(small.astype(f32))
    a1, b1, a2, b2 = (small_t[experts + i : experts + i + 1, :] for i in range(4))
    y1 = xp[...] + dot_nn(attn_all[step], weight_part(w_ref, 3))
    gv = gp[...] * valid
    z = tok_all[step, :, 0:width].astype(f32)
    lane = lax.broadcasted_iota(jnp.int32, (rows, 128), 1)
    chosen = lane == route
    pr = pr_all[step]
    gate = jnp.sum(jnp.where(chosen, pr, 0.0), axis=-1, keepdims=True)
    outp[...] = y1 + gate * z
    store_windows(outp, wide, out_ref, per_group)
    dgate = jnp.sum(gv * z, axis=-1, keepdims=True)
    kept = jnp.where(lane < experts, jnp.where(chosen, 1.0, 0.0) - pr, 0.0)
    dlogits = (dgate * gate * kept).astype(bf16)
    n2, r2 = norm_stats(y1)
    h2 = (n2 * a2 + b2).astype(bf16)
    acc_s[0:128] += dot_tn(dlogits, h2)
    dh2 = dot_nt(dlogits, small) + tok_all[step, :, width : 2 * width].astype(f32)
    acc_s[130:131] += jnp.sum(dh2 * n2, axis=0, keepdims=True)
    acc_s[131:132] += jnp.sum(dh2, axis=0, keepdims=True)
    dy1 = gv + norm_back(dh2, n2, r2, a2)
    gp[...] = dy1
    da = dy1.astype(bf16)
    acc[3] += dot_tn(attn_all[step], da)
    dattn[...] = dot_nt(da, weight_part(w_ref, 3)).astype(bf16)
    run_hooks(plan, step, "pre")

    masks = head_masks()

    def window(w):
        at = pl.ds(pl.multiple_of(w * PAD, PAD), PAD)
        for lg in range(groups):
            cols = slice(lg * 128, (lg + 1) * 128)
            q = qkv_all[step, w, :, lg * 128 : (lg + 1) * 128]
            k = qkv_all[step, w, :, width + lg * 128 : width + (lg + 1) * 128]
            v = qkv_all[step, w, :, 2 * width + lg * 128 : 2 * width + (lg + 1) * 128]
            d_all = spread_heads(dattn[at, cols], masks)
            q_all = spread_heads(q, masks)
            p_low = p_all[step, w, lg]
            p = p_low.astype(f32)
            dp = dot_nt(v, d_all)
            ds = (p * (dp - jnp.sum(dp * p, axis=0, keepdims=True))).astype(bf16)
            dv = dot_nn(p_low, d_all)
            dk = dot_nn(ds, q_all)
            dq = gather_heads(dot_tn(ds, k), masks) * scale
            dqkv[0, at, cols] = dq.astype(bf16)
            dqkv[1, at, cols] = dk.astype(bf16)
            dqkv[2, at, cols] = dv.astype(bf16)

    def windows(j, _):
        for k in range(GROUP):
            window(j * GROUP + k)
        for i in range(per_group):
            run_hooks(plan, step, i, j * GROUP + GROUP - 1)
        return 0

    lax.fori_loop(0, per_group // GROUP, windows, 0)

    n1, r1 = norm_stats(xp[...])
    h1 = (n1 * a1 + b1).astype(bf16)
    dh1 = jnp.zeros((rows, width), f32)
    for part in range(3):
        dpart = dqkv[part]
        acc[part] += dot_tn(h1, dpart)
        dh1 = dh1 + dot_nt(dpart, weight_part(w_ref, part))
    acc_s[128:129] += jnp.sum(dh1 * n1, axis=0, keepdims=True)
    acc_s[129:130] += jnp.sum(dh1, axis=0, keepdims=True)
    outp[...] = gp[...] + norm_back(dh1, n1, r1, a1)
    store_windows(outp, wide, dx_ref, per_group)

    if not fast:

        @pl.when(step == pl.num_programs(0) - 1)
        def _():
            for part in range(4):
                shared_ref[part] = acc[part].astype(bf16)
            small_ref[0:8] = acc_s[0:8]
            small_ref[8:16] = acc_s[128:136]

    run_hooks(plan, step, "end")


def place():
    dp, ex = lax.axis_index("dp"), lax.axis_index("expert")
    return lax.div(dp, 2), lax.rem(dp, 2), lax.div(ex, 2), lax.rem(ex, 2)


def at(z, x, y, c):
    return (z * 2 + x, y * 2 + c)


def push(src, dst, send_sem, recv_sem, device):
    copy = pltpu.make_async_remote_copy(
        src_ref=src,
        dst_ref=dst,
        send_sem=send_sem,
        recv_sem=recv_sem,
        device_id=device,
        device_id_type=pl.DeviceIdType.MESH,
    )
    return copy


def meet(z, x, y, c, depth):
    barrier = pltpu.get_barrier_semaphore()

    def greet(device):
        pl.semaphore_signal(barrier, inc=1, device_id=device, device_id_type=pl.DeviceIdType.MESH)

    greet(at(z, x, y, 1 - c))
    greet(at(z, 1 - x, y, c))
    greet(at(z, x, 1 - y, c))
    for other in range(depth):
        @pl.when(z != other)
        def _():
            greet(at(other, x, y, c))

    pl.semaphore_wait(barrier, 3 + depth - 1)


class Gather:
    def __init__(self, depth, ex_ref, we_ref, sems):
        self.depth = depth
        self.ex, self.we = ex_ref, we_ref
        (self.loc, self.zs, self.zr, self.xs, self.xr, self.ys, self.yr, self.cs, self.cr) = sems
        self.z, self.x, self.y, self.c = place()

    @staticmethod
    def semaphores(depth):
        dma = pltpu.SemaphoreType.DMA
        return [
            dma((1,)),
            dma((2, depth)),
            dma((depth,)),
            dma((3, depth)),
            dma((3, depth)),
            dma((3, depth)),
            dma((3, depth)),
            dma((7, depth)),
            dma((7, depth)),
        ]

    def local(self):
        return pltpu.make_async_copy(self.ex, self.pair(self.y, self.c, self.z, self.x), self.loc.at[0])

    def block(self, y, c, s, z, x):
        return self.we.at[y * 2 + c, s, z * 2 + x]

    def pair(self, y, c, z, x):
        return self.we.at[y * 2 + c, :, z * 2 + x]

    def z_copy(self, up, zo, first=False):
        mine = self.ex if first else self.pair(self.y, self.c, zo, self.x)
        target = self.z + 1 if up else self.z - 1
        return push(
            mine,
            self.pair(self.y, self.c, zo, self.x),
            self.zs.at[0 if up else 1, zo],
            self.zr.at[zo],
            at(target, self.x, self.y, self.c),
        )

    def x_copy(self, kind, zo, y, first=False):
        s = 0 if kind == 0 else 1
        dst = self.block(y, self.c, s, zo, self.x)
        src = self.ex.at[s] if first else dst
        return push(src, dst, self.xs.at[kind, zo], self.xr.at[kind, zo], at(self.z, 1 - self.x, self.y, self.c))

    def y_copy(self, kind, zo, x, first=False):
        s = 1 if kind == 0 else 0
        dst = self.block(self.y, self.c, s, zo, x)
        src = self.ex.at[s] if first else dst
        return push(src, dst, self.ys.at[kind, zo], self.yr.at[kind, zo], at(self.z, self.x, 1 - self.y, self.c))

    def c_copy(self, kind, zo, c, first=False):
        x, y = self.x, self.y
        if kind == 0:
            dst = self.pair(y, c, zo, x)
        elif kind == 1:
            dst = self.block(y, c, 0, zo, 1 - x)
        elif kind == 2:
            dst = self.block(1 - y, c, 1, zo, x)
        elif kind in (3, 4):
            dst = self.block(1 - y, c, 0, zo, x if kind == 3 else 1 - x)
        else:
            dst = self.block(y if kind == 5 else 1 - y, c, 1, zo, 1 - x)
        src = self.ex if first else dst
        return push(src, dst, self.cs.at[kind, zo], self.cr.at[kind, zo], at(self.z, x, y, 1 - self.c))

    def spread(self, zo, first=False):
        self.x_copy(0, zo, self.y, first).start()
        self.y_copy(0, zo, self.x, first).start()
        self.y_copy(1, zo, self.x, first).start()
        self.x_copy(1, zo, self.y, first).start()
        self.c_copy(0, zo, self.c, first).start()

    def begin(self):
        z = self.z
        self.local().start()

        @pl.when(z < self.depth - 1)
        def _():
            self.z_copy(True, z, True).start()

        @pl.when(z > 0)
        def _():
            self.z_copy(False, z, True).start()

        self.spread(z, True)

    def line(self, s):
        z = self.z

        @pl.when(z - s >= 0)
        def _():
            self.z_copy(True, z - s).wait_recv()

            @pl.when(z < self.depth - 1)
            def _():
                self.z_copy(True, z - s).start()

            self.spread(z - s)

        @pl.when(z + s < self.depth)
        def _():
            self.z_copy(True, z + s).wait_recv()

            @pl.when(z > 0)
            def _():
                self.z_copy(False, z + s).start()

            self.spread(z + s)

    def turn(self, zo):
        self.x_copy(0, zo, self.y).wait_recv()
        self.y_copy(2, zo, 1 - self.x).start()
        self.c_copy(1, zo, self.c).start()
        self.y_copy(0, zo, self.x).wait_recv()
        self.x_copy(2, zo, 1 - self.y).start()
        self.c_copy(2, zo, self.c).start()

    def turns(self, s):
        z = self.z
        if s == 0:
            self.turn(z)
            return

        @pl.when(z - s >= 0)
        def _():
            self.turn(z - s)

        @pl.when(z + s < self.depth)
        def _():
            self.turn(z + s)

    def last(self, first, end):
        turn = 1 - 2 * lax.div(self.z, self.depth // 2)
        for j in range(first, end):
            zo = lax.rem(self.z + j * turn + self.depth, self.depth)
            for kind, ck in ((1, 3), (2, 4)):
                self.y_copy(kind, zo, self.x).wait_recv()
                self.c_copy(ck, zo, self.c).start()
            for kind, ck in ((1, 5), (2, 6)):
                self.x_copy(kind, zo, self.y).wait_recv()
                self.c_copy(ck, zo, self.c).start()

    def finish(self):
        z = self.z
        for zo in range(self.depth):
            for kind in range(7):
                self.c_copy(kind, zo, 1 - self.c).wait_recv()
        self.local().wait()
        for zo in range(self.depth):
            @pl.when((z < self.depth - 1) & (zo <= z))
            def _():
                self.z_copy(True, zo).wait_send()

            @pl.when((z > 0) & (zo >= z))
            def _():
                self.z_copy(False, zo).wait_send()

            for kind in range(3):
                self.x_copy(kind, zo, self.y).wait_send()
                self.y_copy(kind, zo, self.x).wait_send()
            for kind in range(7):
                self.c_copy(kind, zo, self.c).wait_send()


class SharedGather:
    def __init__(self, depth, sh_ref, ws_ref, sems):
        self.depth, self.sh, self.ws = depth, sh_ref, ws_ref
        self.loc, self.zs, self.zr, self.xs, self.xr, self.cs, self.cr = sems
        self.z, self.x, self.y, self.c = place()

    @staticmethod
    def semaphores(depth):
        dma = pltpu.SemaphoreType.DMA
        return [dma((1,)), dma((depth,)), dma((depth,)), dma((depth,)), dma((depth,)), dma((2, depth)), dma((2, depth))]

    def slot(self, zo, xo):
        return self.ws.at[self.c, zo * 2 + xo]

    def local(self):
        return pltpu.make_async_copy(self.sh.at[self.c], self.slot(self.z, self.x), self.loc.at[0])

    def z_copy(self, target):
        return push(
            self.sh.at[self.c],
            self.slot(self.z, self.x),
            self.zs.at[target],
            self.zr.at[self.z],
            at(target, self.x, self.y, self.c),
        )

    def z_from(self, zo):
        dst = self.slot(zo, self.x)
        return push(dst, dst, self.zs.at[zo], self.zr.at[zo], at(zo, self.x, self.y, self.c))

    def x_copy(self, zo, first=False):
        dst = self.slot(zo, self.x)
        src = self.sh.at[self.c] if first else dst
        return push(src, dst, self.xs.at[zo], self.xr.at[zo], at(self.z, 1 - self.x, self.y, self.c))

    def c_copy(self, zo, xo, first=False):
        dst = self.slot(zo, xo)
        src = self.sh.at[self.c] if first else dst
        return push(src, dst, self.cs.at[xo, zo], self.cr.at[xo, zo], at(self.z, self.x, self.y, 1 - self.c))

    def others(self):
        return [lax.rem(self.z + j, self.depth) for j in range(1, self.depth)]

    def begin(self):
        self.local().start()
        for zo in self.others():
            self.z_copy(zo).start()
        self.x_copy(self.z, True).start()
        self.c_copy(self.z, self.x, True).start()

    def along_z(self):
        for zo in self.others():
            self.z_from(zo).wait_recv()
            self.x_copy(zo).start()
            self.c_copy(zo, self.x).start()

    def along_x(self):
        for j in range(self.depth):
            zo = lax.rem(self.z + j, self.depth)
            self.x_copy(zo).wait_recv()
            self.c_copy(zo, 1 - self.x).start()
        for zo in range(self.depth):
            for xo in range(2):
                self.c_copy(zo, xo).wait_recv()
        self.local().wait()

    def finish(self):
        for zo in self.others():
            self.z_copy(zo).wait_send()
        for zo in range(self.depth):
            self.x_copy(zo).wait_send()
            for xo in range(2):
                self.c_copy(zo, xo).wait_send()


class Scatter:
    def __init__(self, depth, ge_ref, bufs, sems):
        self.depth = depth
        self.ge = ge_ref
        self.t, self.rc, self.r1, self.r2, self.r3 = bufs
        (self.ls, self.cs, self.cr, self.s1, self.q1, self.s2, self.q2, self.s3, self.q3) = sems
        self.z, self.x, self.y, self.c = place()

    @staticmethod
    def scratch(depth, cols, shard):
        dma = pltpu.SemaphoreType.DMA
        bufs = [
            pltpu.VMEM((2, 2, depth, 2, shard, cols), bf16),
            pltpu.VMEM((2, 2, depth, 2, shard, cols), bf16),
            pltpu.VMEM((2, depth, 2, shard, cols), bf16),
            pltpu.VMEM((2, depth, shard, cols), bf16),
            pltpu.VMEM((2, depth, shard, cols), bf16),
        ]
        sems = [
            dma((2, 2, depth)),
            dma((2, 2, depth)),
            dma((2, 2, depth)),
            dma((2, depth, 2)),
            dma((2, depth, 2)),
            dma((2, depth)),
            dma((2, depth)),
            dma((2, depth)),
            dma((2, depth)),
        ]
        return bufs + sems

    def local(self, i, s, zo):
        y = self.y if i == 0 else 1 - self.y
        return pltpu.make_async_copy(self.ge.at[y * 2 + self.c, s, zo], self.t.at[i, s, zo], self.ls.at[i, s, zo])

    def core(self, i, s, zo):
        y = self.y if i == 0 else 1 - self.y
        return push(
            self.ge.at[y * 2 + 1 - self.c, s, zo],
            self.rc.at[i, s, zo],
            self.cs.at[i, s, zo],
            self.cr.at[i, s, zo],
            at(self.z, self.x, self.y, 1 - self.c),
        )

    def one(self, s, zo, k):
        if s == 0:
            src, device = self.t.at[1, 0, zo, k], at(self.z, self.x, 1 - self.y, self.c)
        else:
            src, device = self.t.at[k, 1, zo, 1 - self.x], at(self.z, 1 - self.x, self.y, self.c)
        return push(src, self.r1.at[s, zo, k], self.s1.at[s, zo, k], self.q1.at[s, zo, k], device)

    def two(self, s, zo):
        if s == 0:
            src, device = self.t.at[0, 0, zo, 1 - self.x], at(self.z, 1 - self.x, self.y, self.c)
        else:
            src, device = self.t.at[1, 1, zo, self.x], at(self.z, self.x, 1 - self.y, self.c)
        return push(src, self.r2.at[s, zo], self.s2.at[s, zo], self.q2.at[s, zo], device)

    def three(self, s, zo):
        return push(
            self.t.at[0, s, zo, self.x],
            self.r3.at[s, self.z],
            self.s3.at[s, zo],
            self.q3.at[s, self.z],
            at(zo, self.x, self.y, self.c),
        )

    def arrived(self, s, zo):
        return push(
            self.r3.at[s, zo], self.r3.at[s, zo], self.s3.at[s, zo], self.q3.at[s, zo], at(zo, self.x, self.y, self.c)
        )

    def begin(self):
        def body(j, _):
            zo = self.order(j)
            for i, s in ((1, 0), (0, 1), (1, 1), (0, 0)):
                self.core(i, s, zo).start()
                self.local(i, s, zo).start()
            return 0

        lax.fori_loop(0, self.depth, body, 0)

    def order(self, j):
        return lax.rem(self.z + j + 1, self.depth)

    def fold(self, ref, other):
        ref[...] = (ref[...].astype(f32) + other[...].astype(f32)).astype(bf16)

    def merge(self, j):
        zo = self.order(j)
        for i, s in ((1, 0), (0, 1), (1, 1), (0, 0)):
            self.core(i, s, zo).wait_recv()
            self.local(i, s, zo).wait()
            for xo in range(2):
                self.fold(self.t.at[i, s, zo, xo], self.rc.at[i, s, zo, xo])
            if (i, s) == (1, 0):
                self.one(0, zo, 0).start()
                self.one(0, zo, 1).start()
            if s == 1:
                self.one(1, zo, i).start()

    def second(self, j):
        zo = self.order(j)
        for k in range(2):
            self.one(0, zo, k).wait_recv()
            self.fold(self.t.at[0, 0, zo, k], self.r1.at[0, zo, k])
        self.two(0, zo).start()
        for k in range(2):
            self.one(1, zo, k).wait_recv()
            self.fold(self.t.at[k, 1, zo, self.x], self.r1.at[1, zo, k])
        self.two(1, zo).start()

    def third(self, j):
        zo = self.order(j)
        for s in range(2):
            self.two(s, zo).wait_recv()
            self.fold(self.t.at[0, s, zo, self.x], self.r2.at[s, zo])

            @pl.when(zo != self.z)
            def _():
                self.three(s, zo).start()

    def result(self, s):
        total = self.t[0, s, self.z, self.x].astype(f32)
        for j in range(1, self.depth):
            zo = lax.rem(self.z + j, self.depth)
            self.arrived(s, zo).wait_recv()
            total = total + self.r3[s, zo].astype(f32)
        return total

    def finish(self):
        def body(j, _):
            zo = self.order(j)
            for s in range(2):
                for i in range(2):
                    self.core(i, s, zo).wait_send()
                for k in range(2):
                    self.one(s, zo, k).wait_send()
                self.two(s, zo).wait_send()

                @pl.when(zo != self.z)
                def _():
                    self.three(s, zo).wait_send()

            return 0

        lax.fori_loop(0, self.depth, body, 0)


def lamb_parts(weight, grad, first, second):
    first_new = BETA_ONE * first + (1.0 - BETA_ONE) * grad
    second_new = BETA_TWO * second + (1.0 - BETA_TWO) * grad * grad
    first_hat = first_new / (1.0 - BETA_ONE**STEP)
    second_hat = second_new / (1.0 - BETA_TWO**STEP)
    direction = first_hat / (jnp.sqrt(second_hat) + ADAM_EPS) + DECAY * weight
    return first_new, second_new, direction


def row_norms(values, lane0):
    lane = lax.broadcasted_iota(jnp.int32, (1, 128), 1)
    out = jnp.zeros((1, 128), f32)
    for i, v in enumerate(values):
        out = out + jnp.where(lane == lane0 + i, jnp.sum(v * v), 0.0)
    return out


def peers(n, me):
    return [lax.rem(me + j, n) for j in range(1, n)]


def meet_all(depth, z, x, y, c):
    barrier = pltpu.get_barrier_semaphore()
    dp, ex = z * 2 + x, y * 2 + c
    n_dp, n_ex = 2 * depth, 4
    for other in peers(n_dp, dp):
        pl.semaphore_signal(barrier, inc=1, device_id=(other, ex), device_id_type=pl.DeviceIdType.MESH)
    for other in peers(n_ex, ex):
        pl.semaphore_signal(barrier, inc=1, device_id=(dp, other), device_id_type=pl.DeviceIdType.MESH)
    pl.semaphore_wait(barrier, n_dp + n_ex - 2)


def shared_scatter(depth, experts, early, middle, meanwhile, operands, state, outputs, scratch):
    gs_ref, sm_ref, ge_ref = operands
    weights, firsts, seconds = state[0:6], state[6:12], state[12:18]
    fs_out, gsm_ref, norm_ref = outputs
    (t, rc, r1, r2, r3, src_c, src_y, src_x, sz, cur, wide, nb, nq, fs_ref) = scratch[:14]
    (ccs, ccr, s1, q1, s2, q2, s3, q3, s4, q4, ms, mr, zs, zr, ns, nr, es, er) = scratch[14:]
    z, x, y, c = place()
    dp, ex = z * 2 + x, y * 2 + c
    n_dp, n_ex = 2 * depth, 4
    shard = fs_ref.shape[1]
    width = fs_ref.shape[2]

    near = [at(z, x, y, 1 - c), at(z, x, 1 - y, c), at(z, 1 - x, y, c)]
    y_of = [y, 1 - y]

    def core(i):
        return push(gs_ref.at[y_of[i], 1 - c], rc.at[i], ccs.at[i], ccr.at[i], near[0])

    order = [lax.rem(z + 1 + j, depth) for j in range(depth)]

    def one(j, k):
        zo = order[j]
        if j % 2 == 0:
            return push(t.at[1, zo, k], r1.at[zo, k], s1.at[zo, k], q1.at[zo, k], near[1])
        return push(t.at[k, zo, 1 - x], r1.at[zo, k], s1.at[zo, k], q1.at[zo, k], near[2])

    def two(j):
        zo = order[j]
        if j % 2 == 0:
            return push(t.at[0, zo, 1 - x], r2.at[zo], s2.at[zo], q2.at[zo], near[2])
        return push(t.at[1, zo, x], r2.at[zo], s2.at[zo], q2.at[zo], near[1])

    def three(zo):
        return push(t.at[0, zo, x], r3.at[z], s3.at[zo], q3.at[z], at(zo, x, y, c))

    def arrived(zo):
        return push(r3.at[zo], r3.at[zo], s3.at[zo], q3.at[zo], at(zo, x, y, c))

    def small_hop(k):
        src = sm_ref if k == 0 else cur.at[k - 1]
        return push(src, (src_c, src_y, src_x)[k], ms.at[k], mr.at[k], near[k])

    def small_z(zo):
        return push(cur.at[2], sz.at[z], zs.at[zo], zr.at[z], at(zo, x, y, c))

    def small_from(zo):
        return push(sz.at[zo], sz.at[zo], zs.at[zo], zr.at[zo], at(zo, x, y, c))

    def fold(ref, a, b):
        ref[...] = (a[...].astype(f32) + b[...].astype(f32)).astype(bf16)

    small_hop(0).start()
    core(1).start()
    core(0).start()
    early()
    small_hop(0).wait_recv()
    cur[0] = sm_ref[...] + src_c[...]
    small_hop(1).start()
    for i in (1, 0):
        core(i).wait_recv()
        for j, zo in enumerate(order):
            for k in range(2):
                fold(t.at[i, zo, k], gs_ref.at[y_of[i], c, zo, k], rc.at[i, zo, k])
            if j % 2 == 0:
                if i == 1:
                    one(j, 0).start()
                    one(j, 1).start()
            else:
                one(j, i).start()
    middle()
    small_hop(1).wait_recv()
    cur[1] = cur[0] + src_y[...]
    small_hop(2).start()
    for j, zo in enumerate(order):
        for k in range(2):
            one(j, k).wait_recv()
            target = t.at[0, zo, k] if j % 2 == 0 else t.at[k, zo, x]
            fold(target, target, r1.at[zo, k])
        two(j).start()
    small_hop(2).wait_recv()
    cur[2] = cur[1] + src_x[...]
    sz[z] = cur[2]
    for zo in range(depth):
        @pl.when(zo != z)
        def _():
            small_z(zo).start()

    for j, zo in enumerate(order):
        two(j).wait_recv()
        target = t.at[0, zo, x]
        fold(target, target, r2.at[zo])
        if j < depth - 1:
            three(zo).start()

    meanwhile()
    totals = row_norms([w[...] for w in weights], 0)
    for i in range(2):
        direction = lamb_parts(weights[4 + i][...], ge_ref[i], firsts[4 + i][...], seconds[4 + i][...])[2]
        totals = totals + row_norms([direction], 10 + i)
    total = t[0, z, x].astype(f32)
    for zo in peers(depth, z):
        arrived(zo).wait_recv()
        total = total + r3[zo].astype(f32)
    fs_ref[ex] = total

    def four(e):
        return push(fs_ref.at[ex], fs_ref.at[ex], s4.at[e], q4.at[ex], (dp, e))

    def four_from(e):
        return push(fs_ref.at[e], fs_ref.at[e], s4.at[e], q4.at[e], (dp, e))

    def quarter(e):
        return push(nq.at[ex], nq.at[ex], es.at[e], er.at[ex], (dp, e))

    def quarter_from(e):
        return push(nq.at[e], nq.at[e], es.at[e], er.at[e], (dp, e))

    def part_of(refs):
        out = refs[1][...]
        for p in range(3):
            out = jnp.where(ex == p, refs[0][:, p * width : (p + 1) * width], out)
        return out

    direction = lamb_parts(part_of(weights), total, part_of(firsts), part_of(seconds))[2]
    lane = lax.broadcasted_iota(jnp.int32, (8, 128), 1)
    nq[ex] = jnp.where(lane == jnp.where(ex == 3, 7, 6), jnp.sum(direction * direction), 0.0)
    for e in peers(n_ex, ex):
        quarter(e).start()
    for e in peers(n_ex, ex):
        four(e).start()
    for zo in peers(depth, z):
        small_from(zo).wait_recv()
    small = sz[0]
    for zo in range(1, depth):
        small = small + sz[zo]
    wide[...] = jnp.transpose(jnp.concatenate([small, jnp.zeros((128 - 16, small.shape[1]), f32)], axis=0))
    mine = jnp.transpose(wide[pl.ds(pl.multiple_of(dp * shard, 16), shard), :])[0:16]
    gsm_ref[...] = mine
    for i, g in ((2, mine[0:experts]), (3, mine[8:12])):
        direction = lamb_parts(weights[i][...], g, firsts[i][...], seconds[i][...])[2]
        totals = totals + row_norms([direction], 6 + i)
    for e in peers(n_ex, ex):
        quarter_from(e).wait_recv()
    combined = jnp.broadcast_to(totals, (8, 128))
    for e in range(n_ex):
        combined = combined + nq[e]
    nb[dp] = combined

    def norm_push(r):
        return push(nb.at[dp], nb.at[dp], ns.at[r], nr.at[dp], (r, ex))

    def norm_from(r):
        return push(nb.at[r], nb.at[r], ns.at[r], nr.at[r], (r, ex))

    for r in peers(n_dp, dp):
        norm_push(r).start()
    for e in peers(n_ex, ex):
        four_from(e).wait_recv()
    fs_out[...] = fs_ref[...]
    for r in peers(n_dp, dp):
        norm_from(r).wait_recv()
    summed = nb[0]
    for r in range(1, n_dp):
        summed = summed + nb[r]
    norm_ref[...] = summed
    for e in peers(n_ex, ex):
        quarter(e).wait_send()

    for r in peers(n_dp, dp):
        norm_push(r).wait_send()
    for e in peers(n_ex, ex):
        four(e).wait_send()
    for i in range(2):
        core(i).wait_send()
    for k in range(3):
        small_hop(k).wait_send()
    for j, zo in enumerate(order):
        for k in range(2):
            one(j, k).wait_send()
        two(j).wait_send()
        if j < depth - 1:
            three(zo).wait_send()
            small_z(zo).wait_send()


def shared_scatter_scratch(depth, shard, width):
    dma = pltpu.SemaphoreType.DMA
    return [
        pltpu.VMEM((2, depth, 2, shard, width), bf16),
        pltpu.VMEM((2, depth, 2, shard, width), bf16),
        pltpu.VMEM((depth, 2, shard, width), bf16),
        pltpu.VMEM((depth, shard, width), bf16),
        pltpu.VMEM((depth, shard, width), bf16),
        pltpu.VMEM((16, width), f32),
        pltpu.VMEM((16, width), f32),
        pltpu.VMEM((16, width), f32),
        pltpu.VMEM((depth, 16, width), f32),
        pltpu.VMEM((3, 16, width), f32),
        pltpu.VMEM((width, 128), f32),
        pltpu.VMEM((2 * depth, 8, 128), f32),
        pltpu.VMEM((4, 8, 128), f32),
        pltpu.VMEM((4, shard, width), f32),
        dma((2,)),
        dma((2,)),
        dma((depth, 2)),
        dma((depth, 2)),
        dma((depth,)),
        dma((depth,)),
        dma((depth,)),
        dma((depth,)),
        dma((4,)),
        dma((4,)),
        dma((3,)),
        dma((3,)),
        dma((depth,)),
        dma((depth,)),
        dma((2 * depth,)),
        dma((2 * depth,)),
        dma((4,)),
        dma((4,)),
    ]


def update_kernel(experts, *refs):
    (gsh_ref, gsm_ref, ge_ref, norm_ref), weights, firsts, seconds = refs[:4], refs[4:10], refs[10:16], refs[16:22]
    w_out, m_out, s_out = refs[22:28], refs[28:34], refs[34:40]
    trust_ref = refs[40]
    width = gsh_ref.shape[2]
    totals = norm_ref[0:1, :]
    lane = lax.broadcasted_iota(jnp.int32, (1, 128), 1)

    def pick(i):
        return jnp.sqrt(jnp.sum(jnp.where(lane == i, totals, 0.0), axis=-1, keepdims=True))

    row = lax.broadcasted_iota(jnp.int32, (2, 6), 1)
    col = lax.broadcasted_iota(jnp.int32, (2, 6), 0)
    trust = jnp.zeros((2, 6), f32)
    whole = slice(None)
    jobs = [(0, slice(p * width, (p + 1) * width), lambda p=p: gsh_ref[p]) for p in range(3)]
    jobs += [(1, whole, lambda: gsh_ref[3]), (2, whole, lambda: gsm_ref[0:experts]), (3, whole, lambda: gsm_ref[8:12])]
    jobs += [(4, whole, lambda: ge_ref[0]), (5, whole, lambda: ge_ref[1])]
    ratios = []
    for i in range(6):
        wn, un = pick(i), pick(6 + i)
        ratios.append(wn / (un + 1e-06))
        trust = jnp.where((row == i) & (col == 0), wn, jnp.where((row == i) & (col == 1), un, trust))
    trust_ref[...] = trust
    for i, cols, grad in jobs:
        weight = weights[i][:, cols]
        first, second, direction = lamb_parts(weight, grad(), firsts[i][:, cols], seconds[i][:, cols])
        w_out[i][:, cols] = weight - RATE * ratios[i] * direction
        m_out[i][:, cols] = first
        s_out[i][:, cols] = second


def per_device(
    dims,
    tokens,
    cotangent,
    routes,
    valid_mask,
    shift_region,
    qkv_weight,
    proj_weight,
    router_weight,
    norm_params,
    expert_in,
    expert_out,
    qkv_first,
    qkv_second,
    proj_first,
    proj_second,
    router_first,
    router_second,
    norm_first,
    norm_second,
    in_first,
    in_second,
    out_first,
    out_second,
):
    rows_here, width = tokens.shape
    experts = router_weight.shape[1]
    hidden = expert_in.shape[2]
    shard = qkv_weight.shape[0]
    capacity = 2 * rows_here // experts
    slots = -(-capacity // TILE) * TILE
    windows = rows_here // WINDOW
    per_group = 8
    steps = windows // per_group
    group_rows = per_group * WINDOW
    padded = windows * PAD

    fast = dims == (8, 4)
    depth = dims[0] // 2
    vmem = pl.BlockSpec(memory_space=pltpu.VMEM)
    anywhere = pl.BlockSpec(memory_space=pl.ANY)

    def remote(collective_id):
        return pltpu.CompilerParams(
            vmem_limit_bytes=VMEM_BYTES, collective_id=collective_id, has_side_effects=True
        )

    x3 = tokens.reshape(steps, group_rows, width)
    g3 = cotangent.reshape(steps, group_rows, width)
    token_rows = (routes.reshape(1, rows_here), shift_region, valid_mask)

    rows = per_group * PAD
    params = pltpu.CompilerParams(vmem_limit_bytes=VMEM_BYTES, dimension_semantics=("arbitrary",))

    def by_step(*shape):
        zeros = (0,) * (len(shape) - 1)
        return pl.BlockSpec(shape, lambda i: (i,) + zeros)

    def whole(*shape):
        zeros = (0,) * len(shape)
        return pl.BlockSpec(shape, lambda i, *_: zeros)

    lanes = width // 128
    token_specs = [anywhere] * 2 + [whole(1, rows_here), whole(rows_here), whole(rows_here)]
    forward_out = [
        by_step(rows, 2 * width),
        by_step(rows, 128),
        by_step(rows, width),
        by_step(per_group, PAD, 3 * width),
        by_step(per_group, lanes, PAD, 4 * PAD),
        whole(padded, 128),
        whole(1, padded),
        whole(1, 128),
        by_step(per_group, 128),
    ]
    forward_shape = [
        jax.ShapeDtypeStruct((padded, 2 * width), bf16),
        jax.ShapeDtypeStruct((padded, 128), f32),
        jax.ShapeDtypeStruct((padded, width), bf16),
        jax.ShapeDtypeStruct((windows, PAD, 3 * width), bf16),
        jax.ShapeDtypeStruct((windows, lanes, PAD, 4 * PAD), bf16),
        jax.ShapeDtypeStruct((padded, 128), jnp.int32),
        jax.ShapeDtypeStruct((1, padded), jnp.int32),
        jax.ShapeDtypeStruct((1, 128), jnp.int32),
        jax.ShapeDtypeStruct((windows, 128), jnp.int32),
    ]
    forward_scratch = [
        pltpu.VMEM((windows, 128), jnp.int32),
        pltpu.VMEM((steps, rows, width), f32),
        pltpu.VMEM((steps, rows, width), f32),
        pltpu.VMEM((steps, rows, width), f32),
        pltpu.VMEM(x3.shape, x3.dtype),
        pltpu.VMEM(g3.shape, g3.dtype),
        pltpu.SemaphoreType.DMA((2, steps)),
        pltpu.VMEM((group_rows, width), f32),
        pltpu.VMEM((rows, 1), jnp.int32),
        pltpu.VMEM((per_group, 1, 4 * PAD), jnp.int32),
        pltpu.VMEM((1, 128), f32),
    ]
    body = functools.partial(forward_kernel, dims, experts, slots, per_group, fast)
    if fast:
        own = (qkv_weight, proj_weight, router_weight.T, norm_params.T, expert_in, expert_out)
        *forward, w_all, w_exp = pl.pallas_call(
            body,
            grid=(steps,),
            in_specs=token_specs + [whole(*v.shape) for v in own],
            out_specs=forward_out + [anywhere, anywhere],
            out_shape=forward_shape
            + [
                jax.ShapeDtypeStruct((2, 2 * depth, shard, 2 * width + 128), bf16),
                jax.ShapeDtypeStruct((experts, 2, 2 * depth, shard, hidden), bf16),
            ],
            scratch_shapes=forward_scratch
            + [
                pltpu.VMEM((2, 2 * depth, shard, 2 * width + 128), bf16),
                pltpu.VMEM((2, shard, 2 * width + 128), bf16),
                pltpu.VMEM((2, shard, hidden), bf16),
                pltpu.SemaphoreType.DMA((1,)),
            ]
            + SharedGather.semaphores(depth)
            + Gather.semaphores(depth),
            compiler_params=remote(0),
            name="attention_forward",
        )(x3, g3, *token_rows, *own)
    else:
        pack = jnp.concatenate([router_weight, norm_params], axis=1)
        pack = jnp.pad(pack, ((0, 0), (0, 128 - pack.shape[1])))
        shared_shard = jnp.stack(
            [
                jnp.concatenate([qkv_weight[:, : 2 * width], pack], axis=1),
                jnp.concatenate([qkv_weight[:, 2 * width :], proj_weight, pack], axis=1),
            ]
        ).astype(bf16)
        expert_shard = jnp.stack([expert_in[0], expert_out[0]]).astype(bf16)
        w_all = lax.all_gather(shared_shard, "dp", axis=1, tiled=True)
        w_exp = lax.all_gather(lax.all_gather(expert_shard, "dp", axis=1, tiled=True), "expert", axis=0, tiled=False)
        forward = pl.pallas_call(
            body,
            grid=(steps,),
            in_specs=token_specs + [whole(*w_all.shape)],
            out_specs=forward_out,
            out_shape=forward_shape,
            scratch_shapes=forward_scratch,
            compiler_params=params,
            name="attention_forward",
        )(x3, g3, *token_rows, w_all)
    hz, pr, attn, qkv, probs, key, key_row, counts, combo = forward
    w_all = w_all.reshape(2, width, 2 * width + 128)
    w_exp = w_exp.reshape(experts, 2, width, hidden)

    grads, tok = pl.pallas_call(
        functools.partial(expert_kernel, slots),
        grid_spec=pltpu.PrefetchScalarGridSpec(
            num_scalar_prefetch=1,
            grid=(experts,),
            in_specs=[
                whole(padded, 2 * width),
                whole(1, padded),
                whole(padded, 128),
                pl.BlockSpec((1, 2, width, hidden), lambda e, *_: (e, 0, 0, 0)),
            ],
            out_specs=[
                pl.BlockSpec((1, 2, width, hidden), lambda e, *_: (e, 0, 0, 0)),
                whole(padded, 2 * width),
            ],
            scratch_shapes=[pltpu.VMEM((2, width, hidden), f32), pltpu.VMEM((padded, 2 * width), f32)],
        ),
        out_shape=[
            jax.ShapeDtypeStruct((experts, 2, width, hidden), bf16),
            jax.ShapeDtypeStruct((padded, 2 * width), bf16),
        ],
        compiler_params=params,
        name="experts",
    )(counts[0], hz, key_row, key, w_exp)

    staged = (
        w_all,
        x3,
        g3,
        tok.reshape(steps, rows, 2 * width),
        pr.reshape(steps, rows, 128),
        attn.reshape(steps, rows, width),
        qkv.reshape(steps, per_group, PAD, 3 * width),
        probs.reshape(steps, per_group, lanes, PAD, 4 * PAD),
    )
    backward_in = (combo, *staged)
    backward_specs = [by_step(per_group, 128)] + [anywhere] * len(staged)
    backward_out = [
        by_step(1, group_rows, width),
        by_step(1, group_rows, width),
        whole(4, width, width),
        whole(16, width),
    ]
    backward_shape = [
        jax.ShapeDtypeStruct((steps, group_rows, width), bf16),
        jax.ShapeDtypeStruct((steps, group_rows, width), f32),
        jax.ShapeDtypeStruct((4, width, width), bf16),
        jax.ShapeDtypeStruct((16, width), f32),
    ]
    backward_scratch = [
        pltpu.VMEM((rows, width), f32),
        pltpu.VMEM((rows, width), f32),
        pltpu.VMEM((group_rows, width), f32),
        pltpu.VMEM((rows, width), f32),
        pltpu.VMEM((rows, width), bf16),
        pltpu.VMEM((3, rows, width), bf16),
        pltpu.VMEM((4, width, width), f32),
        pltpu.VMEM((136, width), f32),
        *[pltpu.VMEM(v.shape, v.dtype) for v in staged],
        pltpu.SemaphoreType.DMA((8, steps)),
    ]
    weights_now = (qkv_weight, proj_weight, router_weight.T, norm_params.T, expert_in[0], expert_out[0])
    firsts_now = (qkv_first, proj_first, router_first.T, norm_first.T, in_first[0], out_first[0])
    seconds_now = (qkv_second, proj_second, router_second.T, norm_second.T, in_second[0], out_second[0])
    state = (*weights_now, *firsts_now, *seconds_now)
    body = functools.partial(backward_kernel, dims, experts, per_group, fast)
    if fast:
        finals = [
            jax.ShapeDtypeStruct((2, shard, hidden), f32),
            jax.ShapeDtypeStruct((4, shard, width), f32),
            jax.ShapeDtypeStruct((16, shard), f32),
            jax.ShapeDtypeStruct((8, 128), f32),
        ]
        out3, dx3, g_exp, shared, small, norms = pl.pallas_call(
            body,
            grid=(steps,),
            in_specs=backward_specs + [anywhere] * (1 + len(state)),
            out_specs=backward_out[:2] + [whole(*v.shape) for v in finals],
            out_shape=backward_shape[:2] + finals,
            scratch_shapes=backward_scratch
            + Scatter.scratch(depth, hidden, shard)
            + [pltpu.VMEM(v.shape, v.dtype) for v in state]
            + [
                pltpu.SemaphoreType.DMA((len(state),)),
                pltpu.VMEM((2, 2, depth, 2, shard, width), bf16),
                pltpu.VMEM((16, width), f32),
            ]
            + shared_scatter_scratch(depth, shard, width),
            compiler_params=remote(1),
            name="attention_backward",
        )(*backward_in, grads.reshape(experts, 2, depth, 2, shard, hidden), *state)
    else:
        out3, dx3, shared_grad, small_grad = pl.pallas_call(
            body,
            grid=(steps,),
            in_specs=backward_specs,
            out_specs=backward_out,
            out_shape=backward_shape,
            scratch_shapes=backward_scratch,
            compiler_params=params,
            name="attention_backward",
        )(*backward_in)
    block_output = out3.reshape(rows_here, width)
    input_grad = dx3.reshape(rows_here, width)

    if not fast:
        shared = lax.psum(shared_grad.astype(f32), ("expert", "dp"))
        small = lax.psum(small_grad, ("expert", "dp"))
        g_exp = lax.psum(grads.astype(f32), ("expert", "dp"))
        start = lax.axis_index("dp") * shard
        shared = lax.dynamic_slice_in_dim(shared, start, shard, axis=1)
        small = lax.dynamic_slice_in_dim(small, start, shard, axis=1)
        g_exp = lax.dynamic_index_in_dim(g_exp, lax.axis_index("expert"), 0, keepdims=False)
        g_exp = lax.dynamic_slice_in_dim(g_exp, start, shard, axis=1)
        reduced = (
            jnp.concatenate([shared[0], shared[1], shared[2]], axis=1),
            shared[3],
            small[0:experts],
            small[8:12],
            g_exp[0],
            g_exp[1],
        )
        steps_now = [lamb_parts(*entry)[2] for entry in zip(weights_now, reduced, firsts_now, seconds_now)]
        sums = jnp.stack([jnp.sum(v * v) for v in (*weights_now, *steps_now)])
        norms = jnp.broadcast_to(jnp.pad(lax.psum(sums, "dp"), (0, 128 - 12)), (8, 128))
    cuts, part = 1, shard

    def rows_of(v):
        if v.shape[-2] != shard:
            return whole(*v.shape)
        lead = v.shape[:-2]
        return pl.BlockSpec((*lead, part, v.shape[-1]), lambda i: (0,) * len(lead) + (i, 0))

    grads_now = (shared, small, g_exp, norms)
    results = pl.pallas_call(
        functools.partial(update_kernel, experts),
        grid=(cuts,),
        in_specs=[rows_of(v) for v in (*grads_now, *state)],
        out_specs=[rows_of(v) for v in weights_now] * 3 + [whole(2, 6)],
        out_shape=[jax.ShapeDtypeStruct(v.shape, f32) for v in weights_now] * 3
        + [jax.ShapeDtypeStruct((2, 6), f32)],
        compiler_params=params,
        name="lamb_update",
    )(*grads_now, *state)

    def restore(values):
        return (values[0], values[1], values[2].T, values[3].T, values[4][None], values[5][None])

    return (
        block_output,
        input_grad,
        *restore(results[0:6]),
        *restore(results[6:12]),
        *restore(results[12:18]),
        results[18].T[None],
    )


def solution(mesh):
    tok2 = P(("dp", "expert"), None)
    tok1 = P(("dp", "expert"))
    row = P("dp", None)
    exp = P("expert", "dp", None)
    shared4 = (row, row, row, row)
    placed = (tok2, tok2, tok2, tok1, tok1, *shared4, exp, exp, *shared4, *shared4, exp, exp, exp, exp)
    results = (tok2, tok2, *((*shared4, exp, exp) * 3), P("expert", None, None))
    dims = (mesh.shape["dp"], mesh.shape["expert"])
    return jax.shard_map(
        functools.partial(per_device, dims),
        mesh=mesh,
        in_specs=placed,
        out_specs=results,
        check_vma=False,
    )
```

```python
import functools

import jax
import jax.numpy as jnp
from jax import lax
from jax.experimental import pallas as pl
from jax.experimental.pallas import tpu as pltpu
from jax.sharding import PartitionSpec as P

HEADS = 12
HEAD_DIM = 32
WINDOW = 49
PAD = 64
STEP = 5
TILE = 256
GROUP = 4
NORM_EPS = 1e-05
MASKED = -1e30
BETA_ONE = 0.9
BETA_TWO = 0.999
ADAM_EPS = 1e-06
DECAY = 0.01
RATE = 0.3
VMEM_BYTES = 60 * 1024 * 1024

f32 = jnp.float32
bf16 = jnp.bfloat16


def dot_nn(a, b):
    return lax.dot_general(a, b, (((1,), (0,)), ((), ())), preferred_element_type=f32)


def dot_nt(a, b):
    return lax.dot_general(a, b, (((1,), (1,)), ((), ())), preferred_element_type=f32)


def dot_tn(a, b):
    return lax.dot_general(a, b, (((0,), (0,)), ((), ())), preferred_element_type=f32)


def norm_stats(v):
    width = v.shape[-1]
    mean = jnp.sum(v, axis=-1, keepdims=True) * (1.0 / width)
    centred = v - mean
    var = jnp.sum(centred * centred, axis=-1, keepdims=True) * (1.0 / width)
    rstd = lax.rsqrt(var + NORM_EPS)
    return centred * rstd, rstd


def norm_back(d, normed, rstd, gain):
    width = d.shape[-1]
    dn = d * gain
    m1 = jnp.sum(dn, axis=-1, keepdims=True) * (1.0 / width)
    m2 = jnp.sum(dn * normed, axis=-1, keepdims=True) * (1.0 / width)
    return rstd * (dn - m1 - normed * m2)


def head_masks():
    lane = lax.broadcasted_iota(jnp.int32, (PAD, 128), 1)
    return [lane // HEAD_DIM == h for h in range(4)]


def spread_heads(v, masks):
    zero = jnp.zeros_like(v)
    return jnp.concatenate([jnp.where(m, v, zero) for m in masks], axis=0)


def gather_heads(v, masks):
    out = jnp.where(masks[0], v[0:PAD], 0.0)
    for h in range(1, 4):
        out = jnp.where(masks[h], v[h * PAD : (h + 1) * PAD], out)
    return out


def weight_part(w_ref, part):
    width = (w_ref.shape[-1] - 128) // 2
    cols = slice((part % 2) * width, (part % 2 + 1) * width)
    if len(w_ref.shape) == 4:
        return w_ref[part // 2, :, :, cols].reshape(width, width)
    return w_ref[part // 2, :, cols]


def small_part(w_ref):
    width = (w_ref.shape[-1] - 128) // 2
    if len(w_ref.shape) == 4:
        return w_ref[0, :, :, 2 * width :].reshape(width, 128)
    return w_ref[0, :, 2 * width :]


def load_windows(src_ref, wide_ref, dst_ref, per_group):
    width = dst_ref.shape[-1]
    wide_ref[...] = src_ref[0].astype(f32)
    for k in range(per_group):
        dst_ref[k * PAD : k * PAD + WINDOW, :] = wide_ref[k * WINDOW : (k + 1) * WINDOW, :]
        dst_ref[k * PAD + WINDOW : (k + 1) * PAD, :] = jnp.zeros((PAD - WINDOW, width), f32)


def store_windows(src_ref, wide_ref, out_ref, per_group):
    for k in range(per_group):
        wide_ref[k * WINDOW : (k + 1) * WINDOW, :] = src_ref[k * PAD : k * PAD + WINDOW, :]
    out_ref[0] = wide_ref[...].astype(out_ref.dtype)


def token_columns(combo_ref, per_group):
    turned = jnp.transpose(combo_ref[...].astype(f32))
    return jnp.concatenate([turned[0:PAD, k : k + 1] for k in range(per_group)], axis=0).astype(jnp.int32)


def route_of(combo):
    return jnp.where(combo >= 512, combo & 15, -1)


def valid_of(combo):
    return ((combo >> 8) & 1).astype(f32)


def run_hooks(plan, step, index, w=None):
    for (k, i), jobs in plan.items():
        if i == index:
            due = step == k if w is None else (step == k) & (w == i)

            @pl.when(due)
            def _():
                for job in jobs:
                    job()


def forward_kernel(dims, experts, slots, per_group, fast, *refs):
    depth = dims[0] // 2
    plan = {}
    step = pl.program_id(0)
    if fast:
        x_ref, g_ref, *token_rows = refs[:5]
        qkv_w, proj_w, router_w, norm_w, in_w, out_w = refs[5:11]
        hz_ref, pr_ref, attn_ref, qkv_ref, p_ref, key_ref, keyrow_ref, count_ref, combo_ref, x_out, g_out, ws_out, we_ref = refs[11:24]
        combos, xp_all, gp_all, normed_all, xb, gb, in_sem, wide, codes, regions, carry, w_ref, sh, ex, ws_sem = refs[24:39]
        shared_sems, gather_sems = refs[39:46], refs[46:]
        gather = Gather(depth, ex, we_ref, gather_sems)
        shared = SharedGather(depth, sh, w_ref, shared_sems)

        def enter():
            meet(gather.z, gather.x, gather.y, gather.c, depth)
            width = qkv_w.shape[1] // 3
            shard = qkv_w.shape[0]
            small = jnp.concatenate([router_w[...], norm_w[...]], axis=0)
            small = jnp.concatenate([small, jnp.zeros((128 - small.shape[0], shard), f32)], axis=0)
            sh[0, :, 0 : 2 * width] = qkv_w[:, 0 : 2 * width].astype(bf16)
            sh[0, :, 2 * width :] = jnp.transpose(small).astype(bf16)
            sh[1, :, 0:width] = qkv_w[:, 2 * width :].astype(bf16)
            sh[1, :, width : 2 * width] = proj_w[...].astype(bf16)
            sh[1, :, 2 * width :] = jnp.zeros((shard, 128), bf16)
            shared.begin()
            ex[0] = in_w[0].astype(bf16)
            ex[1] = out_w[0].astype(bf16)
            gather.begin()

        def store_shared():
            pltpu.make_async_copy(w_ref, ws_out, ws_sem.at[0]).start()

        def leave():
            gather.finish()
            shared.finish()
            pltpu.make_async_copy(w_ref, ws_out, ws_sem.at[0]).wait()

        g = gather

        def from_z():
            shared.along_z()
            gather.turns(0)

        def first_weights():
            gather.line(1)
            shared.along_x()
            store_shared()

        plan = {
            (0, "start"): [enter],
            (0, "prepared"): [from_z],
            (0, "norm"): [first_weights],
            (0, 7): [lambda: g.line(2)],
            (0, "end"): [lambda: g.turns(1)],
            (1, 3): [lambda: g.line(3)],
            (1, 7): [lambda: g.turns(2)],
            (2, "qkv"): [lambda: g.turns(3)],
            (2, 7): [lambda: g.last(0, 2)],
            (2, "end"): [lambda: g.last(2, depth), leave],
        }
    else:
        x_ref, g_ref, *token_rows = refs[:5]
        w_ref = refs[5]
        hz_ref, pr_ref, attn_ref, qkv_ref, p_ref, key_ref, keyrow_ref, count_ref, combo_ref, x_out, g_out = refs[6:17]
        combos, xp_all, gp_all, normed_all, xb, gb, in_sem, wide, codes, regions, carry = refs[17:28]
    rows = per_group * PAD
    width = x_ref.shape[-1]
    groups = width // 128
    steps = xb.shape[0]
    run_hooks(plan, step, "start")

    def fetch(k):
        return (
            pltpu.make_async_copy(x_ref.at[k], xb.at[k], in_sem.at[0, k]),
            pltpu.make_async_copy(g_ref.at[k], gb.at[k], in_sem.at[1, k]),
        )

    @pl.when(step == 0)
    def _():
        for k in range(steps):
            for copy in fetch(k):
                copy.start()

        def prepare(k, _):
            for copy in fetch(k):
                copy.wait()
            load_windows(xb.at[pl.ds(k, 1)], wide, xp_all.at[k], per_group)
            load_windows(gb.at[pl.ds(k, 1)], wide, gp_all.at[k], per_group)
            normed_all[k] = norm_stats(xp_all[k])[0]
            return 0

        lax.fori_loop(0, steps, prepare, 0)

    run_hooks(plan, step, "prepared")

    @pl.when(step == 0)
    def _():
        carry[...] = jnp.zeros_like(carry)
        packed = (16 * token_rows[1][...] + 256 * token_rows[2][...] + 512).reshape(1, -1) + token_rows[0][...]
        combos[...] = jnp.zeros_like(combos)
        for k in range(combos.shape[0]):
            piece = packed[:, k * WINDOW : (k + 1) * WINDOW]
            combos[k : k + 1, 0:WINDOW] = piece
            combos[k : k + 1, PAD : PAD + WINDOW] = piece
        lane = lax.broadcasted_iota(jnp.int32, (rows, 128), 1)
        before = lax.broadcasted_iota(jnp.int32, (rows, rows), 1) < lax.broadcasted_iota(jnp.int32, (rows, rows), 0)
        before = jnp.where(before, 1.0, 0.0).astype(bf16)
        for k in range(steps):
            route = route_of(token_columns(combos.at[k * per_group : (k + 1) * per_group], per_group))
            onehot = jnp.where(lane == route, 1.0, 0.0)
            ranks = dot_nn(before, onehot.astype(bf16)) + carry[0:1, :]
            slot = jnp.sum(ranks * onehot, axis=-1, keepdims=True)
            seen = jnp.sum(onehot, axis=-1, keepdims=True)
            key = (route.astype(f32) * slots + slot) * seen + (seen - 1.0)
            key = jnp.broadcast_to(key, (rows, 128))
            key_ref[k * rows : (k + 1) * rows, :] = key.astype(jnp.int32)
            keyrow_ref[:, k * rows : (k + 1) * rows] = jnp.transpose(key)[0:1, :].astype(jnp.int32)
            carry[...] = carry[...] + jnp.sum(onehot, axis=0, keepdims=True)
        count_ref[...] = carry[...].astype(jnp.int32)

    combo_ref[...] = combos[pl.ds(pl.multiple_of(step * per_group, per_group), per_group), :]
    combo = token_columns(combo_ref, per_group)
    valid = valid_of(combo)
    route = route_of(combo)
    codes[...] = jnp.where((combo >> 8) & 1 == 1, (combo >> 4) & 15, -1)
    flat = combo_ref[...]
    flat = jnp.where(flat >= 512, (flat >> 4) & 15, -3)
    for k in range(per_group):
        regions[k] = jnp.concatenate([flat[k : k + 1, :]] * 2, axis=1)

    run_hooks(plan, step, "norm")
    normed = normed_all[step]
    small = small_part(w_ref)
    small_t = jnp.transpose(small.astype(f32))
    a1, b1, a2, b2 = (small_t[experts + i : experts + i + 1, :] for i in range(4))
    h1 = (normed * a1 + b1).astype(bf16)
    for part in range(3):
        raw = dot_nn(h1, weight_part(w_ref, part))
        if part == 0:
            raw = raw * (HEAD_DIM**-0.5)
        qkv_ref[:, :, part * width : (part + 1) * width] = raw.astype(bf16).reshape(per_group, PAD, width)
    run_hooks(plan, step, "qkv")

    masks = head_masks()
    key_i = lax.broadcasted_iota(jnp.int32, (PAD, 4 * PAD), 0)
    lane_i = lax.broadcasted_iota(jnp.int32, (PAD, 4 * PAD), 1)
    diagonal = key_i == lax.rem(lane_i, PAD)

    def window(w):
        at = pl.ds(pl.multiple_of(w * PAD, PAD), PAD)
        allowed = (codes[at, :] == regions[w]) | diagonal
        for lg in range(groups):
            q = qkv_ref[w, :, lg * 128 : (lg + 1) * 128]
            k = qkv_ref[w, :, width + lg * 128 : width + (lg + 1) * 128]
            v = qkv_ref[w, :, 2 * width + lg * 128 : 2 * width + (lg + 1) * 128]
            s = dot_nt(k, spread_heads(q, masks))
            s = jnp.where(allowed, s, MASKED)
            e = jnp.exp(s - jnp.max(s, axis=0, keepdims=True))
            p = (e * (1.0 / jnp.sum(e, axis=0, keepdims=True))).astype(bf16)
            p_ref[w, lg] = p
            o = dot_tn(p, v)
            attn_ref[at, lg * 128 : (lg + 1) * 128] = gather_heads(o, masks).astype(bf16)

    def windows(j, _):
        for k in range(GROUP):
            window(j * GROUP + k)
        for i in range(per_group):
            run_hooks(plan, step, i, j * GROUP + GROUP - 1)
        return 0

    lax.fori_loop(0, per_group // GROUP, windows, 0)

    y1 = xp_all[step] + dot_nn(attn_ref[...], weight_part(w_ref, 3))
    normed2, _ = norm_stats(y1)
    h2 = (normed2 * a2 + b2).astype(bf16)
    lane = lax.broadcasted_iota(jnp.int32, (rows, 128), 1)
    logits = jnp.where(lane < experts, dot_nn(h2, small), MASKED)
    e = jnp.exp(logits - jnp.max(logits, axis=-1, keepdims=True))
    pr = e * (1.0 / jnp.sum(e, axis=-1, keepdims=True))
    pr_ref[...] = pr
    chosen = lane == route
    gate = jnp.sum(jnp.where(chosen, pr, 0.0), axis=-1, keepdims=True)
    gv = gp_all[step] * valid
    g_out[...] = gv
    x_out[...] = xp_all[step]
    hz_ref[:, 0:width] = h2
    hz_ref[:, width : 2 * width] = (gate * gv).astype(bf16)

    run_hooks(plan, step, "end")


def expert_kernel(slots, counts_ref, hz_ref, keyrow_ref, keycol_ref, we_ref, grad_ref, tok_ref, acc, tok_acc):
    e = pl.program_id(0)
    width = hz_ref.shape[-1] // 2
    total = hz_ref.shape[0]

    @pl.when(e == 0)
    def _():
        tok_acc[...] = jnp.zeros_like(tok_acc)

    acc[...] = jnp.zeros_like(acc)
    used = counts_ref[e]

    def tile(offset, size):
        base = e * slots + offset
        pick = keyrow_ref[...] == base + lax.broadcasted_iota(jnp.int32, (size, total), 0)
        both = dot_nn(jnp.where(pick, 1.0, 0.0).astype(bf16), hz_ref[...]).astype(bf16)
        rows, dz = both[:, 0:width], both[:, width : 2 * width]
        up = dot_nn(rows, we_ref[0, 0])
        cdf = 0.5 * (1.0 + lax.erf(up * 2.0**-0.5))
        hidden = (up * cdf).astype(bf16)
        slope = cdf + up * (jnp.exp(-0.5 * up * up) * (2.0 * jnp.pi) ** -0.5)
        ret = dot_nt(hidden, we_ref[0, 1]).astype(bf16)
        dup = (dot_nn(dz, we_ref[0, 1]) * slope).astype(bf16)
        back = dot_nt(dup, we_ref[0, 0]).astype(bf16)
        acc[1] += dot_tn(dz, hidden)
        acc[0] += dot_tn(rows, dup)
        keys = jnp.concatenate([keycol_ref[...]] * (size // 128), axis=1)
        put = keys == base + lax.broadcasted_iota(jnp.int32, (total, size), 1)
        tok_acc[...] += dot_nn(jnp.where(put, 1.0, 0.0).astype(bf16), jnp.concatenate([ret, back], axis=1))

    def large(t, _):
        tile(t * TILE, TILE)
        return 0

    count = (used + TILE // 2 - 1) // TILE
    lax.fori_loop(0, count, large, 0)

    @pl.when(used > count * TILE)
    def _():
        tile(count * TILE, TILE // 2)

    grad_ref[0] = acc[...].astype(bf16)

    @pl.when(e == pl.num_programs(0) - 1)
    def _():
        tok_ref[...] = tok_acc[...].astype(bf16)


def backward_kernel(dims, experts, per_group, fast, *refs):
    depth = dims[0] // 2
    plan = {}
    step = pl.program_id(0)
    combo_ref, sources, refs = refs[0], refs[1:9], refs[9:]
    if fast:
        ge_ref, state_hbm = refs[0], refs[1:19]
        out_ref, dx_ref, gexp_ref = refs[19:22]
        results = refs[22:25]
        refs = refs[25:]
    else:
        out_ref, dx_ref, shared_ref, small_ref = refs[:4]
        refs = refs[4:]
    gp, wide, outp, dattn, dqkv, acc, acc_w, acc_s = refs[:8]
    buffers, in_sem = refs[8:16], refs[16]
    w_ref = buffers[0]
    x_all, g_all, tok_all, pr_all, attn_all, qkv_all, p_all = buffers[1:]

    def fetch(i, k):
        if i == 0:
            return pltpu.make_async_copy(sources[0], w_ref, in_sem.at[0, 0])
        return pltpu.make_async_copy(sources[i].at[k], buffers[i].at[k], in_sem.at[i, k])

    def fetch_all():
        fetch(0, 0).start()
        for k in range(x_all.shape[0]):
            for i in range(1, 8):
                fetch(i, k).start()

    if fast:
        sc = Scatter(depth, ge_ref, refs[17:22], refs[22:31])
        state, state_sem, shared_ref, small_ref = refs[31:49], refs[49], refs[50], refs[51]

        def load_state(i):
            return pltpu.make_async_copy(state_hbm[i], state[i], state_sem.at[i])

        def enter():
            meet_all(depth, sc.z, sc.x, sc.y, sc.c)
            sc.begin()
            fetch_all()
            sc.merge(0)

        def start_state():
            for i in range(18):
                load_state(i).start()

        def early():
            sc.second(depth - 1)
            sc.third(depth - 2)

        def middle():
            sc.third(depth - 1)

        def meanwhile():
            for s in range(2):
                gexp_ref[s] = sc.result(s)
            for i in range(18):
                load_state(i).wait()

        def leave():
            for part in range(4):
                shape = shared_ref.shape[2:]
                shared_ref[part // 2, part % 2] = shared_grad(part).reshape(shape)
            small_ref[0:8] = acc_s[0:8]
            small_ref[8:16] = acc_s[128:136]
            shared_scatter(
                depth, experts, early, middle, meanwhile, (shared_ref, small_ref, gexp_ref), state, results, refs[52:]
            )
            sc.finish()

        plan = {
            (0, "start"): [enter],
            (0, "pre"): [lambda: sc.merge(1)],
            (0, 7): [lambda: sc.second(0)],
            (1, "start"): [lambda: sc.merge(2)],
            (1, "pre"): [lambda: sc.second(1), start_state],
            (1, 3): [lambda: sc.merge(3), lambda: sc.third(0)],
            (1, "end"): [lambda: sc.second(2)],
            (2, "pre"): [lambda: sc.third(1)],
            (2, "end"): [leave],
        }
    else:
        plan = {(0, "start"): [fetch_all]}
    rows = per_group * PAD

    def shared_grad(part):
        width = acc.shape[0]
        return (acc[...] if part == 3 else acc_w[:, part * width : (part + 1) * width]).astype(bf16)

    width = x_all.shape[-1]
    groups = width // 128
    scale = HEAD_DIM**-0.5

    @pl.when(step == 0)
    def _():
        acc[...] = jnp.zeros_like(acc)
        acc_w[...] = jnp.zeros_like(acc_w)
        acc_s[...] = jnp.zeros_like(acc_s)

    run_hooks(plan, step, "start")

    @pl.when(step == 0)
    def _():
        fetch(0, 0).wait()

    for i in range(1, 8):
        fetch(i, step).wait()
    combo = token_columns(combo_ref, per_group)
    route = route_of(combo)
    small = small_part(w_ref)
    small_t = jnp.transpose(small.astype(f32))
    a1, b1, a2, b2 = (small_t[experts + i : experts + i + 1, :] for i in range(4))
    y1 = x_all[step] + dot_nn(attn_all[step], weight_part(w_ref, 3))
    gv = g_all[step]
    z = tok_all[step, :, 0:width].astype(f32)
    lane = lax.broadcasted_iota(jnp.int32, (rows, 128), 1)
    chosen = lane == route
    pr = pr_all[step]
    gate = jnp.sum(jnp.where(chosen, pr, 0.0), axis=-1, keepdims=True)
    outp[...] = y1 + gate * z
    store_windows(outp, wide, out_ref, per_group)
    dgate = jnp.sum(gv * z, axis=-1, keepdims=True)
    kept = jnp.where(lane < experts, jnp.where(chosen, 1.0, 0.0) - pr, 0.0)
    dlogits = (dgate * gate * kept).astype(bf16)
    n2, r2 = norm_stats(y1)
    h2 = (n2 * a2 + b2).astype(bf16)
    acc_s[0:128] += dot_tn(dlogits, h2)
    dh2 = dot_nt(dlogits, small) + tok_all[step, :, width : 2 * width].astype(f32)
    acc_s[130:131] += jnp.sum(dh2 * n2, axis=0, keepdims=True)
    acc_s[131:132] += jnp.sum(dh2, axis=0, keepdims=True)
    dy1 = gv + norm_back(dh2, n2, r2, a2)
    gp[...] = dy1
    da = dy1.astype(bf16)
    acc[...] += dot_tn(attn_all[step], da)
    dattn[...] = dot_nt(da, weight_part(w_ref, 3)).astype(bf16)
    run_hooks(plan, step, "pre")

    masks = head_masks()

    def window(w):
        at = pl.ds(pl.multiple_of(w * PAD, PAD), PAD)
        for lg in range(groups):
            cols = slice(lg * 128, (lg + 1) * 128)
            q = qkv_all[step, w, :, lg * 128 : (lg + 1) * 128]
            k = qkv_all[step, w, :, width + lg * 128 : width + (lg + 1) * 128]
            v = qkv_all[step, w, :, 2 * width + lg * 128 : 2 * width + (lg + 1) * 128]
            d_all = spread_heads(dattn[at, cols], masks)
            q_all = spread_heads(q, masks)
            p_low = p_all[step, w, lg]
            p = p_low.astype(f32)
            dp = dot_nt(v, d_all)
            ds = (p * (dp - jnp.sum(dp * p, axis=0, keepdims=True))).astype(bf16)
            dv = dot_nn(p_low, d_all)
            dk = dot_nn(ds, q_all)
            dq = gather_heads(dot_tn(ds, k), masks) * scale
            dqkv[at, 0 * width + lg * 128 : 0 * width + (lg + 1) * 128] = dq.astype(bf16)
            dqkv[at, 1 * width + lg * 128 : 1 * width + (lg + 1) * 128] = dk.astype(bf16)
            dqkv[at, 2 * width + lg * 128 : 2 * width + (lg + 1) * 128] = dv.astype(bf16)

    def windows(j, _):
        for k in range(GROUP):
            window(j * GROUP + k)
        for i in range(per_group):
            run_hooks(plan, step, i, j * GROUP + GROUP - 1)
        return 0

    lax.fori_loop(0, per_group // GROUP, windows, 0)

    n1, r1 = norm_stats(x_all[step])
    h1 = (n1 * a1 + b1).astype(bf16)
    acc_w[...] += dot_tn(h1, dqkv[...])
    dh1 = dot_nt(dqkv[:, 0 : 2 * width], w_ref[0, :, 0 : 2 * width]) + dot_nt(dqkv[:, 2 * width :], weight_part(w_ref, 2))
    acc_s[128:129] += jnp.sum(dh1 * n1, axis=0, keepdims=True)
    acc_s[129:130] += jnp.sum(dh1, axis=0, keepdims=True)
    outp[...] = gp[...] + norm_back(dh1, n1, r1, a1)
    store_windows(outp, wide, dx_ref, per_group)

    if not fast:

        @pl.when(step == pl.num_programs(0) - 1)
        def _():
            for part in range(4):
                shared_ref[part] = shared_grad(part)
            small_ref[0:8] = acc_s[0:8]
            small_ref[8:16] = acc_s[128:136]

    run_hooks(plan, step, "end")


def place():
    dp, ex = lax.axis_index("dp"), lax.axis_index("expert")
    return lax.div(dp, 2), lax.rem(dp, 2), lax.div(ex, 2), lax.rem(ex, 2)


def at(z, x, y, c):
    return (z * 2 + x, y * 2 + c)


def push(src, dst, send_sem, recv_sem, device):
    copy = pltpu.make_async_remote_copy(
        src_ref=src,
        dst_ref=dst,
        send_sem=send_sem,
        recv_sem=recv_sem,
        device_id=device,
        device_id_type=pl.DeviceIdType.MESH,
    )
    return copy


def meet(z, x, y, c, depth):
    barrier = pltpu.get_barrier_semaphore()

    def greet(device):
        pl.semaphore_signal(barrier, inc=1, device_id=device, device_id_type=pl.DeviceIdType.MESH)

    greet(at(z, x, y, 1 - c))
    greet(at(z, 1 - x, y, c))
    greet(at(z, x, 1 - y, c))
    for other in range(depth):
        @pl.when(z != other)
        def _():
            greet(at(other, x, y, c))

    pl.semaphore_wait(barrier, 3 + depth - 1)


class Gather:
    def __init__(self, depth, ex_ref, we_ref, sems):
        self.depth = depth
        self.ex, self.we = ex_ref, we_ref
        (self.loc, self.zs, self.zr, self.xs, self.xr, self.ys, self.yr, self.cs, self.cr) = sems
        self.z, self.x, self.y, self.c = place()

    @staticmethod
    def semaphores(depth):
        dma = pltpu.SemaphoreType.DMA
        return [
            dma((1,)),
            dma((2, depth)),
            dma((depth,)),
            dma((3, depth)),
            dma((3, depth)),
            dma((3, depth)),
            dma((3, depth)),
            dma((7, depth)),
            dma((7, depth)),
        ]

    def local(self):
        return pltpu.make_async_copy(self.ex, self.pair(self.y, self.c, self.z, self.x), self.loc.at[0])

    def block(self, y, c, s, z, x):
        return self.we.at[y * 2 + c, s, z * 2 + x]

    def pair(self, y, c, z, x):
        return self.we.at[y * 2 + c, :, z * 2 + x]

    def z_copy(self, up, zo, first=False):
        mine = self.ex if first else self.pair(self.y, self.c, zo, self.x)
        target = self.z + 1 if up else self.z - 1
        return push(
            mine,
            self.pair(self.y, self.c, zo, self.x),
            self.zs.at[0 if up else 1, zo],
            self.zr.at[zo],
            at(target, self.x, self.y, self.c),
        )

    def x_copy(self, kind, zo, y, first=False):
        s = 0 if kind == 0 else 1
        dst = self.block(y, self.c, s, zo, self.x)
        src = self.ex.at[s] if first else dst
        return push(src, dst, self.xs.at[kind, zo], self.xr.at[kind, zo], at(self.z, 1 - self.x, self.y, self.c))

    def y_copy(self, kind, zo, x, first=False):
        s = 1 if kind == 0 else 0
        dst = self.block(self.y, self.c, s, zo, x)
        src = self.ex.at[s] if first else dst
        return push(src, dst, self.ys.at[kind, zo], self.yr.at[kind, zo], at(self.z, self.x, 1 - self.y, self.c))

    def c_copy(self, kind, zo, c, first=False):
        x, y = self.x, self.y
        if kind == 0:
            dst = self.pair(y, c, zo, x)
        elif kind == 1:
            dst = self.block(y, c, 0, zo, 1 - x)
        elif kind == 2:
            dst = self.block(1 - y, c, 1, zo, x)
        elif kind in (3, 4):
            dst = self.block(1 - y, c, 0, zo, x if kind == 3 else 1 - x)
        else:
            dst = self.block(y if kind == 5 else 1 - y, c, 1, zo, 1 - x)
        src = self.ex if first else dst
        return push(src, dst, self.cs.at[kind, zo], self.cr.at[kind, zo], at(self.z, x, y, 1 - self.c))

    def spread(self, zo, first=False):
        self.x_copy(0, zo, self.y, first).start()
        self.y_copy(0, zo, self.x, first).start()
        self.y_copy(1, zo, self.x, first).start()
        self.x_copy(1, zo, self.y, first).start()
        self.c_copy(0, zo, self.c, first).start()

    def begin(self):
        z = self.z
        self.local().start()

        @pl.when(z < self.depth - 1)
        def _():
            self.z_copy(True, z, True).start()

        @pl.when(z > 0)
        def _():
            self.z_copy(False, z, True).start()

        self.spread(z, True)

    def line(self, s):
        z = self.z

        @pl.when(z - s >= 0)
        def _():
            self.z_copy(True, z - s).wait_recv()

            @pl.when(z < self.depth - 1)
            def _():
                self.z_copy(True, z - s).start()

            self.spread(z - s)

        @pl.when(z + s < self.depth)
        def _():
            self.z_copy(True, z + s).wait_recv()

            @pl.when(z > 0)
            def _():
                self.z_copy(False, z + s).start()

            self.spread(z + s)

    def turn(self, zo):
        self.x_copy(0, zo, self.y).wait_recv()
        self.y_copy(2, zo, 1 - self.x).start()
        self.c_copy(1, zo, self.c).start()
        self.y_copy(0, zo, self.x).wait_recv()
        self.x_copy(2, zo, 1 - self.y).start()
        self.c_copy(2, zo, self.c).start()

    def turns(self, s):
        z = self.z
        if s == 0:
            self.turn(z)
            return

        @pl.when(z - s >= 0)
        def _():
            self.turn(z - s)

        @pl.when(z + s < self.depth)
        def _():
            self.turn(z + s)

    def last(self, first, end):
        turn = 1 - 2 * lax.div(self.z, self.depth // 2)
        for j in range(first, end):
            zo = lax.rem(self.z + j * turn + self.depth, self.depth)
            for kind, ck in ((1, 3), (2, 4)):
                self.y_copy(kind, zo, self.x).wait_recv()
                self.c_copy(ck, zo, self.c).start()
            for kind, ck in ((1, 5), (2, 6)):
                self.x_copy(kind, zo, self.y).wait_recv()
                self.c_copy(ck, zo, self.c).start()

    def finish(self):
        z = self.z
        for zo in range(self.depth):
            for kind in range(7):
                self.c_copy(kind, zo, 1 - self.c).wait_recv()
        self.local().wait()
        for zo in range(self.depth):
            @pl.when((z < self.depth - 1) & (zo <= z))
            def _():
                self.z_copy(True, zo).wait_send()

            @pl.when((z > 0) & (zo >= z))
            def _():
                self.z_copy(False, zo).wait_send()

            for kind in range(3):
                self.x_copy(kind, zo, self.y).wait_send()
                self.y_copy(kind, zo, self.x).wait_send()
            for kind in range(7):
                self.c_copy(kind, zo, self.c).wait_send()


class SharedGather:
    def __init__(self, depth, sh_ref, ws_ref, sems):
        self.depth, self.sh, self.ws = depth, sh_ref, ws_ref
        self.loc, self.zs, self.zr, self.xs, self.xr, self.cs, self.cr = sems
        self.z, self.x, self.y, self.c = place()

    @staticmethod
    def semaphores(depth):
        dma = pltpu.SemaphoreType.DMA
        return [dma((1,)), dma((depth,)), dma((depth,)), dma((depth,)), dma((depth,)), dma((2, depth)), dma((2, depth))]

    def slot(self, zo, xo):
        return self.ws.at[self.c, zo * 2 + xo]

    def local(self):
        return pltpu.make_async_copy(self.sh.at[self.c], self.slot(self.z, self.x), self.loc.at[0])

    def z_copy(self, target):
        return push(
            self.sh.at[self.c],
            self.slot(self.z, self.x),
            self.zs.at[target],
            self.zr.at[self.z],
            at(target, self.x, self.y, self.c),
        )

    def z_from(self, zo):
        dst = self.slot(zo, self.x)
        return push(dst, dst, self.zs.at[zo], self.zr.at[zo], at(zo, self.x, self.y, self.c))

    def x_copy(self, zo, first=False):
        dst = self.slot(zo, self.x)
        src = self.sh.at[self.c] if first else dst
        return push(src, dst, self.xs.at[zo], self.xr.at[zo], at(self.z, 1 - self.x, self.y, self.c))

    def c_copy(self, zo, xo, first=False):
        dst = self.slot(zo, xo)
        src = self.sh.at[self.c] if first else dst
        return push(src, dst, self.cs.at[xo, zo], self.cr.at[xo, zo], at(self.z, self.x, self.y, 1 - self.c))

    def others(self):
        return [lax.rem(self.z + j, self.depth) for j in range(1, self.depth)]

    def begin(self):
        self.local().start()
        for zo in self.others():
            self.z_copy(zo).start()
        self.x_copy(self.z, True).start()
        self.c_copy(self.z, self.x, True).start()

    def along_z(self):
        for zo in self.others():
            self.z_from(zo).wait_recv()
            self.x_copy(zo).start()
            self.c_copy(zo, self.x).start()

    def along_x(self):
        for j in range(self.depth):
            zo = lax.rem(self.z + j, self.depth)
            self.x_copy(zo).wait_recv()
            self.c_copy(zo, 1 - self.x).start()
        for zo in range(self.depth):
            for xo in range(2):
                self.c_copy(zo, xo).wait_recv()
        self.local().wait()

    def finish(self):
        for zo in self.others():
            self.z_copy(zo).wait_send()
        for zo in range(self.depth):
            self.x_copy(zo).wait_send()
            for xo in range(2):
                self.c_copy(zo, xo).wait_send()


class Scatter:
    def __init__(self, depth, ge_ref, bufs, sems):
        self.depth = depth
        self.ge = ge_ref
        self.t, self.rc, self.r1, self.r2, self.r3 = bufs
        (self.ls, self.cs, self.cr, self.s1, self.q1, self.s2, self.q2, self.s3, self.q3) = sems
        self.z, self.x, self.y, self.c = place()

    @staticmethod
    def scratch(depth, cols, shard):
        dma = pltpu.SemaphoreType.DMA
        bufs = [
            pltpu.VMEM((2, 2, depth, 2, shard, cols), bf16),
            pltpu.VMEM((2, 2, depth, 2, shard, cols), bf16),
            pltpu.VMEM((2, depth, 2, shard, cols), bf16),
            pltpu.VMEM((2, depth, shard, cols), bf16),
            pltpu.VMEM((2, depth, shard, cols), bf16),
        ]
        sems = [
            dma((2, 2, depth)),
            dma((2, 2, depth)),
            dma((2, 2, depth)),
            dma((2, depth, 2)),
            dma((2, depth, 2)),
            dma((2, depth)),
            dma((2, depth)),
            dma((2, depth)),
            dma((2, depth)),
        ]
        return bufs + sems

    def local(self, i, s, zo):
        y = self.y if i == 0 else 1 - self.y
        return pltpu.make_async_copy(self.ge.at[y * 2 + self.c, s, zo], self.t.at[i, s, zo], self.ls.at[i, s, zo])

    def core(self, i, s, zo):
        y = self.y if i == 0 else 1 - self.y
        return push(
            self.ge.at[y * 2 + 1 - self.c, s, zo],
            self.rc.at[i, s, zo],
            self.cs.at[i, s, zo],
            self.cr.at[i, s, zo],
            at(self.z, self.x, self.y, 1 - self.c),
        )

    def one(self, s, zo, k):
        if s == 0:
            src, device = self.t.at[1, 0, zo, k], at(self.z, self.x, 1 - self.y, self.c)
        else:
            src, device = self.t.at[k, 1, zo, 1 - self.x], at(self.z, 1 - self.x, self.y, self.c)
        return push(src, self.r1.at[s, zo, k], self.s1.at[s, zo, k], self.q1.at[s, zo, k], device)

    def two(self, s, zo):
        if s == 0:
            src, device = self.t.at[0, 0, zo, 1 - self.x], at(self.z, 1 - self.x, self.y, self.c)
        else:
            src, device = self.t.at[1, 1, zo, self.x], at(self.z, self.x, 1 - self.y, self.c)
        return push(src, self.r2.at[s, zo], self.s2.at[s, zo], self.q2.at[s, zo], device)

    def three(self, s, zo):
        return push(
            self.t.at[0, s, zo, self.x],
            self.r3.at[s, self.z],
            self.s3.at[s, zo],
            self.q3.at[s, self.z],
            at(zo, self.x, self.y, self.c),
        )

    def arrived(self, s, zo):
        return push(
            self.r3.at[s, zo], self.r3.at[s, zo], self.s3.at[s, zo], self.q3.at[s, zo], at(zo, self.x, self.y, self.c)
        )

    def begin(self):
        def body(j, _):
            zo = self.order(j)
            for i, s in ((1, 0), (0, 1), (1, 1), (0, 0)):
                self.core(i, s, zo).start()
                self.local(i, s, zo).start()
            return 0

        lax.fori_loop(0, self.depth, body, 0)

    def order(self, j):
        return lax.rem(self.z + j + 1, self.depth)

    def fold(self, ref, other):
        ref[...] = (ref[...].astype(f32) + other[...].astype(f32)).astype(bf16)

    def merge(self, j):
        zo = self.order(j)
        for i, s in ((1, 0), (0, 1), (1, 1), (0, 0)):
            self.core(i, s, zo).wait_recv()
            self.local(i, s, zo).wait()
            for xo in range(2):
                self.fold(self.t.at[i, s, zo, xo], self.rc.at[i, s, zo, xo])
            if (i, s) == (1, 0):
                self.one(0, zo, 0).start()
                self.one(0, zo, 1).start()
            if s == 1:
                self.one(1, zo, i).start()

    def second(self, j):
        zo = self.order(j)
        for k in range(2):
            self.one(0, zo, k).wait_recv()
            self.fold(self.t.at[0, 0, zo, k], self.r1.at[0, zo, k])
        self.two(0, zo).start()
        for k in range(2):
            self.one(1, zo, k).wait_recv()
            self.fold(self.t.at[k, 1, zo, self.x], self.r1.at[1, zo, k])
        self.two(1, zo).start()

    def third(self, j):
        zo = self.order(j)
        for s in range(2):
            self.two(s, zo).wait_recv()
            self.fold(self.t.at[0, s, zo, self.x], self.r2.at[s, zo])

            @pl.when(zo != self.z)
            def _():
                self.three(s, zo).start()

    def result(self, s):
        total = self.t[0, s, self.z, self.x].astype(f32)
        for j in range(1, self.depth):
            zo = lax.rem(self.z + j, self.depth)
            self.arrived(s, zo).wait_recv()
            total = total + self.r3[s, zo].astype(f32)
        return total

    def finish(self):
        def body(j, _):
            zo = self.order(j)
            for s in range(2):
                for i in range(2):
                    self.core(i, s, zo).wait_send()
                for k in range(2):
                    self.one(s, zo, k).wait_send()
                self.two(s, zo).wait_send()

                @pl.when(zo != self.z)
                def _():
                    self.three(s, zo).wait_send()

            return 0

        lax.fori_loop(0, self.depth, body, 0)


def lamb_parts(weight, grad, first, second):
    first_new = BETA_ONE * first + (1.0 - BETA_ONE) * grad
    second_new = BETA_TWO * second + (1.0 - BETA_TWO) * grad * grad
    first_hat = first_new / (1.0 - BETA_ONE**STEP)
    second_hat = second_new / (1.0 - BETA_TWO**STEP)
    direction = first_hat / (jnp.sqrt(second_hat) + ADAM_EPS) + DECAY * weight
    return first_new, second_new, direction


def row_norms(values, lane0):
    lane = lax.broadcasted_iota(jnp.int32, (1, 128), 1)
    out = jnp.zeros((1, 128), f32)
    for i, v in enumerate(values):
        out = out + jnp.where(lane == lane0 + i, jnp.sum(v * v), 0.0)
    return out


def peers(n, me):
    return [lax.rem(me + j, n) for j in range(1, n)]


def meet_all(depth, z, x, y, c):
    barrier = pltpu.get_barrier_semaphore()
    dp, ex = z * 2 + x, y * 2 + c
    n_dp, n_ex = 2 * depth, 4
    for other in peers(n_dp, dp):
        pl.semaphore_signal(barrier, inc=1, device_id=(other, ex), device_id_type=pl.DeviceIdType.MESH)
    for other in peers(n_ex, ex):
        pl.semaphore_signal(barrier, inc=1, device_id=(dp, other), device_id_type=pl.DeviceIdType.MESH)
    pl.semaphore_wait(barrier, n_dp + n_ex - 2)


def shared_scatter(depth, experts, early, middle, meanwhile, operands, state, outputs, scratch):
    gs_ref, sm_ref, ge_ref = operands
    weights, firsts, seconds = state[0:6], state[6:12], state[12:18]
    fs_out, gsm_ref, norm_ref = outputs
    (t, rc, r1, r2, r3, src_c, src_y, src_x, sz, cur, wide, nb, nq, fs_ref) = scratch[:14]
    (ccs, ccr, s1, q1, s2, q2, s3, q3, s4, q4, ms, mr, zs, zr, ns, nr, es, er) = scratch[14:]
    z, x, y, c = place()
    dp, ex = z * 2 + x, y * 2 + c
    n_dp, n_ex = 2 * depth, 4
    shard = fs_ref.shape[1]
    width = fs_ref.shape[2]

    near = [at(z, x, y, 1 - c), at(z, x, 1 - y, c), at(z, 1 - x, y, c)]
    y_of = [y, 1 - y]

    def core(i):
        return push(gs_ref.at[y_of[i], 1 - c], rc.at[i], ccs.at[i], ccr.at[i], near[0])

    order = [lax.rem(z + 1 + j, depth) for j in range(depth)]

    def one(j, k):
        zo = order[j]
        if j % 2 == 0:
            return push(t.at[1, zo, k], r1.at[zo, k], s1.at[zo, k], q1.at[zo, k], near[1])
        return push(t.at[k, zo, 1 - x], r1.at[zo, k], s1.at[zo, k], q1.at[zo, k], near[2])

    def two(j):
        zo = order[j]
        if j % 2 == 0:
            return push(t.at[0, zo, 1 - x], r2.at[zo], s2.at[zo], q2.at[zo], near[2])
        return push(t.at[1, zo, x], r2.at[zo], s2.at[zo], q2.at[zo], near[1])

    def three(zo):
        return push(t.at[0, zo, x], r3.at[z], s3.at[zo], q3.at[z], at(zo, x, y, c))

    def arrived(zo):
        return push(r3.at[zo], r3.at[zo], s3.at[zo], q3.at[zo], at(zo, x, y, c))

    def small_hop(k):
        src = sm_ref if k == 0 else cur.at[k - 1]
        return push(src, (src_c, src_y, src_x)[k], ms.at[k], mr.at[k], near[k])

    def small_z(zo):
        return push(cur.at[2], sz.at[z], zs.at[zo], zr.at[z], at(zo, x, y, c))

    def small_from(zo):
        return push(sz.at[zo], sz.at[zo], zs.at[zo], zr.at[zo], at(zo, x, y, c))

    def fold(ref, a, b):
        ref[...] = (a[...].astype(f32) + b[...].astype(f32)).astype(bf16)

    small_hop(0).start()
    core(1).start()
    core(0).start()
    early()
    small_hop(0).wait_recv()
    cur[0] = sm_ref[...] + src_c[...]
    small_hop(1).start()
    for i in (1, 0):
        core(i).wait_recv()
        for j, zo in enumerate(order):
            for k in range(2):
                fold(t.at[i, zo, k], gs_ref.at[y_of[i], c, zo, k], rc.at[i, zo, k])
            if j % 2 == 0:
                if i == 1:
                    one(j, 0).start()
                    one(j, 1).start()
            else:
                one(j, i).start()
    middle()
    small_hop(1).wait_recv()
    cur[1] = cur[0] + src_y[...]
    small_hop(2).start()
    for j, zo in enumerate(order):
        for k in range(2):
            one(j, k).wait_recv()
            target = t.at[0, zo, k] if j % 2 == 0 else t.at[k, zo, x]
            fold(target, target, r1.at[zo, k])
        two(j).start()
    small_hop(2).wait_recv()
    cur[2] = cur[1] + src_x[...]
    sz[z] = cur[2]
    for zo in range(depth):
        @pl.when(zo != z)
        def _():
            small_z(zo).start()

    for j, zo in enumerate(order):
        two(j).wait_recv()
        target = t.at[0, zo, x]
        fold(target, target, r2.at[zo])
        if j < depth - 1:
            three(zo).start()

    meanwhile()
    totals = row_norms([w[...] for w in weights], 0)
    for i in range(2):
        direction = lamb_parts(weights[4 + i][...], ge_ref[i], firsts[4 + i][...], seconds[4 + i][...])[2]
        totals = totals + row_norms([direction], 10 + i)
    total = t[0, z, x].astype(f32)
    for zo in peers(depth, z):
        arrived(zo).wait_recv()
        total = total + r3[zo].astype(f32)
    fs_ref[ex] = total

    def four(e):
        return push(fs_ref.at[ex], fs_ref.at[ex], s4.at[e], q4.at[ex], (dp, e))

    def four_from(e):
        return push(fs_ref.at[e], fs_ref.at[e], s4.at[e], q4.at[e], (dp, e))

    def quarter(e):
        return push(nq.at[ex], nq.at[ex], es.at[e], er.at[ex], (dp, e))

    def quarter_from(e):
        return push(nq.at[e], nq.at[e], es.at[e], er.at[e], (dp, e))

    def part_of(refs):
        out = refs[1][...]
        for p in range(3):
            out = jnp.where(ex == p, refs[0][:, p * width : (p + 1) * width], out)
        return out

    direction = lamb_parts(part_of(weights), total, part_of(firsts), part_of(seconds))[2]
    lane = lax.broadcasted_iota(jnp.int32, (8, 128), 1)
    nq[ex] = jnp.where(lane == jnp.where(ex == 3, 7, 6), jnp.sum(direction * direction), 0.0)
    for e in peers(n_ex, ex):
        quarter(e).start()
    for e in peers(n_ex, ex):
        four(e).start()
    for zo in peers(depth, z):
        small_from(zo).wait_recv()
    small = sz[0]
    for zo in range(1, depth):
        small = small + sz[zo]
    wide[...] = jnp.transpose(jnp.concatenate([small, jnp.zeros((128 - 16, small.shape[1]), f32)], axis=0))
    mine = jnp.transpose(wide[pl.ds(pl.multiple_of(dp * shard, 16), shard), :])[0:16]
    gsm_ref[...] = mine
    for i, g in ((2, mine[0:experts]), (3, mine[8:12])):
        direction = lamb_parts(weights[i][...], g, firsts[i][...], seconds[i][...])[2]
        totals = totals + row_norms([direction], 6 + i)
    for e in peers(n_ex, ex):
        quarter_from(e).wait_recv()
    combined = jnp.broadcast_to(totals, (8, 128))
    for e in range(n_ex):
        combined = combined + nq[e]
    nb[dp] = combined

    def norm_push(r):
        return push(nb.at[dp], nb.at[dp], ns.at[r], nr.at[dp], (r, ex))

    def norm_from(r):
        return push(nb.at[r], nb.at[r], ns.at[r], nr.at[r], (r, ex))

    for r in peers(n_dp, dp):
        norm_push(r).start()
    for e in peers(n_ex, ex):
        four_from(e).wait_recv()
    fs_out[...] = fs_ref[...]
    for r in peers(n_dp, dp):
        norm_from(r).wait_recv()
    summed = nb[0]
    for r in range(1, n_dp):
        summed = summed + nb[r]
    norm_ref[...] = summed
    for e in peers(n_ex, ex):
        quarter(e).wait_send()

    for r in peers(n_dp, dp):
        norm_push(r).wait_send()
    for e in peers(n_ex, ex):
        four(e).wait_send()
    for i in range(2):
        core(i).wait_send()
    for k in range(3):
        small_hop(k).wait_send()
    for j, zo in enumerate(order):
        for k in range(2):
            one(j, k).wait_send()
        two(j).wait_send()
        if j < depth - 1:
            three(zo).wait_send()
            small_z(zo).wait_send()


def shared_scatter_scratch(depth, shard, width):
    dma = pltpu.SemaphoreType.DMA
    return [
        pltpu.VMEM((2, depth, 2, shard, width), bf16),
        pltpu.VMEM((2, depth, 2, shard, width), bf16),
        pltpu.VMEM((depth, 2, shard, width), bf16),
        pltpu.VMEM((depth, shard, width), bf16),
        pltpu.VMEM((depth, shard, width), bf16),
        pltpu.VMEM((16, width), f32),
        pltpu.VMEM((16, width), f32),
        pltpu.VMEM((16, width), f32),
        pltpu.VMEM((depth, 16, width), f32),
        pltpu.VMEM((3, 16, width), f32),
        pltpu.VMEM((width, 128), f32),
        pltpu.VMEM((2 * depth, 8, 128), f32),
        pltpu.VMEM((4, 8, 128), f32),
        pltpu.VMEM((4, shard, width), f32),
        dma((2,)),
        dma((2,)),
        dma((depth, 2)),
        dma((depth, 2)),
        dma((depth,)),
        dma((depth,)),
        dma((depth,)),
        dma((depth,)),
        dma((4,)),
        dma((4,)),
        dma((3,)),
        dma((3,)),
        dma((depth,)),
        dma((depth,)),
        dma((2 * depth,)),
        dma((2 * depth,)),
        dma((4,)),
        dma((4,)),
    ]


def update_kernel(experts, *refs):
    (gsh_ref, gsm_ref, ge_ref, norm_ref), weights, firsts, seconds = refs[:4], refs[4:10], refs[10:16], refs[16:22]
    w_out, m_out, s_out = refs[22:28], refs[28:34], refs[34:40]
    trust_ref = refs[40]
    width = gsh_ref.shape[2]
    totals = norm_ref[0:1, :]
    lane = lax.broadcasted_iota(jnp.int32, (1, 128), 1)

    def pick(i):
        return jnp.sqrt(jnp.sum(jnp.where(lane == i, totals, 0.0), axis=-1, keepdims=True))

    row = lax.broadcasted_iota(jnp.int32, (2, 6), 1)
    col = lax.broadcasted_iota(jnp.int32, (2, 6), 0)
    trust = jnp.zeros((2, 6), f32)
    whole = slice(None)
    jobs = [(0, slice(p * width, (p + 1) * width), lambda p=p: gsh_ref[p]) for p in range(3)]
    jobs += [(1, whole, lambda: gsh_ref[3]), (2, whole, lambda: gsm_ref[0:experts]), (3, whole, lambda: gsm_ref[8:12])]
    jobs += [(4, whole, lambda: ge_ref[0]), (5, whole, lambda: ge_ref[1])]
    ratios = []
    for i in range(6):
        wn, un = pick(i), pick(6 + i)
        ratios.append(wn / (un + 1e-06))
        trust = jnp.where((row == i) & (col == 0), wn, jnp.where((row == i) & (col == 1), un, trust))
    trust_ref[...] = trust
    for i, cols, grad in jobs:
        weight = weights[i][:, cols]
        first, second, direction = lamb_parts(weight, grad(), firsts[i][:, cols], seconds[i][:, cols])
        w_out[i][:, cols] = weight - RATE * ratios[i] * direction
        m_out[i][:, cols] = first
        s_out[i][:, cols] = second


def per_device(
    dims,
    tokens,
    cotangent,
    routes,
    valid_mask,
    shift_region,
    qkv_weight,
    proj_weight,
    router_weight,
    norm_params,
    expert_in,
    expert_out,
    qkv_first,
    qkv_second,
    proj_first,
    proj_second,
    router_first,
    router_second,
    norm_first,
    norm_second,
    in_first,
    in_second,
    out_first,
    out_second,
):
    rows_here, width = tokens.shape
    experts = router_weight.shape[1]
    hidden = expert_in.shape[2]
    shard = qkv_weight.shape[0]
    capacity = 2 * rows_here // experts
    slots = -(-capacity // TILE) * TILE
    windows = rows_here // WINDOW
    per_group = 8
    steps = windows // per_group
    group_rows = per_group * WINDOW
    padded = windows * PAD

    fast = dims == (8, 4)
    depth = dims[0] // 2
    vmem = pl.BlockSpec(memory_space=pltpu.VMEM)
    anywhere = pl.BlockSpec(memory_space=pl.ANY)

    def remote(collective_id):
        return pltpu.CompilerParams(
            vmem_limit_bytes=VMEM_BYTES, collective_id=collective_id, has_side_effects=True
        )

    x3 = tokens.reshape(steps, group_rows, width)
    g3 = cotangent.reshape(steps, group_rows, width)
    token_rows = (routes.reshape(1, rows_here), shift_region, valid_mask)

    rows = per_group * PAD
    params = pltpu.CompilerParams(vmem_limit_bytes=VMEM_BYTES, dimension_semantics=("arbitrary",))

    def by_step(*shape):
        zeros = (0,) * (len(shape) - 1)
        return pl.BlockSpec(shape, lambda i: (i,) + zeros)

    def whole(*shape):
        zeros = (0,) * len(shape)
        return pl.BlockSpec(shape, lambda i, *_: zeros)

    lanes = width // 128
    token_specs = [anywhere] * 2 + [whole(1, rows_here), whole(rows_here), whole(rows_here)]
    forward_out = [
        by_step(rows, 2 * width),
        by_step(rows, 128),
        by_step(rows, width),
        by_step(per_group, PAD, 3 * width),
        by_step(per_group, lanes, PAD, 4 * PAD),
        whole(padded, 128),
        whole(1, padded),
        whole(1, 128),
        by_step(per_group, 128),
        by_step(rows, width),
        by_step(rows, width),
    ]
    forward_shape = [
        jax.ShapeDtypeStruct((padded, 2 * width), bf16),
        jax.ShapeDtypeStruct((padded, 128), f32),
        jax.ShapeDtypeStruct((padded, width), bf16),
        jax.ShapeDtypeStruct((windows, PAD, 3 * width), bf16),
        jax.ShapeDtypeStruct((windows, lanes, PAD, 4 * PAD), bf16),
        jax.ShapeDtypeStruct((padded, 128), jnp.int32),
        jax.ShapeDtypeStruct((1, padded), jnp.int32),
        jax.ShapeDtypeStruct((1, 128), jnp.int32),
        jax.ShapeDtypeStruct((windows, 128), jnp.int32),
        jax.ShapeDtypeStruct((padded, width), f32),
        jax.ShapeDtypeStruct((padded, width), f32),
    ]
    forward_scratch = [
        pltpu.VMEM((windows, 128), jnp.int32),
        pltpu.VMEM((steps, rows, width), f32),
        pltpu.VMEM((steps, rows, width), f32),
        pltpu.VMEM((steps, rows, width), f32),
        pltpu.VMEM(x3.shape, x3.dtype),
        pltpu.VMEM(g3.shape, g3.dtype),
        pltpu.SemaphoreType.DMA((2, steps)),
        pltpu.VMEM((group_rows, width), f32),
        pltpu.VMEM((rows, 1), jnp.int32),
        pltpu.VMEM((per_group, 1, 4 * PAD), jnp.int32),
        pltpu.VMEM((1, 128), f32),
    ]
    body = functools.partial(forward_kernel, dims, experts, slots, per_group, fast)
    if fast:
        own = (qkv_weight, proj_weight, router_weight.T, norm_params.T, expert_in, expert_out)
        *forward, w_all, w_exp = pl.pallas_call(
            body,
            grid=(steps,),
            in_specs=token_specs + [whole(*v.shape) for v in own],
            out_specs=forward_out + [anywhere, anywhere],
            out_shape=forward_shape
            + [
                jax.ShapeDtypeStruct((2, 2 * depth, shard, 2 * width + 128), bf16),
                jax.ShapeDtypeStruct((experts, 2, 2 * depth, shard, hidden), bf16),
            ],
            scratch_shapes=forward_scratch
            + [
                pltpu.VMEM((2, 2 * depth, shard, 2 * width + 128), bf16),
                pltpu.VMEM((2, shard, 2 * width + 128), bf16),
                pltpu.VMEM((2, shard, hidden), bf16),
                pltpu.SemaphoreType.DMA((1,)),
            ]
            + SharedGather.semaphores(depth)
            + Gather.semaphores(depth),
            compiler_params=remote(0),
            name="attention_forward",
        )(x3, g3, *token_rows, *own)
    else:
        pack = jnp.concatenate([router_weight, norm_params], axis=1)
        pack = jnp.pad(pack, ((0, 0), (0, 128 - pack.shape[1])))
        shared_shard = jnp.stack(
            [
                jnp.concatenate([qkv_weight[:, : 2 * width], pack], axis=1),
                jnp.concatenate([qkv_weight[:, 2 * width :], proj_weight, pack], axis=1),
            ]
        ).astype(bf16)
        expert_shard = jnp.stack([expert_in[0], expert_out[0]]).astype(bf16)
        w_all = lax.all_gather(shared_shard, "dp", axis=1, tiled=True)
        w_exp = lax.all_gather(lax.all_gather(expert_shard, "dp", axis=1, tiled=True), "expert", axis=0, tiled=False)
        forward = pl.pallas_call(
            body,
            grid=(steps,),
            in_specs=token_specs + [whole(*w_all.shape)],
            out_specs=forward_out,
            out_shape=forward_shape,
            scratch_shapes=forward_scratch,
            compiler_params=params,
            name="attention_forward",
        )(x3, g3, *token_rows, w_all)
    hz, pr, attn, qkv, probs, key, key_row, counts, combo, x_pad, g_pad = forward
    w_all = w_all.reshape(2, width, 2 * width + 128)
    w_exp = w_exp.reshape(experts, 2, width, hidden)

    grads, tok = pl.pallas_call(
        functools.partial(expert_kernel, slots),
        grid_spec=pltpu.PrefetchScalarGridSpec(
            num_scalar_prefetch=1,
            grid=(experts,),
            in_specs=[
                whole(padded, 2 * width),
                whole(1, padded),
                whole(padded, 128),
                pl.BlockSpec((1, 2, width, hidden), lambda e, *_: (e, 0, 0, 0)),
            ],
            out_specs=[
                pl.BlockSpec((1, 2, width, hidden), lambda e, *_: (e, 0, 0, 0)),
                whole(padded, 2 * width),
            ],
            scratch_shapes=[pltpu.VMEM((2, width, hidden), f32), pltpu.VMEM((padded, 2 * width), f32)],
        ),
        out_shape=[
            jax.ShapeDtypeStruct((experts, 2, width, hidden), bf16),
            jax.ShapeDtypeStruct((padded, 2 * width), bf16),
        ],
        compiler_params=params,
        name="experts",
    )(counts[0], hz, key_row, key, w_exp)

    staged = (
        w_all,
        x_pad.reshape(steps, rows, width),
        g_pad.reshape(steps, rows, width),
        tok.reshape(steps, rows, 2 * width),
        pr.reshape(steps, rows, 128),
        attn.reshape(steps, rows, width),
        qkv.reshape(steps, per_group, PAD, 3 * width),
        probs.reshape(steps, per_group, lanes, PAD, 4 * PAD),
    )
    backward_in = (combo, *staged)
    backward_specs = [by_step(per_group, 128)] + [anywhere] * len(staged)
    backward_out = [
        by_step(1, group_rows, width),
        by_step(1, group_rows, width),
        whole(4, width, width),
        whole(16, width),
    ]
    backward_shape = [
        jax.ShapeDtypeStruct((steps, group_rows, width), bf16),
        jax.ShapeDtypeStruct((steps, group_rows, width), f32),
        jax.ShapeDtypeStruct((4, width, width), bf16),
        jax.ShapeDtypeStruct((16, width), f32),
    ]
    backward_scratch = [
        pltpu.VMEM((rows, width), f32),
        pltpu.VMEM((group_rows, width), f32),
        pltpu.VMEM((rows, width), f32),
        pltpu.VMEM((rows, width), bf16),
        pltpu.VMEM((rows, 3 * width), bf16),
        pltpu.VMEM((width, width), f32),
        pltpu.VMEM((width, 3 * width), f32),
        pltpu.VMEM((136, width), f32),
        *[pltpu.VMEM(v.shape, v.dtype) for v in staged],
        pltpu.SemaphoreType.DMA((8, steps)),
    ]
    weights_now = (qkv_weight, proj_weight, router_weight.T, norm_params.T, expert_in[0], expert_out[0])
    firsts_now = (qkv_first, proj_first, router_first.T, norm_first.T, in_first[0], out_first[0])
    seconds_now = (qkv_second, proj_second, router_second.T, norm_second.T, in_second[0], out_second[0])
    state = (*weights_now, *firsts_now, *seconds_now)
    body = functools.partial(backward_kernel, dims, experts, per_group, fast)
    if fast:
        finals = [
            jax.ShapeDtypeStruct((2, shard, hidden), f32),
            jax.ShapeDtypeStruct((4, shard, width), f32),
            jax.ShapeDtypeStruct((16, shard), f32),
            jax.ShapeDtypeStruct((8, 128), f32),
        ]
        out3, dx3, g_exp, shared, small, norms = pl.pallas_call(
            body,
            grid=(steps,),
            in_specs=backward_specs + [anywhere] * (1 + len(state)),
            out_specs=backward_out[:2] + [whole(*v.shape) for v in finals],
            out_shape=backward_shape[:2] + finals,
            scratch_shapes=backward_scratch
            + Scatter.scratch(depth, hidden, shard)
            + [pltpu.VMEM(v.shape, v.dtype) for v in state]
            + [
                pltpu.SemaphoreType.DMA((len(state),)),
                pltpu.VMEM((2, 2, depth, 2, shard, width), bf16),
                pltpu.VMEM((16, width), f32),
            ]
            + shared_scatter_scratch(depth, shard, width),
            compiler_params=remote(1),
            name="attention_backward",
        )(*backward_in, grads.reshape(experts, 2, depth, 2, shard, hidden), *state)
    else:
        out3, dx3, shared_grad, small_grad = pl.pallas_call(
            body,
            grid=(steps,),
            in_specs=backward_specs,
            out_specs=backward_out,
            out_shape=backward_shape,
            scratch_shapes=backward_scratch,
            compiler_params=params,
            name="attention_backward",
        )(*backward_in)
    block_output = out3.reshape(rows_here, width)
    input_grad = dx3.reshape(rows_here, width)

    if not fast:
        shared = lax.psum(shared_grad.astype(f32), ("expert", "dp"))
        small = lax.psum(small_grad, ("expert", "dp"))
        g_exp = lax.psum(grads.astype(f32), ("expert", "dp"))
        start = lax.axis_index("dp") * shard
        shared = lax.dynamic_slice_in_dim(shared, start, shard, axis=1)
        small = lax.dynamic_slice_in_dim(small, start, shard, axis=1)
        g_exp = lax.dynamic_index_in_dim(g_exp, lax.axis_index("expert"), 0, keepdims=False)
        g_exp = lax.dynamic_slice_in_dim(g_exp, start, shard, axis=1)
        reduced = (
            jnp.concatenate([shared[0], shared[1], shared[2]], axis=1),
            shared[3],
            small[0:experts],
            small[8:12],
            g_exp[0],
            g_exp[1],
        )
        steps_now = [lamb_parts(*entry)[2] for entry in zip(weights_now, reduced, firsts_now, seconds_now)]
        sums = jnp.stack([jnp.sum(v * v) for v in (*weights_now, *steps_now)])
        norms = jnp.broadcast_to(jnp.pad(lax.psum(sums, "dp"), (0, 128 - 12)), (8, 128))
    cuts, part = 1, shard

    def rows_of(v):
        if v.shape[-2] != shard:
            return whole(*v.shape)
        lead = v.shape[:-2]
        return pl.BlockSpec((*lead, part, v.shape[-1]), lambda i: (0,) * len(lead) + (i, 0))

    grads_now = (shared, small, g_exp, norms)
    results = pl.pallas_call(
        functools.partial(update_kernel, experts),
        grid=(cuts,),
        in_specs=[rows_of(v) for v in (*grads_now, *state)],
        out_specs=[rows_of(v) for v in weights_now] * 3 + [whole(2, 6)],
        out_shape=[jax.ShapeDtypeStruct(v.shape, f32) for v in weights_now] * 3
        + [jax.ShapeDtypeStruct((2, 6), f32)],
        compiler_params=params,
        name="lamb_update",
    )(*grads_now, *state)

    def restore(values):
        return (values[0], values[1], values[2].T, values[3].T, values[4][None], values[5][None])

    return (
        block_output,
        input_grad,
        *restore(results[0:6]),
        *restore(results[6:12]),
        *restore(results[12:18]),
        results[18].T[None],
    )


def solution(mesh):
    tok2 = P(("dp", "expert"), None)
    tok1 = P(("dp", "expert"))
    row = P("dp", None)
    exp = P("expert", "dp", None)
    shared4 = (row, row, row, row)
    placed = (tok2, tok2, tok2, tok1, tok1, *shared4, exp, exp, *shared4, *shared4, exp, exp, exp, exp)
    results = (tok2, tok2, *((*shared4, exp, exp) * 3), P("expert", None, None))
    dims = (mesh.shape["dp"], mesh.shape["expert"])
    return jax.shard_map(
        functools.partial(per_device, dims),
        mesh=mesh,
        in_specs=placed,
        out_specs=results,
        check_vma=False,
    )
```
